32 devices in a mesh: ctx: 16 (over z, y, core), head: 2 (over x).
Axes of the slice: x: 2, y: 2, z: 4, core: 2. Of those that a mesh axis runs over, the one named last changes fastest.
Arguments:
- queries: bfloat16 [8192, 2048], P('ctx', 'head'), may hold values from -6 to 6
- keys: bfloat16 [8192, 2048], P('ctx', 'head'), may hold values from -6 to 6
- values: bfloat16 [8192, 2048], P('ctx', 'head'), may hold values from -6 to 6
- rates: float32 [8192, 2], P('ctx', 'head'), may hold values from 0.0005524272 to 0.0055242716
- w_up: bfloat16 [2, 1024, 512], P('head'), may hold values from -0.1875 to 0.1875
- w_gate: bfloat16 [2, 1024, 512], P('head'), may hold values from -0.1875 to 0.1875
- w_down: bfloat16 [2, 512, 1024], P('head'), may hold values from -0.25 to 0.25
- w_out: bfloat16 [2048, 5120], P('head'), may hold values from -0.125 to 0.125
Outputs:
- mixed: bfloat16 [8192, 5120], P('ctx', 'head')
The draws below stay inside these ranges and needn't reach their ends.
All inputs are finite; a program needn't handle non-finite values.
Results may differ from the reference program's by a relative error of at most 0.018.
Values may be sent and summed in bfloat16 or wider, within the bound.
A program may use at most 128 MiB of HBM per device.

```python
import math
import jax
import jax.numpy as jnp
from jax import lax

D = 5120
FD = 1024
FH = 512
STEPS = 2
FHEADS = 2
TOKENS = 8192


def steps_of(own_key, shape, cuts, low, high):
    def one(position, shards_of):
        heights = jax.random.uniform(jax.random.fold_in(jax.random.fold_in(own_key, 6), position), (shards_of,), jnp.float32, low / len(cuts), high / len(cuts))
        return jnp.repeat(jnp.exp(heights), shape[position] // shards_of).reshape((-1,) + (1,) * (len(shape) - position - 1))

    loudness = one(*cuts[0])
    for cut in cuts[1:]:
        loudness = loudness * one(*cut)
    return loudness


def bell_draw(key, shape, spread, limit, cuts=(), held_as=jnp.bfloat16):
    entries = jax.random.normal(key, shape, jnp.float32) * spread
    if len(cuts) > 0:
        entries = steps_of(key, shape, cuts, -0.22, 0.18) * entries
    return jnp.clip(entries, min=-limit, max=limit).astype(held_as)


def setup_inputs(seed: int = 0) -> dict:
    key_of = jax.random.split(jax.random.key(seed), 9)
    return {
        "queries": bell_draw(key_of[0], (TOKENS, FHEADS * FD), 1.0, 6.0, ((0, 16), (1, 2))),
        "keys": bell_draw(key_of[1], (TOKENS, FHEADS * FD), 1.0, 6.0, ((0, 16), (1, 2))),
        "values": bell_draw(key_of[2], (TOKENS, FHEADS * FD), 1.0, 6.0, ((0, 16), (1, 2))),
        "rates": jnp.clip(jnp.exp(math.log(0.0055242716) - 2.30258503 * jax.random.uniform(key_of[3], (TOKENS, FHEADS), jnp.float32) ** steps_of(key_of[3], (TOKENS, FHEADS), ((0, 16), (1, 2)), -0.2, 0.2)), 0.0005524272, 0.0055242716),
        "w_up": bell_draw(key_of[4], (FHEADS, FD, FH), FD ** -0.5, 0.1875, ((0, 2),)),
        "w_gate": bell_draw(key_of[5], (FHEADS, FD, FH), FD ** -0.5, 0.1875, ((0, 2),)),
        "w_down": bell_draw(key_of[6], (FHEADS, FH, FD), FH ** -0.5, 0.25, ((0, 2),)),
        "w_out": bell_draw(key_of[7], (FHEADS * FD, D), (FHEADS * FD) ** -0.5, 0.125, ((0, 2),)),
    }


def frob(matrix):
    return jnp.sqrt(jnp.sum(matrix * matrix))

def tdot(left, right):
    return lax.dot_general(left, right, (((0,), (0,)), ((), ())), preferred_element_type=jnp.float32)

def one_head(keys_h, values_h, queries_h, rate, first, third, second):
    sizes = [frob(first), frob(third), frob(second)]
    targets = (rate[:, None] * values_h.astype(jnp.float32)).astype(jnp.bfloat16)
    weights = [first, third, second]
    for step in range(STEPS):
        b_one = weights[0].astype(jnp.bfloat16)
        b_three = weights[1].astype(jnp.bfloat16)
        b_two = weights[2].astype(jnp.bfloat16)
        act = jnp.dot(keys_h, b_one, preferred_element_type=jnp.float32)
        lin = jnp.dot(keys_h, b_three, preferred_element_type=jnp.float32)
        sig = jax.nn.sigmoid(act)
        hidden = (act * sig * lin).astype(jnp.bfloat16)
        err = lax.dot_general(targets, b_two, (((1,), (1,)), ((), ())), preferred_element_type=jnp.float32)
        pgrad = (err * lin * sig * (1.0 + act * (1.0 - sig))).astype(jnp.bfloat16)
        qgrad = (err * act * sig).astype(jnp.bfloat16)
        grads = [tdot(keys_h, pgrad), tdot(keys_h, qgrad), tdot(hidden, targets)]
        updated = []
        for weight, grad, size in zip(weights, grads, sizes):
            moved = weight + grad
            updated.append(moved * size / jnp.sqrt(jnp.sum(moved * moved) + 1e-06))
        weights = updated
    b_one = weights[0].astype(jnp.bfloat16)
    b_three = weights[1].astype(jnp.bfloat16)
    b_two = weights[2].astype(jnp.bfloat16)
    act = jnp.dot(queries_h, b_one, preferred_element_type=jnp.float32)
    lin = jnp.dot(queries_h, b_three, preferred_element_type=jnp.float32)
    hidq = (jax.nn.silu(act) * lin).astype(jnp.bfloat16)
    return jnp.dot(hidq, b_two, preferred_element_type=jnp.float32).astype(jnp.bfloat16)

def reference(queries, keys, values, rates, w_up, w_gate, w_down, w_out):
    pieces = []
    for head in range(FHEADS):
        lo = head * FD
        pieces.append(one_head(keys[:, lo:lo + FD], values[:, lo:lo + FD], queries[:, lo:lo + FD], rates[:, head], w_up[head].astype(jnp.float32), w_gate[head].astype(jnp.float32), w_down[head].astype(jnp.float32)))
    joined = jnp.concatenate(pieces, axis=1)
    return jnp.dot(joined, w_out, preferred_element_type=jnp.float32).astype(jnp.bfloat16)
```

```python
import functools

import jax
import jax.numpy as jnp
from jax import lax
from jax.experimental import pallas as pl
from jax.experimental.pallas import tpu as pltpu
from jax.sharding import PartitionSpec as P

STEPS = 2
F32 = jnp.float32
BF16 = jnp.bfloat16
MESH = pl.DeviceIdType.MESH
GROUP = 3
LANE_PARTS = 2
CORES = 2
RING_ROWS = 4
TILES = 4
ORDERS = ((0, 1, 2), (2, 0, 1))


def ring_place(chip, width):
    row, turn = chip // width, width - 1 - chip % width
    odd = turn % 2
    along = (1 - odd) * (row - 1) + odd * (RING_ROWS - 1 - row)
    return jnp.where(row == 0, chip, width + (RING_ROWS - 1) * turn + along)


def ring_chip(place, width):
    past = jnp.maximum(place - width, 0)
    turn, along = past // (RING_ROWS - 1), past % (RING_ROWS - 1)
    odd = turn % 2
    row = (1 - odd) * (1 + along) + odd * (RING_ROWS - 1 - along)
    return jnp.where(place < width, place, row * width + width - 1 - turn)


def dot(left, right, dims=((1,), (0,))):
    return lax.dot_general(left, right, (dims, ((), ())), preferred_element_type=F32)


def square_sum(block):
    return jnp.sum((block * block).reshape(-1, 8, block.shape[-1]), axis=0)


def lane_fold(block):
    return block[:, :128] + block[:, 128:]


def layer_kernel(n_ctx, q, k, v, r, w0, w1, w2, w_out, out, *scratch):
    (
        ks, us, qs, vin, kt, ut, first0, first1, in2, first2,
        acts, mid, grads, blocks, arrived, kept, tally, tally_in, norm_sums,
        hq, near_hid, far_hid, near_w2, far_w2, far_scale, scale_out,
        w_near, w_far, near, total_out,
        ring_send, ring_recv, pair_send, pair_recv, tally_send, tally_recv,
        side_send, side_recv, w2_send, w2_recv, hid_send, hid_recv, local_sem,
    ) = scratch
    tokens, rows = k.shape
    cols = first0.shape[1]
    half = w_out.shape[1] // 2
    ring = n_ctx // CORES
    width = ring // RING_ROWS
    size = rows // ring
    bits = n_ctx.bit_length() - 1
    me = lax.axis_index("ctx")
    head = lax.axis_index("head")
    core = me % CORES
    chip = me // CORES
    place = ring_place(chip, width)
    right = {"ctx": ring_chip((place + 1) % ring, width) * CORES + core}
    left = {"ctx": ring_chip((place + ring - 1) % ring, width) * CORES + core}
    sibling = {"ctx": chip * CORES + 1 - core}
    across = {"head": 1 - head}
    diagonal = {"ctx": chip * CORES + 1 - core, "head": 1 - head}
    tally_partners = [
        {"ctx": me + (1 - 2 * ((me // (1 << bit)) % 2)) * (1 << bit)}
        for bit in range(bits)
    ]

    def remote(source, target, send_sem, recv_sem, device):
        return pltpu.make_async_remote_copy(
            src_ref=source,
            dst_ref=target,
            send_sem=send_sem,
            recv_sem=recv_sem,
            device_id=device,
            device_id_type=MESH,
        )

    def local(slot, source, target):
        return pltpu.make_async_copy(source, target, local_sem.at[slot])

    own_cols = pl.ds(pl.multiple_of(core * cols, 128), cols)
    own, other = slice(0, tokens), slice(tokens, 2 * tokens)
    loads = [
        local(0, k, ks.at[own, :]),
        local(1, v, vin),
        local(2, w0.at[:, own_cols], first0),
        local(3, w1.at[:, own_cols], first1),
        local(4, w2.at[pl.ds(pl.multiple_of(core * cols, 128), cols), :], in2),
        local(5, q, qs.at[own, :]),
    ]
    for load in loads:
        load.start()

    partners = [right, left, sibling, across, diagonal] + tally_partners
    barrier = pltpu.get_barrier_semaphore()
    for target in partners:
        pl.semaphore_signal(barrier, inc=1, device_id=target, device_id_type=MESH)
    pl.semaphore_wait(barrier, len(partners))

    def pair(slot, source, target):
        return remote(source, target, pair_send.at[slot], pair_recv.at[slot], sibling)

    k_pair = pair(0, k, ks.at[other, :])
    k_pair.start()
    near_cols = pl.ds(pl.multiple_of(head * half, 128), half)
    far_cols = pl.ds(pl.multiple_of((1 - head) * half, 128), half)
    depth = rows // CORES
    own_rows = pl.ds(pl.multiple_of(core * depth, depth), depth)
    w_swap = remote(
        w_out.at[own_rows, far_cols], w_far.at[own_rows, :],
        side_send.at[0], side_recv.at[0], across,
    )
    w_swap.start()

    loads[1].wait()
    rate = jnp.broadcast_to(r[...], (128, tokens)).T
    for t in range(rows // 128):
        at = slice(t * 128, (t + 1) * 128)
        scaled = (rate * vin[:, at].astype(F32)).astype(BF16)
        us[own, at] = scaled
        ut[at, own] = scaled.T
    u_pair = pair(1, us.at[own, :], us.at[other, :])
    u_pair.start()
    loads[0].wait()
    for t in range(rows // 128):
        at = slice(t * 128, (t + 1) * 128)
        kt[at, own] = ks[own, at].T
    kt_pair = pair(2, kt.at[:, own], kt.at[:, other])
    kt_pair.start()
    ut_pair = pair(3, ut.at[:, own], ut.at[:, other])
    ut_pair.start()
    q_pair = pair(4, q, qs.at[other, :])
    q_pair.start()
    w_copy = local(6, w_out.at[:, near_cols], w_near)
    w_copy.start()
    for load in loads[2:5]:
        load.wait()
    for t in range(rows // 128):
        at = slice(t * 128, (t + 1) * 128)
        first2[at, :] = in2[:, at].T

    firsts = (first0, first1, first2)
    scales = [None] * GROUP

    def weight(step, w):
        if step == 0:
            return firsts[w][...]
        return jnp.concatenate([blocks[2 * w], blocks[2 * w + 1]], axis=1)

    def act_dot(step, w, source, at):
        product = dot(source[at, :], weight(step, w))
        acts[w, at, :] = product

    for w, source in enumerate((ks, ks, us)):
        act_dot(0, w, source, own)
    k_pair.wait_recv()
    for w in range(2):
        act_dot(0, w, ks, other)
    u_pair.wait_recv()
    act_dot(0, 2, us, other)

    flows = [(w, h) for w in range(GROUP) for h in range(LANE_PARTS)]

    def reach(h):
        longer = ring // 2
        return (longer, ring - 1 - longer) if h == 0 else (ring - 1 - longer, longer)

    def chunk(number):
        return pl.ds(pl.multiple_of((number % ring) * size, size), size)

    for step in range(STEPS):
        order = ORDERS[step % 2]
        copies = {}

        def gates(piece, carry):
            at = pl.ds(pl.multiple_of(piece * 128, 128), 128)
            act, lin, err = acts[0, at, :], acts[1, at, :], acts[2, at, :]
            if step > 0:
                act, lin, err = act * scales[0], lin * scales[1], err * scales[2]
            sig = jax.nn.sigmoid(act)
            gate = act * sig
            mid[0, at, :] = (err * lin * sig * (1.0 + act * (1.0 - sig))).astype(BF16)
            mid[1, at, :] = (err * gate).astype(BF16)
            mid[2, at, :] = (gate * lin).astype(BF16)
            return carry

        lax.fori_loop(0, 2 * tokens // 128, gates, 0)
        if step == 0:
            kt_pair.wait_recv()
            ut_pair.wait_recv()

        def send(flow, slot, source, target, device):
            copy = remote(
                source, target, ring_send.at[flow, slot], ring_recv.at[flow, slot], device
            )
            copy.start()
            copies[flow, slot] = copy

        def send_sum(flow, to_right, s):
            far, back = reach(flow % LANE_PARTS)
            at = chunk(place + far - s) if to_right else chunk(place + ring - back + s)
            slot = s if to_right else far + s
            device = right if to_right else left
            send(flow, slot, grads.at[flow, at, :], arrived.at[flow, slot], device)

        def send_block(flow, to_right, t):
            far, back = reach(flow % LANE_PARTS)
            at = chunk(place + ring - t) if to_right else chunk(place + t)
            slot = ring - 1 + (t if to_right else far + t)
            device = right if to_right else left
            here = blocks.at[flow, at, :]
            send(flow, slot, here, here, device)

        def pass_sum(flow, to_right, s):
            far, back = reach(flow % LANE_PARTS)
            slot = s if to_right else far + s
            at = chunk(place + far - 1 - s) if to_right else chunk(place + ring + 1 - back + s)
            copies[flow, slot].wait_recv()
            total = grads[flow, at, :].astype(F32) + arrived[flow, slot].astype(F32)
            grads[flow, at, :] = total.astype(BF16)
            send_sum(flow, to_right, s + 1)

        w2_copies = []

        def send_w2(flow, number):
            h = flow % LANE_PARTS
            here = chunk(number)
            slot = len(w2_copies)
            copy = remote(
                blocks.at[flow, here, :], far_w2.at[h, here, :],
                w2_send.at[slot], w2_recv.at[slot], across,
            )
            copy.start()
            w2_copies.append(copy)

        for w in order:
            source = ut if w == 2 else kt

            def grad_rows(piece, carry):
                at = pl.ds(pl.multiple_of(piece * (rows // 4), rows // 4), rows // 4)
                product = dot(source[at, :], mid[w]).astype(BF16)
                grads[2 * w, at, :] = product[:, :128]
                grads[2 * w + 1, at, :] = product[:, 128:]
                return carry

            lax.fori_loop(0, 4, grad_rows, 0)
            for h in range(LANE_PARTS):
                send_sum(2 * w + h, True, 0)
                send_sum(2 * w + h, False, 0)
        if step == 0:
            for w in range(GROUP):
                norm_sums[0, w] = lane_fold(square_sum(firsts[w][...].astype(F32)))
            norm_pair = pair(5, norm_sums.at[0], norm_sums.at[1])
            norm_pair.start()
        turn = ring // 2 - 1
        ordered = [2 * w + h for w in order for h in range(LANE_PARTS)]
        for s in range(turn):
            for flow in ordered:
                far, back = reach(flow % LANE_PARTS)
                if s < far - 1:
                    pass_sum(flow, True, s)
                if s < back - 1:
                    pass_sum(flow, False, s)
        for flow in ordered:
            far, back = reach(flow % LANE_PARTS)
            w, h = flows[flow]
            at = chunk(place)
            copies[flow, far - 1].wait_recv()
            copies[flow, ring - 2].wait_recv()
            total = grads[flow, at, :].astype(F32) + arrived[flow, far - 1].astype(F32)
            total = total + arrived[flow, ring - 2].astype(F32)
            if step == 0:
                lanes = slice(h * 128, (h + 1) * 128)
                moved = firsts[w][at, lanes].astype(F32) + total
            else:
                moved = kept[flow] * scales[w] + total
            kept[flow] = moved
            rounded = moved.astype(BF16)
            blocks[flow, at, :] = rounded
            send_block(flow, True, 0)
            send_block(flow, False, 0)
            if step == STEPS - 1 and w == 2:
                send_w2(flow, place)
            part = square_sum(rounded.astype(F32))
            tally[0, w] = part if h == 0 else tally[0, w] + part
        tallies = []

        def start_tally(stage):
            copy = remote(
                tally.at[stage], tally_in.at[step * bits + stage],
                tally_send.at[stage], tally_recv.at[step * bits + stage],
                tally_partners[stage],
            )
            copy.start()
            tallies.append(copy)

        def end_tally(stage):
            tallies[stage].wait_recv()
            tally[stage + 1] = tally[stage] + tally_in[step * bits + stage]
            if stage + 1 < bits:
                start_tally(stage + 1)

        start_tally(0)
        ended = 0
        for t in range(turn + 1):
            for w in order:
                for h in range(LANE_PARTS):
                    flow = 2 * w + h
                    far, back = reach(h)
                    for to_right, count in ((True, far), (False, back)):
                        if t >= count:
                            continue
                        copies[flow, ring - 1 + (t if to_right else far + t)].wait_recv()
                        if t < count - 1:
                            send_block(flow, to_right, t + 1)
                        if step == STEPS - 1 and w == 2:
                            send_w2(flow, place + (ring - 1 - t if to_right else 1 + t))
                if t == turn:
                    if step < STEPS - 1:
                        source = us if w == 2 else ks
                        act_dot(1, w, source, own)
                        act_dot(1, w, source, other)
                    elif w == 2:
                        w2_pair = pair(6, blocks.at[4:6], near_w2)
                        w2_pair.start()
                    else:
                        if w == 0:
                            q_pair.wait_recv()
                            loads[5].wait()
                        act_dot(1, w, qs, own)
                        act_dot(1, w, qs, other)
            if t < turn and ended < bits:
                end_tally(ended)
                ended += 1
        while ended < bits:
            end_tally(ended)
            ended += 1
        if step == 0:
            norm_pair.wait()
            norms = [
                jnp.sqrt(jnp.sum(norm_sums[0, w] + norm_sums[1, w], keepdims=True))
                for w in range(GROUP)
            ]
        for copy in list(copies.values()) + tallies:
            copy.wait_send()
        scales = [
            norms[w] / jnp.sqrt(jnp.sum(tally[bits, w], keepdims=True) + 1e-06)
            for w in range(GROUP)
        ]

    tile = tokens // TILES
    scale_out[...] = jnp.broadcast_to(scales[2], scale_out.shape)
    scale_swap = remote(
        scale_out, far_scale, side_send.at[1], side_recv.at[1], across
    )
    scale_swap.start()
    hid_copies = []

    def send_hid(slot, source, target, device):
        copy = remote(source, target, hid_send.at[slot], hid_recv.at[slot], device)
        copy.start()
        return copy

    for t in range(TILES):
        trio = []
        for side in range(CORES):
            at = slice(side * tokens + t * tile, side * tokens + (t + 1) * tile)
            act = acts[0, at, :] * scales[0]
            lin = acts[1, at, :] * scales[1]
            hq[at, :] = (act * jax.nn.sigmoid(act) * lin).astype(BF16)
            to = slice(t * tile, (t + 1) * tile)
            if side == 0:
                trio.append(send_hid(3 * t, hq.at[at, :], far_hid.at[0, to, :], across))
            else:
                trio.append(
                    send_hid(3 * t + 1, hq.at[at, :], far_hid.at[1, to, :], diagonal)
                )
                trio.append(send_hid(3 * t + 2, hq.at[at, :], near_hid.at[to, :], sibling))
        hid_copies.append(trio)
    w_swap.wait()
    w_share = pair(7, w_far.at[own_rows, :], w_far.at[own_rows, :])
    w_share.start()
    w2_pair.wait()
    own_w2 = jnp.concatenate([blocks[4], blocks[5]], axis=1)
    wide = ((1,), (1,))
    for t in range(TILES):
        at = slice(t * tile, (t + 1) * tile)
        hid_copies[t][2].wait_recv()
        mine = dot(hq[at, :], own_w2, wide)
        theirs = dot(
            near_hid[at, :], jnp.concatenate([near_w2[0], near_w2[1]], axis=1), wide
        )
        near[at, :] = ((mine + theirs) * scales[2]).astype(BF16)
    for copy in w2_copies:
        copy.wait()
    far_pair = pair(8, far_w2.at[0:2], far_w2.at[2:4])
    far_pair.start()
    w_copy.wait()
    stripe = half // 5

    def near_cols_of(c, carry):
        lanes = pl.ds(pl.multiple_of(c * stripe, 128), stripe)
        total_out[:, lanes] = dot(near[...], w_near[:, lanes])
        return carry

    lax.fori_loop(0, 5, near_cols_of, 0)
    scale_swap.wait()
    far_pair.wait()
    w_share.wait()
    scale = jnp.max(far_scale[...], keepdims=True)
    for t in range(TILES):
        at = slice(t * tile, (t + 1) * tile)
        hid_copies[t][0].wait_recv()
        hid_copies[t][1].wait_recv()
        mine = dot(
            far_hid[0, at, :], jnp.concatenate([far_w2[0], far_w2[1]], axis=1), wide
        )
        theirs = dot(
            far_hid[1, at, :], jnp.concatenate([far_w2[2], far_w2[3]], axis=1), wide
        )
        near[at, :] = ((mine + theirs) * scale).astype(BF16)

        def far_cols_of(c, carry):
            lanes = pl.ds(pl.multiple_of(c * stripe, 128), stripe)
            added = total_out[at, lanes] + dot(near[at, :], w_far[:, lanes])
            out[at, lanes] = added.astype(BF16)
            return carry

        lax.fori_loop(0, 5, far_cols_of, 0)
    for trio in hid_copies:
        for copy in trio:
            copy.wait_send()
    for copy in (k_pair, u_pair, kt_pair, ut_pair, q_pair):
        copy.wait_send()


def shards(n_ctx, queries, keys, values, rates, w_up, w_gate, w_down, w_out):
    tokens, rows = keys.shape
    cols = w_up.shape[2] // CORES
    half = w_out.shape[1] // 2
    ring = n_ctx // CORES
    size = rows // ring
    bits = n_ctx.bit_length() - 1
    flows = GROUP * LANE_PARTS
    vmem = pl.BlockSpec(memory_space=pltpu.VMEM)
    anywhere = pl.BlockSpec(memory_space=pl.ANY)
    dma = pltpu.SemaphoreType.DMA
    return pl.pallas_call(
        functools.partial(layer_kernel, n_ctx),
        out_shape=jax.ShapeDtypeStruct((tokens, half), BF16),
        in_specs=[anywhere] * 3 + [vmem] + [anywhere] * 4,
        out_specs=vmem,
        scratch_shapes=[
            pltpu.VMEM((2 * tokens, rows), BF16),
            pltpu.VMEM((2 * tokens, rows), BF16),
            pltpu.VMEM((2 * tokens, rows), BF16),
            pltpu.VMEM((tokens, rows), BF16),
            pltpu.VMEM((rows, 2 * tokens), BF16),
            pltpu.VMEM((rows, 2 * tokens), BF16),
            pltpu.VMEM((rows, cols), BF16),
            pltpu.VMEM((rows, cols), BF16),
            pltpu.VMEM((cols, rows), BF16),
            pltpu.VMEM((rows, cols), BF16),
            pltpu.VMEM((GROUP, 2 * tokens, cols), F32),
            pltpu.VMEM((GROUP, 2 * tokens, cols), BF16),
            pltpu.VMEM((flows, rows, cols // LANE_PARTS), BF16),
            pltpu.VMEM((flows, rows, cols // LANE_PARTS), BF16),
            pltpu.VMEM((flows, ring - 1, size, cols // LANE_PARTS), BF16),
            pltpu.VMEM((flows, size, cols // LANE_PARTS), F32),
            pltpu.VMEM((bits + 1, GROUP, 8, 128), F32),
            pltpu.VMEM((STEPS * bits, GROUP, 8, 128), F32),
            pltpu.VMEM((CORES, GROUP, 8, 128), F32),
            pltpu.VMEM((2 * tokens, cols), BF16),
            pltpu.VMEM((tokens, cols), BF16),
            pltpu.VMEM((CORES, tokens, cols), BF16),
            pltpu.VMEM((LANE_PARTS, rows, cols // LANE_PARTS), BF16),
            pltpu.VMEM((CORES * LANE_PARTS, rows, cols // LANE_PARTS), BF16),
            pltpu.VMEM((8, 128), F32),
            pltpu.VMEM((8, 128), F32),
            pltpu.VMEM((rows, half), BF16),
            pltpu.VMEM((rows, half), BF16),
            pltpu.VMEM((tokens, rows), BF16),
            pltpu.VMEM((tokens, half), F32),
            dma((flows, 2 * (ring - 1))),
            dma((flows, 2 * (ring - 1))),
            dma((9,)),
            dma((9,)),
            dma((bits,)),
            dma((STEPS * bits,)),
            dma((2,)),
            dma((2,)),
            dma((LANE_PARTS * ring,)),
            dma((LANE_PARTS * ring,)),
            dma((3 * TILES,)),
            dma((3 * TILES,)),
            dma((7,)),
        ],
        compiler_params=pltpu.CompilerParams(
            collective_id=0, has_side_effects=True, vmem_limit_bytes=60 << 20
        ),
    )(queries, keys, values, rates.T, w_up[0], w_gate[0], w_down[0], w_out)


def solution(mesh):
    def body(*args):
        return shards(mesh.shape["ctx"], *args)

    return jax.shard_map(
        body,
        mesh=mesh,
        in_specs=(
            P("ctx", "head"),
            P("ctx", "head"),
            P("ctx", "head"),
            P("ctx", "head"),
            P("head", None, None),
            P("head", None, None),
            P("head", None, None),
            P("head", None),
        ),
        out_specs=P("ctx", "head"),
        check_vma=False,
    )
```

```python
import functools

import jax
import jax.numpy as jnp
from jax import lax
from jax.experimental import pallas as pl
from jax.experimental.pallas import tpu as pltpu
from jax.sharding import PartitionSpec as P

STEPS = 2
F32 = jnp.float32
BF16 = jnp.bfloat16
MESH = pl.DeviceIdType.MESH
GROUP = 3
LANE_PARTS = 2
CORES = 2
RING_ROWS = 4
TILES = 2
PIECES = 4
STRIPES = 5
FIRST_SENT = (2, 0, 1)


def ring_place(chip, width):
    row, turn = chip // width, width - 1 - chip % width
    odd = turn % 2
    along = (1 - odd) * (row - 1) + odd * (RING_ROWS - 1 - row)
    return jnp.where(row == 0, chip, width + (RING_ROWS - 1) * turn + along)


def ring_chip(place, width):
    past = jnp.maximum(place - width, 0)
    turn, along = past // (RING_ROWS - 1), past % (RING_ROWS - 1)
    odd = turn % 2
    row = (1 - odd) * (1 + along) + odd * (RING_ROWS - 1 - along)
    return jnp.where(place < width, place, row * width + width - 1 - turn)


def dot(left, right, dims=((1,), (0,))):
    return lax.dot_general(left, right, (dims, ((), ())), preferred_element_type=F32)


def square_sum(block):
    return jnp.sum((block * block).reshape(-1, 8, block.shape[-1]), axis=0)


def lane_fold(block):
    return block[:, :128] + block[:, 128:]


def layer_kernel(n_ctx, q, k, v, r, w0, w1, w2, w_out, out, *scratch):
    (
        ks, us, qs, vin, kt, ut, first0, first1, in2, first2,
        acts, mid, grads, blocks, arrived, kept, tally, tally_in, norm_sums,
        hq, near_hid, far_hid, near_w2, far_w2, far_scale, scale_out,
        w_near, w_far, near, total_out, staged,
        ring_send, ring_recv, pair_send, pair_recv, tally_send, tally_recv,
        side_send, side_recv, w2_send, w2_recv, hid_send, hid_recv, local_sem, out_sem,
    ) = scratch
    tokens, rows = k.shape
    cols = first0.shape[1]
    half = w_out.shape[1] // 2
    ring = n_ctx // CORES
    width = ring // RING_ROWS
    size = rows // ring
    bits = n_ctx.bit_length() - 1
    me = lax.axis_index("ctx")
    head = lax.axis_index("head")
    core = me % CORES
    chip = me // CORES
    place = ring_place(chip, width)
    right = {"ctx": ring_chip((place + 1) % ring, width) * CORES + core}
    left = {"ctx": ring_chip((place + ring - 1) % ring, width) * CORES + core}
    sibling = {"ctx": chip * CORES + 1 - core}
    across = {"head": 1 - head}
    diagonal = {"ctx": chip * CORES + 1 - core, "head": 1 - head}
    tally_partners = [
        {"ctx": me + (1 - 2 * ((me // (1 << bit)) % 2)) * (1 << bit)}
        for bit in range(bits)
    ]

    def remote(source, target, send_sem, recv_sem, device):
        return pltpu.make_async_remote_copy(
            src_ref=source,
            dst_ref=target,
            send_sem=send_sem,
            recv_sem=recv_sem,
            device_id=device,
            device_id_type=MESH,
        )

    def local(slot, source, target):
        return pltpu.make_async_copy(source, target, local_sem.at[slot])

    own_cols = pl.ds(pl.multiple_of(core * cols, 128), cols)
    own, other = slice(0, tokens), slice(tokens, 2 * tokens)
    loads = [
        local(0, k, ks.at[own, :]),
        local(1, v, vin),
        local(2, w0.at[:, own_cols], first0),
        local(3, w1.at[:, own_cols], first1),
        local(4, w2.at[pl.ds(pl.multiple_of(core * cols, 128), cols), :], in2),
        local(5, q, qs.at[own, :]),
    ]
    for load in loads:
        load.start()

    partners = [right, left, sibling, across, diagonal] + tally_partners
    barrier = pltpu.get_barrier_semaphore()
    for target in partners:
        pl.semaphore_signal(barrier, inc=1, device_id=target, device_id_type=MESH)
    pl.semaphore_wait(barrier, len(partners))

    def pair(slot, source, target):
        return remote(source, target, pair_send.at[slot], pair_recv.at[slot], sibling)

    k_pair = pair(0, k, ks.at[other, :])
    k_pair.start()
    near_cols = pl.ds(pl.multiple_of(head * half, 128), half)
    far_cols = pl.ds(pl.multiple_of((1 - head) * half, 128), half)
    depth = rows // CORES
    own_rows = pl.ds(pl.multiple_of(core * depth, depth), depth)
    w_swap = remote(
        w_out.at[own_rows, far_cols], w_far.at[own_rows, :],
        side_send.at[0], side_recv.at[0], across,
    )
    w_swap.start()

    loads[1].wait()
    rate = jnp.broadcast_to(r[...], (128, tokens)).T
    for t in range(rows // 128):
        at = slice(t * 128, (t + 1) * 128)
        scaled = (rate * vin[:, at].astype(F32)).astype(BF16)
        us[own, at] = scaled
        ut[at, own] = scaled.T
    u_pair = pair(1, us.at[own, :], us.at[other, :])
    u_pair.start()

    def turned(source, target, side):
        for t in range(rows // 128):
            at = slice(t * 128, (t + 1) * 128)
            target[at, side] = source[side, at].T

    loads[0].wait()
    turned(ks, kt, own)
    q_pair = pair(2, q, qs.at[other, :])
    q_pair.start()
    w_copy = local(6, w_out.at[:, near_cols], w_near)
    w_copy.start()
    for load in loads[2:5]:
        load.wait()
    for t in range(rows // 128):
        at = slice(t * 128, (t + 1) * 128)
        first2[at, :] = in2[:, at].T

    firsts = (first0, first1, first2)
    scales = [None] * GROUP

    def weight(step, w):
        if step == 0:
            return firsts[w][...]
        return jnp.concatenate([blocks[2 * w], blocks[2 * w + 1]], axis=1)

    def act_dot(step, w, source, at):
        product = dot(source[at, :], weight(step, w))
        acts[w, at, :] = product

    act_dot(0, 0, ks, own)
    act_dot(0, 1, ks, own)
    k_pair.wait_recv()
    act_dot(0, 0, ks, other)
    act_dot(0, 1, ks, other)
    turned(ks, kt, other)

    pieces = 2 * tokens // 128

    def hid_gates(by):
        def one(piece, carry):
            at = pl.ds(pl.multiple_of(piece * 128, 128), 128)
            act, lin = acts[0, at, :], acts[1, at, :]
            if by[0] is not None:
                act, lin = act * by[0], lin * by[1]
            mid[2, at, :] = (act * jax.nn.sigmoid(act) * lin).astype(BF16)
            return carry

        lax.fori_loop(0, pieces, one, 0)

    def err_gates(by):
        def one(piece, carry):
            at = pl.ds(pl.multiple_of(piece * 128, 128), 128)
            act, lin, err = acts[0, at, :], acts[1, at, :], acts[2, at, :]
            if by[0] is not None:
                act, lin, err = act * by[0], lin * by[1], err * by[2]
            sig = jax.nn.sigmoid(act)
            mid[0, at, :] = (err * lin * sig * (1.0 + act * (1.0 - sig))).astype(BF16)
            mid[1, at, :] = (err * (act * sig)).astype(BF16)
            return carry

        lax.fori_loop(0, pieces, one, 0)

    hid_gates(scales)

    flows = [(w, h) for w in range(GROUP) for h in range(LANE_PARTS)]

    def reach(h):
        longer = ring // 2
        return (longer, ring - 1 - longer) if h == 0 else (ring - 1 - longer, longer)

    def chunk(number):
        return pl.ds(pl.multiple_of((number % ring) * size, size), size)

    copies = {}
    for step in range(STEPS):

        def send(flow, slot, source, target, device):
            copy = remote(
                source, target, ring_send.at[flow, slot], ring_recv.at[flow, slot], device
            )
            copy.start()
            copies[flow, slot] = copy

        def send_sum(flow, to_right, s):
            far, back = reach(flow % LANE_PARTS)
            at = chunk(place + far - s) if to_right else chunk(place + ring - back + s)
            slot = s if to_right else far + s
            device = right if to_right else left
            send(flow, slot, grads.at[flow, at, :], arrived.at[flow, slot], device)

        def send_block(flow, to_right, t):
            far, back = reach(flow % LANE_PARTS)
            at = chunk(place + ring - t) if to_right else chunk(place + t)
            slot = ring - 1 + (t if to_right else far + t)
            device = right if to_right else left
            here = blocks.at[flow, at, :]
            send(flow, slot, here, here, device)

        def pass_sum(flow, to_right, s):
            far, back = reach(flow % LANE_PARTS)
            slot = s if to_right else far + s
            at = chunk(place + far - 1 - s) if to_right else chunk(place + ring + 1 - back + s)
            copies[flow, slot].wait_recv()
            total = grads[flow, at, :].astype(F32) + arrived[flow, slot].astype(F32)
            grads[flow, at, :] = total.astype(BF16)
            send_sum(flow, to_right, s + 1)

        w2_copies = []

        def send_w2(flow, number):
            h = flow % LANE_PARTS
            here = chunk(number)
            slot = len(w2_copies)
            copy = remote(
                blocks.at[flow, here, :], far_w2.at[h, here, :],
                w2_send.at[slot], w2_recv.at[slot], across,
            )
            copy.start()
            w2_copies.append(copy)

        def grad(w):
            source = ut if w == 2 else kt

            def grad_rows(piece, carry):
                at = pl.ds(pl.multiple_of(piece * (rows // PIECES), rows // PIECES), rows // PIECES)
                product = dot(source[at, :], mid[w]).astype(BF16)
                grads[2 * w, at, :] = product[:, :128]
                grads[2 * w + 1, at, :] = product[:, 128:]
                return carry

            lax.fori_loop(0, PIECES, grad_rows, 0)
            for h in range(LANE_PARTS):
                send_sum(2 * w + h, True, 0)
                send_sum(2 * w + h, False, 0)

        if step == 0:
            u_pair.wait_recv()
            turned(us, ut, other)
            grad(2)
            act_dot(0, 2, us, own)
            act_dot(0, 2, us, other)
        err_gates(scales)
        grad(0)
        grad(1)
        if step == 0:
            for w in range(GROUP):
                norm_sums[0, w] = lane_fold(square_sum(firsts[w][...].astype(F32)))
            norm_pair = pair(3, norm_sums.at[0], norm_sums.at[1])
            norm_pair.start()
        turn = ring // 2 - 1
        ordered = [2 * w + h for w in range(GROUP) for h in range(LANE_PARTS)]
        for s in range(turn):
            for flow in ordered:
                far, back = reach(flow % LANE_PARTS)
                if s < far - 1:
                    pass_sum(flow, True, s)
                if s < back - 1:
                    pass_sum(flow, False, s)
        for flow in ordered:
            far, back = reach(flow % LANE_PARTS)
            w, h = flows[flow]
            at = chunk(place)
            copies[flow, far - 1].wait_recv()
            copies[flow, ring - 2].wait_recv()
            total = grads[flow, at, :].astype(F32) + arrived[flow, far - 1].astype(F32)
            total = total + arrived[flow, ring - 2].astype(F32)
            if step == 0:
                lanes = slice(h * 128, (h + 1) * 128)
                moved = firsts[w][at, lanes].astype(F32) + total
            else:
                moved = kept[flow] * scales[w] + total
            kept[flow] = moved
            rounded = moved.astype(BF16)
            blocks[flow, at, :] = rounded
            send_block(flow, True, 0)
            send_block(flow, False, 0)
            if step == STEPS - 1 and w == 2:
                send_w2(flow, place)
            part = square_sum(rounded.astype(F32))
            tally[0, w] = part if h == 0 else tally[0, w] + part
        tallies = []

        def start_tally(stage):
            copy = remote(
                tally.at[stage], tally_in.at[step * bits + stage],
                tally_send.at[stage], tally_recv.at[step * bits + stage],
                tally_partners[stage],
            )
            copy.start()
            tallies.append(copy)

        def end_tally(stage):
            tallies[stage].wait_recv()
            tally[stage + 1] = tally[stage] + tally_in[step * bits + stage]
            if stage + 1 < bits:
                start_tally(stage + 1)

        def take_block(flow, t):
            far, back = reach(flow % LANE_PARTS)
            for to_right, count in ((True, far), (False, back)):
                if t >= count:
                    continue
                copies[flow, ring - 1 + (t if to_right else far + t)].wait_recv()
                if t < count - 1:
                    send_block(flow, to_right, t + 1)
                if step == STEPS - 1 and flow // LANE_PARTS == 2:
                    send_w2(flow, place + (ring - 1 - t if to_right else 1 + t))

        start_tally(0)
        ended = 0
        for t in range(turn):
            for flow in ordered:
                take_block(flow, t)
                if flow == ordered[3] and ended < bits - 1:
                    end_tally(ended)
                    ended += 1
        if step == 0:
            norm_pair.wait()
            norms = [
                jnp.sqrt(jnp.sum(norm_sums[0, w] + norm_sums[1, w], keepdims=True))
                for w in range(GROUP)
            ]
        else:
            q_pair.wait_recv()
            loads[5].wait()
        source = ks if step == 0 else qs
        for w in range(2):
            for h in range(LANE_PARTS):
                take_block(2 * w + h, turn)
            act_dot(1, w, source, own)
            act_dot(1, w, source, other)
        while ended < bits:
            end_tally(ended)
            ended += 1
        scales = [
            norms[w] / jnp.sqrt(jnp.sum(tally[bits, w], keepdims=True) + 1e-06)
            for w in range(GROUP)
        ]
        for (flow, slot), copy in copies.items():
            if slot < ring - 1:
                copy.wait_send()
        old = {key: copy for key, copy in copies.items() if key[1] >= ring - 1}
        if step == 0:
            hid_gates(scales)
            grad(2)
            for h in range(LANE_PARTS):
                take_block(4 + h, turn)
            act_dot(1, 2, us, own)
            act_dot(1, 2, us, other)
        for copy in list(old.values()) + tallies:
            copy.wait_send()

    tile = tokens // TILES
    scale_out[...] = jnp.broadcast_to(scales[2], scale_out.shape)
    scale_swap = remote(
        scale_out, far_scale, side_send.at[1], side_recv.at[1], across
    )
    scale_swap.start()
    hid_copies = []

    def send_hid(slot, source, target, device):
        copy = remote(source, target, hid_send.at[slot], hid_recv.at[slot], device)
        copy.start()
        return copy

    def send_tile(t):
        trio = []
        for side in range(CORES):
            at = slice(side * tokens + t * tile, side * tokens + (t + 1) * tile)
            act = acts[0, at, :] * scales[0]
            lin = acts[1, at, :] * scales[1]
            hq[at, :] = (act * jax.nn.sigmoid(act) * lin).astype(BF16)
            to = slice(t * tile, (t + 1) * tile)
            if side == 0:
                trio.append(send_hid(3 * t, hq.at[at, :], far_hid.at[0, to, :], across))
            else:
                trio.append(
                    send_hid(3 * t + 1, hq.at[at, :], far_hid.at[1, to, :], diagonal)
                )
                trio.append(send_hid(3 * t + 2, hq.at[at, :], near_hid.at[to, :], sibling))
        hid_copies.append(trio)

    for t in range(TILES // 2):
        send_tile(t)
    for h in range(LANE_PARTS):
        take_block(4 + h, turn)
    w2_pair = pair(4, blocks.at[4:6], near_w2)
    w2_pair.start()
    for t in range(TILES // 2, TILES):
        send_tile(t)
    w_swap.wait()
    w_share = pair(5, w_far.at[own_rows, :], w_far.at[own_rows, :])
    w_share.start()
    w2_pair.wait()
    own_w2 = jnp.concatenate([blocks[4], blocks[5]], axis=1)
    wide = ((1,), (1,))
    for t in range(TILES):
        at = slice(t * tile, (t + 1) * tile)
        hid_copies[t][2].wait_recv()
        mine = dot(hq[at, :], own_w2, wide)
        theirs = dot(
            near_hid[at, :], jnp.concatenate([near_w2[0], near_w2[1]], axis=1), wide
        )
        near[at, :] = ((mine + theirs) * scales[2]).astype(BF16)
    for copy in w2_copies:
        copy.wait()
    far_pair = pair(6, far_w2.at[0:2], far_w2.at[2:4])
    far_pair.start()
    w_copy.wait()
    stripe = half // STRIPES

    def near_cols_of(c, carry):
        lanes = pl.ds(pl.multiple_of(c * stripe, 128), stripe)
        total_out[:, lanes] = dot(near[...], w_near[:, lanes])
        return carry

    lax.fori_loop(0, STRIPES, near_cols_of, 0)
    scale_swap.wait()
    far_pair.wait()
    w_share.wait()
    scale = jnp.max(far_scale[...], keepdims=True)

    def out_copy(t, at, lanes, c):
        here = staged.at[at, lanes]
        return pltpu.make_async_copy(here, out.at[at, lanes], out_sem.at[t * STRIPES + c])

    for t in range(TILES):
        at = slice(t * tile, (t + 1) * tile)
        hid_copies[t][0].wait_recv()
        hid_copies[t][1].wait_recv()
        mine = dot(
            far_hid[0, at, :], jnp.concatenate([far_w2[0], far_w2[1]], axis=1), wide
        )
        theirs = dot(
            far_hid[1, at, :], jnp.concatenate([far_w2[2], far_w2[3]], axis=1), wide
        )
        near[at, :] = ((mine + theirs) * scale).astype(BF16)

        def far_cols_of(c, carry):
            lanes = pl.ds(pl.multiple_of(c * stripe, 128), stripe)
            added = total_out[at, lanes] + dot(near[at, :], w_far[:, lanes])
            staged[at, lanes] = added.astype(BF16)
            out_copy(t, at, lanes, c).start()
            return carry

        lax.fori_loop(0, STRIPES, far_cols_of, 0)
    for t in range(TILES):
        at = slice(t * tile, (t + 1) * tile)

        def written(c, carry):
            lanes = pl.ds(pl.multiple_of(c * stripe, 128), stripe)
            out_copy(t, at, lanes, c).wait()
            return carry

        lax.fori_loop(0, STRIPES, written, 0)
    for trio in hid_copies:
        for copy in trio:
            copy.wait_send()
    for copy in (k_pair, u_pair, q_pair):
        copy.wait_send()


def shards(n_ctx, queries, keys, values, rates, w_up, w_gate, w_down, w_out):
    tokens, rows = keys.shape
    cols = w_up.shape[2] // CORES
    half = w_out.shape[1] // 2
    ring = n_ctx // CORES
    size = rows // ring
    bits = n_ctx.bit_length() - 1
    flows = GROUP * LANE_PARTS
    vmem = pl.BlockSpec(memory_space=pltpu.VMEM)
    anywhere = pl.BlockSpec(memory_space=pl.ANY)
    dma = pltpu.SemaphoreType.DMA
    return pl.pallas_call(
        functools.partial(layer_kernel, n_ctx),
        out_shape=jax.ShapeDtypeStruct((tokens, half), BF16),
        in_specs=[anywhere] * 3 + [vmem] + [anywhere] * 4,
        out_specs=anywhere,
        scratch_shapes=[
            pltpu.VMEM((2 * tokens, rows), BF16),
            pltpu.VMEM((2 * tokens, rows), BF16),
            pltpu.VMEM((2 * tokens, rows), BF16),
            pltpu.VMEM((tokens, rows), BF16),
            pltpu.VMEM((rows, 2 * tokens), BF16),
            pltpu.VMEM((rows, 2 * tokens), BF16),
            pltpu.VMEM((rows, cols), BF16),
            pltpu.VMEM((rows, cols), BF16),
            pltpu.VMEM((cols, rows), BF16),
            pltpu.VMEM((rows, cols), BF16),
            pltpu.VMEM((GROUP, 2 * tokens, cols), F32),
            pltpu.VMEM((GROUP, 2 * tokens, cols), BF16),
            pltpu.VMEM((flows, rows, cols // LANE_PARTS), BF16),
            pltpu.VMEM((flows, rows, cols // LANE_PARTS), BF16),
            pltpu.VMEM((flows, ring - 1, size, cols // LANE_PARTS), BF16),
            pltpu.VMEM((flows, size, cols // LANE_PARTS), F32),
            pltpu.VMEM((bits + 1, GROUP, 8, 128), F32),
            pltpu.VMEM((STEPS * bits, GROUP, 8, 128), F32),
            pltpu.VMEM((CORES, GROUP, 8, 128), F32),
            pltpu.VMEM((2 * tokens, cols), BF16),
            pltpu.VMEM((tokens, cols), BF16),
            pltpu.VMEM((CORES, tokens, cols), BF16),
            pltpu.VMEM((LANE_PARTS, rows, cols // LANE_PARTS), BF16),
            pltpu.VMEM((CORES * LANE_PARTS, rows, cols // LANE_PARTS), BF16),
            pltpu.VMEM((8, 128), F32),
            pltpu.VMEM((8, 128), F32),
            pltpu.VMEM((rows, half), BF16),
            pltpu.VMEM((rows, half), BF16),
            pltpu.VMEM((tokens, rows), BF16),
            pltpu.VMEM((tokens, half), F32),
            pltpu.VMEM((tokens, half), BF16),
            dma((flows, 2 * (ring - 1))),
            dma((flows, 2 * (ring - 1))),
            dma((7,)),
            dma((7,)),
            dma((bits,)),
            dma((STEPS * bits,)),
            dma((2,)),
            dma((2,)),
            dma((LANE_PARTS * ring,)),
            dma((LANE_PARTS * ring,)),
            dma((3 * TILES,)),
            dma((3 * TILES,)),
            dma((7,)),
            dma((TILES * STRIPES,)),
        ],
        compiler_params=pltpu.CompilerParams(
            collective_id=0, has_side_effects=True, vmem_limit_bytes=60 << 20
        ),
    )(queries, keys, values, rates.T, w_up[0], w_gate[0], w_down[0], w_out)


def solution(mesh):
    def body(*args):
        return shards(mesh.shape["ctx"], *args)

    return jax.shard_map(
        body,
        mesh=mesh,
        in_specs=(
            P("ctx", "head"),
            P("ctx", "head"),
            P("ctx", "head"),
            P("ctx", "head"),
            P("head", None, None),
            P("head", None, None),
            P("head", None, None),
            P("head", None),
        ),
        out_specs=P("ctx", "head"),
        check_vma=False,
    )
```

```python
import functools

import jax
import jax.numpy as jnp
from jax import lax
from jax.experimental import pallas as pl
from jax.experimental.pallas import tpu as pltpu
from jax.sharding import PartitionSpec as P

STEPS = 2
F32 = jnp.float32
BF16 = jnp.bfloat16
MESH = pl.DeviceIdType.MESH
GROUP = 3
LANE_PARTS = 2
CORES = 2
RING_ROWS = 4
TILES = (4, 2, 2)
PIECES = 2
STRIPES = 5
COPY_PIECES = 8
FIRST_SENT = (2, 0, 1)


def ring_place(chip, width):
    row, turn = chip // width, width - 1 - chip % width
    odd = turn % 2
    along = (1 - odd) * (row - 1) + odd * (RING_ROWS - 1 - row)
    return jnp.where(row == 0, chip, width + (RING_ROWS - 1) * turn + along)


def ring_chip(place, width):
    past = jnp.maximum(place - width, 0)
    turn, along = past // (RING_ROWS - 1), past % (RING_ROWS - 1)
    odd = turn % 2
    row = (1 - odd) * (1 + along) + odd * (RING_ROWS - 1 - along)
    return jnp.where(place < width, place, row * width + width - 1 - turn)


def dot(left, right, dims=((1,), (0,))):
    return lax.dot_general(left, right, (dims, ((), ())), preferred_element_type=F32)


def square_sum(block):
    return jnp.sum((block * block).reshape(-1, 8, block.shape[-1]), axis=0)


def lane_fold(block):
    return block[:, :128] + block[:, 128:]


def layer_kernel(n_ctx, q, k, v, r, w0, w1, w2, w_out, out, *scratch):
    (
        ks, us, qs, vin, kt, ut, first0, first1, in2, first2,
        acts, mid, grads, blocks, arrived, kept, tally, tally_in, norm_sums,
        hq, near_hid, far_hid, near_w2, far_w2, far_scale, scale_out,
        w_near, w_far, near, total_out, staged,
        ring_send, ring_recv, pair_send, pair_recv, tally_send, tally_recv,
        side_send, side_recv, w2_send, w2_recv, near_send, near_recv, hid_send, hid_recv, local_sem, out_sem,
    ) = scratch
    tokens, rows = k.shape
    cols = first0.shape[1]
    half = w_out.shape[1] // 2
    ring = n_ctx // CORES
    width = ring // RING_ROWS
    size = rows // ring
    bits = n_ctx.bit_length() - 1
    me = lax.axis_index("ctx")
    head = lax.axis_index("head")
    core = me % CORES
    chip = me // CORES
    place = ring_place(chip, width)
    right = {"ctx": ring_chip((place + 1) % ring, width) * CORES + core}
    left = {"ctx": ring_chip((place + ring - 1) % ring, width) * CORES + core}
    sibling = {"ctx": chip * CORES + 1 - core}
    across = {"head": 1 - head}
    diagonal = {"ctx": chip * CORES + 1 - core, "head": 1 - head}
    tally_partners = [
        {"ctx": me + (1 - 2 * ((me // (1 << bit)) % 2)) * (1 << bit)}
        for bit in range(bits)
    ]

    def remote(source, target, send_sem, recv_sem, device):
        return pltpu.make_async_remote_copy(
            src_ref=source,
            dst_ref=target,
            send_sem=send_sem,
            recv_sem=recv_sem,
            device_id=device,
            device_id_type=MESH,
        )

    def local(slot, source, target):
        return pltpu.make_async_copy(source, target, local_sem.at[slot])

    own_cols = pl.ds(pl.multiple_of(core * cols, 128), cols)
    own, other = slice(0, tokens), slice(tokens, 2 * tokens)
    loads = [
        local(0, k, ks.at[own, :]),
        local(1, v, vin),
        local(2, w0.at[:, own_cols], first0),
        local(3, w1.at[:, own_cols], first1),
        local(4, w2.at[pl.ds(pl.multiple_of(core * cols, 128), cols), :], in2),
        local(5, q, qs.at[own, :]),
    ]
    for load in loads[:5]:
        load.start()

    partners = [right, left, sibling, across, diagonal] + tally_partners
    barrier = pltpu.get_barrier_semaphore()
    for target in partners:
        pl.semaphore_signal(barrier, inc=1, device_id=target, device_id_type=MESH)
    pl.semaphore_wait(barrier, len(partners))

    def pair(slot, source, target):
        return remote(source, target, pair_send.at[slot], pair_recv.at[slot], sibling)

    k_pair = pair(0, k, ks.at[other, :])
    k_pair.start()
    loads[5].start()
    near_cols = pl.ds(pl.multiple_of(head * half, 128), half)
    far_cols = pl.ds(pl.multiple_of((1 - head) * half, 128), half)
    depth = rows // CORES
    own_rows = pl.ds(pl.multiple_of(core * depth, depth), depth)
    w_swap = remote(
        w_out.at[own_rows, far_cols], w_far.at[own_rows, :],
        side_send.at[0], side_recv.at[0], across,
    )
    w_swap.start()

    loads[1].wait()
    rate = jnp.broadcast_to(r[...], (128, tokens)).T
    for t in range(rows // 128):
        at = slice(t * 128, (t + 1) * 128)
        scaled = (rate * vin[:, at].astype(F32)).astype(BF16)
        us[own, at] = scaled
        ut[at, own] = scaled.T
    u_pair = pair(1, us.at[own, :], us.at[other, :])
    u_pair.start()

    def turned(source, target, side):
        for t in range(rows // 128):
            at = slice(t * 128, (t + 1) * 128)
            target[at, side] = source[side, at].T

    loads[0].wait()
    turned(ks, kt, own)
    q_pair = pair(2, q, qs.at[other, :])
    q_pair.start()
    w_copy = local(6, w_out.at[:, near_cols], w_near)
    w_copy.start()
    for load in loads[2:5]:
        load.wait()
    for t in range(rows // 128):
        at = slice(t * 128, (t + 1) * 128)
        first2[at, :] = in2[:, at].T

    firsts = (first0, first1, first2)
    scales = [None] * GROUP

    def weight(step, w):
        if step == 0:
            return firsts[w][...]
        return jnp.concatenate([blocks[2 * w], blocks[2 * w + 1]], axis=1)

    def act_dot(step, w, source, at):
        product = dot(source[at, :], weight(step, w))
        acts[w, at, :] = product

    for w, source in enumerate((ks, ks, us)):
        act_dot(0, w, source, own)

    half_pieces = tokens // 128
    whole = (0, 2 * half_pieces)

    def hid_gates(by, span):
        def one(piece, carry):
            at = pl.ds(pl.multiple_of(piece * 128, 128), 128)
            act, lin = acts[0, at, :], acts[1, at, :]
            if by[0] is not None:
                act, lin = act * by[0], lin * by[1]
            mid[2, at, :] = (act * jax.nn.sigmoid(act) * lin).astype(BF16)
            return carry

        lax.fori_loop(*span, one, 0)

    def err_gates(by, span):
        def one(piece, carry):
            at = pl.ds(pl.multiple_of(piece * 128, 128), 128)
            act, lin, err = acts[0, at, :], acts[1, at, :], acts[2, at, :]
            if by[0] is not None:
                act, lin, err = act * by[0], lin * by[1], err * by[2]
            sig = jax.nn.sigmoid(act)
            mid[0, at, :] = (err * lin * sig * (1.0 + act * (1.0 - sig))).astype(BF16)
            mid[1, at, :] = (err * (act * sig)).astype(BF16)
            return carry

        lax.fori_loop(*span, one, 0)

    hid_gates(scales, (0, half_pieces))
    err_gates(scales, (0, half_pieces))
    k_pair.wait_recv()
    act_dot(0, 0, ks, other)
    act_dot(0, 1, ks, other)
    hid_gates(scales, (half_pieces, 2 * half_pieces))

    flows = [(w, h) for w in range(GROUP) for h in range(LANE_PARTS)]

    def reach(h):
        longer = ring // 2
        return (longer, ring - 1 - longer) if h == 0 else (ring - 1 - longer, longer)

    def chunk(number):
        return pl.ds(pl.multiple_of((number % ring) * size, size), size)

    copies = {}

    def ring_sent(phase):
        all_sent = grads.at[:, : (ring - 1) * size, :]
        remote(all_sent, all_sent, ring_send.at[phase], ring_recv.at[0, 0], right).wait_send()

    for step in range(STEPS):

        def send(flow, slot, source, target, device):
            phase = ring_send.at[0 if slot < ring - 1 else 1]
            copy = remote(source, target, phase, ring_recv.at[flow, slot], device)
            copy.start()
            copies[flow, slot] = copy

        def send_sum(flow, to_right, s):
            far, back = reach(flow % LANE_PARTS)
            at = chunk(place + far - s) if to_right else chunk(place + ring - back + s)
            slot = s if to_right else far + s
            device = right if to_right else left
            send(flow, slot, grads.at[flow, at, :], arrived.at[flow, slot], device)

        def send_block(flow, to_right, t):
            far, back = reach(flow % LANE_PARTS)
            at = chunk(place + ring - t) if to_right else chunk(place + t)
            slot = ring - 1 + (t if to_right else far + t)
            device = right if to_right else left
            here = blocks.at[flow, at, :]
            send(flow, slot, here, here, device)

        def pass_sum(flow, to_right, s):
            far, back = reach(flow % LANE_PARTS)
            slot = s if to_right else far + s
            at = chunk(place + far - 1 - s) if to_right else chunk(place + ring + 1 - back + s)
            copies[flow, slot].wait_recv()
            total = grads[flow, at, :].astype(F32) + arrived[flow, slot].astype(F32)
            grads[flow, at, :] = total.astype(BF16)
            send_sum(flow, to_right, s + 1)

        def send_w2(flow, number):
            here = chunk(number)
            target = far_w2.at[flow % LANE_PARTS, here, :]
            remote(blocks.at[flow, here, :], target, w2_send, w2_recv, across).start()
            target = near_w2.at[flow % LANE_PARTS, here, :]
            remote(
                blocks.at[flow, here, :], target, near_send, near_recv, sibling
            ).start()

        def grad(w):
            source = ut if w == 2 else kt

            for piece in range(PIECES):
                at = slice(piece * (rows // PIECES), (piece + 1) * (rows // PIECES))
                product = dot(source[at, :], mid[w]).astype(BF16)
                grads[2 * w, at, :] = product[:, :128]
                grads[2 * w + 1, at, :] = product[:, 128:]
            for h in range(LANE_PARTS):
                send_sum(2 * w + h, True, 0)
                send_sum(2 * w + h, False, 0)

        if step == 0:
            u_pair.wait_recv()
            turned(us, ut, other)
            grad(2)
            act_dot(0, 2, us, other)
            err_gates(scales, (half_pieces, 2 * half_pieces))
            turned(ks, kt, other)
        else:
            err_gates(scales, whole)
        grad(0)
        grad(1)
        if step == 0:
            for w in range(GROUP):
                norm_sums[0, w] = lane_fold(square_sum(firsts[w][...].astype(F32)))
            norm_pair = pair(3, norm_sums.at[0], norm_sums.at[1])
            norm_pair.start()
        turn = ring // 2 - 1
        ordered = [2 * w + h for w in range(GROUP) for h in range(LANE_PARTS)]
        for s in range(turn):
            for flow in ordered:
                far, back = reach(flow % LANE_PARTS)
                if s < far - 1:
                    pass_sum(flow, True, s)
                if s < back - 1:
                    pass_sum(flow, False, s)
        for flow in ordered:
            far, back = reach(flow % LANE_PARTS)
            w, h = flows[flow]
            at = chunk(place)
            copies[flow, far - 1].wait_recv()
            copies[flow, ring - 2].wait_recv()
            total = grads[flow, at, :].astype(F32) + arrived[flow, far - 1].astype(F32)
            total = total + arrived[flow, ring - 2].astype(F32)
            if step == 0:
                lanes = slice(h * 128, (h + 1) * 128)
                moved = firsts[w][at, lanes].astype(F32) + total
            else:
                moved = kept[flow] * scales[w] + total
            kept[flow] = moved
            rounded = moved.astype(BF16)
            blocks[flow, at, :] = rounded
            send_block(flow, True, 0)
            send_block(flow, False, 0)
            if step == STEPS - 1 and w == 2:
                send_w2(flow, place)
            part = square_sum(rounded.astype(F32))
            tally[0, w] = part if h == 0 else tally[0, w] + part
        tallies = []

        def start_tally(stage):
            copy = remote(
                tally.at[stage], tally_in.at[step * bits + stage],
                tally_send.at[stage], tally_recv.at[step * bits + stage],
                tally_partners[stage],
            )
            copy.start()
            tallies.append(copy)

        def end_tally(stage):
            tallies[stage].wait_recv()
            tally[stage + 1] = tally[stage] + tally_in[step * bits + stage]
            if stage + 1 < bits:
                start_tally(stage + 1)

        def take_block(flow, t):
            far, back = reach(flow % LANE_PARTS)
            for to_right, count in ((True, far), (False, back)):
                if t >= count:
                    continue
                copies[flow, ring - 1 + (t if to_right else far + t)].wait_recv()
                if t < count - 1:
                    send_block(flow, to_right, t + 1)
                if step == STEPS - 1 and flow // LANE_PARTS == 2:
                    send_w2(flow, place + (ring - 1 - t if to_right else 1 + t))

        start_tally(0)
        ended = 0
        for t in range(turn):
            for flow in ordered:
                take_block(flow, t)
                if flow == ordered[3] and ended < bits - 1:
                    end_tally(ended)
                    ended += 1
        if step == 0:
            norm_pair.wait()
            norms = [
                jnp.sqrt(jnp.sum(norm_sums[0, w] + norm_sums[1, w], keepdims=True))
                for w in range(GROUP)
            ]
        else:
            q_pair.wait_recv()
            loads[5].wait()
        source = ks if step == 0 else qs
        for w in range(2):
            for h in range(LANE_PARTS):
                take_block(2 * w + h, turn)
            act_dot(1, w, source, own)
            act_dot(1, w, source, other)
        while ended < bits:
            end_tally(ended)
            ended += 1
        scales = [
            norms[w] / jnp.sqrt(jnp.sum(tally[bits, w], keepdims=True) + 1e-06)
            for w in range(GROUP)
        ]
        ring_sent(0)
        if step == 0:
            hid_gates(scales, whole)
            grad(2)
            for h in range(LANE_PARTS):
                take_block(4 + h, turn)
            act_dot(1, 2, us, own)
            act_dot(1, 2, us, other)
        ring_sent(1)
        for copy in tallies:
            copy.wait_send()

    ends = [tokens * sum(TILES[: t + 1]) // sum(TILES) for t in range(len(TILES))]
    tiles = [(end - tokens * part // sum(TILES), end) for end, part in zip(ends, TILES)]
    scale_out[...] = jnp.broadcast_to(scales[2], scale_out.shape)
    scale_swap = remote(
        scale_out, far_scale, side_send.at[1], side_recv.at[1], across
    )
    scale_swap.start()
    hid_copies = []

    def send_hid(slot, source, target, device):
        copy = remote(source, target, hid_send, hid_recv.at[slot], device)
        copy.start()
        return copy

    def hidden_of(side, first, last):
        at = slice(side * tokens + first, side * tokens + last)
        act = acts[0, at, :] * scales[0]
        lin = acts[1, at, :] * scales[1]
        hq[at, :] = (act * jax.nn.sigmoid(act) * lin).astype(BF16)

    def send_tile(t):
        first, last = tiles[t]
        to, at = slice(first, last), slice(tokens + first, tokens + last)
        hid_copies.append((
            send_hid(2 * t, hq.at[to, :], far_hid.at[0, to, :], across),
            send_hid(2 * t + 1, hq.at[at, :], far_hid.at[1, to, :], diagonal),
        ))

    for h in range(LANE_PARTS):
        take_block(4 + h, turn)
    for side in range(CORES):
        hidden_of(side, *tiles[0])
    send_tile(0)
    for side in (1, 0):
        hidden_of(side, tiles[1][0], tokens)
    near_copy = send_hid(2 * len(TILES), hq.at[other, :], near_hid, sibling)
    send_tile(1)
    w_swap.wait()
    w_share = pair(4, w_far.at[own_rows, :], w_far.at[own_rows, :])
    w_share.start()
    wide = ((1,), (1,))
    stripe = half // STRIPES

    def near_stripes(first, last):
        def one(c, carry):
            lanes = pl.ds(pl.multiple_of(c * stripe, 128), stripe)
            total_out[:, lanes] = dot(near[...], w_near[:, lanes])
            return carry

        lax.fori_loop(first, last, one, 0)

    remote(near_w2, near_w2, near_send, near_recv, sibling).wait()
    near_copy.wait_recv()
    mine = dot(hq[own, :], jnp.concatenate([blocks[4], blocks[5]], axis=1), wide)
    theirs = dot(near_hid[...], jnp.concatenate([near_w2[0], near_w2[1]], axis=1), wide)
    near[...] = ((mine + theirs) * scales[2]).astype(BF16)
    send_tile(2)
    w_copy.wait()
    near_stripes(0, STRIPES - 2)
    remote(far_w2.at[0:2], far_w2.at[0:2], w2_send, w2_recv, across).wait()
    far_pair = pair(5, far_w2.at[0:2], far_w2.at[2:4])
    far_pair.start()
    near_stripes(STRIPES - 2, STRIPES)
    scale_swap.wait()
    w_share.wait()
    far_pair.wait()
    scale = jnp.max(far_scale[...], keepdims=True)
    for t, (first, last) in enumerate(tiles):
        at = slice(first, last)
        hid_copies[t][0].wait_recv()
        hid_copies[t][1].wait_recv()
        mine = dot(
            far_hid[0, at, :], jnp.concatenate([far_w2[0], far_w2[1]], axis=1), wide
        )
        theirs = dot(
            far_hid[1, at, :], jnp.concatenate([far_w2[2], far_w2[3]], axis=1), wide
        )
        near[at, :] = ((mine + theirs) * scale).astype(BF16)

        def far_cols_of(c, carry):
            lanes = pl.ds(pl.multiple_of(c * stripe, 128), stripe)
            added = total_out[at, lanes] + dot(near[at, :], w_far[:, lanes])
            staged[at, lanes] = added.astype(BF16)
            pltpu.make_async_copy(staged.at[at, lanes], out.at[at, lanes], out_sem).start()
            return carry

        lax.fori_loop(0, STRIPES, far_cols_of, 0)
    pltpu.make_async_copy(staged, out, out_sem).wait()
    hid_sent = us.at[: (CORES + 1) * tokens * cols // rows, :]
    remote(hid_sent, hid_sent, hid_send, hid_recv.at[0], sibling).wait_send()
    for copy in (k_pair, u_pair, q_pair):
        copy.wait_send()


def copy_kernel(source, target, held, in_sem, out_sem):
    rows = held.shape[0] // COPY_PIECES
    pieces = [pl.ds(piece * rows, rows) for piece in range(COPY_PIECES)]
    reads = [
        pltpu.make_async_copy(source.at[at, :], held.at[at, :], in_sem.at[piece])
        for piece, at in enumerate(pieces)
    ]
    for read in reads:
        read.start()
    for read, at in zip(reads, pieces):
        read.wait()
        pltpu.make_async_copy(held.at[at, :], target.at[at, :], out_sem).start()
    pltpu.make_async_copy(held, target, out_sem).wait()


def shards(n_ctx, queries, keys, values, rates, w_up, w_gate, w_down, w_out):
    tokens, rows = keys.shape
    cols = w_up.shape[2] // CORES
    half = w_out.shape[1] // 2
    ring = n_ctx // CORES
    size = rows // ring
    bits = n_ctx.bit_length() - 1
    flows = GROUP * LANE_PARTS
    vmem = pl.BlockSpec(memory_space=pltpu.VMEM)
    anywhere = pl.BlockSpec(memory_space=pl.ANY)
    dma = pltpu.SemaphoreType.DMA
    mixed = pl.pallas_call(
        functools.partial(layer_kernel, n_ctx),
        out_shape=jax.ShapeDtypeStruct((tokens, half), BF16),
        in_specs=[anywhere] * 3 + [vmem] + [anywhere] * 4,
        out_specs=anywhere,
        scratch_shapes=[
            pltpu.VMEM((2 * tokens, rows), BF16),
            pltpu.VMEM((2 * tokens, rows), BF16),
            pltpu.VMEM((2 * tokens, rows), BF16),
            pltpu.VMEM((tokens, rows), BF16),
            pltpu.VMEM((rows, 2 * tokens), BF16),
            pltpu.VMEM((rows, 2 * tokens), BF16),
            pltpu.VMEM((rows, cols), BF16),
            pltpu.VMEM((rows, cols), BF16),
            pltpu.VMEM((cols, rows), BF16),
            pltpu.VMEM((rows, cols), BF16),
            pltpu.VMEM((GROUP, 2 * tokens, cols), F32),
            pltpu.VMEM((GROUP, 2 * tokens, cols), BF16),
            pltpu.VMEM((flows, rows, cols // LANE_PARTS), BF16),
            pltpu.VMEM((flows, rows, cols // LANE_PARTS), BF16),
            pltpu.VMEM((flows, ring - 1, size, cols // LANE_PARTS), BF16),
            pltpu.VMEM((flows, size, cols // LANE_PARTS), F32),
            pltpu.VMEM((bits + 1, GROUP, 8, 128), F32),
            pltpu.VMEM((STEPS * bits, GROUP, 8, 128), F32),
            pltpu.VMEM((CORES, GROUP, 8, 128), F32),
            pltpu.VMEM((2 * tokens, cols), BF16),
            pltpu.VMEM((tokens, cols), BF16),
            pltpu.VMEM((CORES, tokens, cols), BF16),
            pltpu.VMEM((LANE_PARTS, rows, cols // LANE_PARTS), BF16),
            pltpu.VMEM((CORES * LANE_PARTS, rows, cols // LANE_PARTS), BF16),
            pltpu.VMEM((8, 128), F32),
            pltpu.VMEM((8, 128), F32),
            pltpu.VMEM((rows, half), BF16),
            pltpu.VMEM((rows, half), BF16),
            pltpu.VMEM((tokens, rows), BF16),
            pltpu.VMEM((tokens, half), F32),
            pltpu.VMEM((tokens, half), BF16),
            dma((2,)),
            dma((flows, 2 * (ring - 1))),
            dma((6,)),
            dma((6,)),
            dma((bits,)),
            dma((STEPS * bits,)),
            dma((2,)),
            dma((2,)),
            dma,
            dma,
            dma,
            dma,
            dma,
            dma((2 * len(TILES) + 1,)),
            dma((7,)),
            dma,
        ],
        compiler_params=pltpu.CompilerParams(
            collective_id=0, has_side_effects=True, vmem_limit_bytes=60 << 20
        ),
    )(queries, keys, values, rates.T, w_up[0], w_gate[0], w_down[0], w_out)
    return pl.pallas_call(
        copy_kernel,
        out_shape=jax.ShapeDtypeStruct((tokens, half), BF16),
        in_specs=[anywhere],
        out_specs=anywhere,
        scratch_shapes=[pltpu.VMEM((tokens, half), BF16), dma((COPY_PIECES,)), dma],
    )(mixed)


def solution(mesh):
    def body(*args):
        return shards(mesh.shape["ctx"], *args)

    return jax.shard_map(
        body,
        mesh=mesh,
        in_specs=(
            P("ctx", "head"),
            P("ctx", "head"),
            P("ctx", "head"),
            P("ctx", "head"),
            P("head", None, None),
            P("head", None, None),
            P("head", None, None),
            P("head", None),
        ),
        out_specs=P("ctx", "head"),
        check_vma=False,
    )
```

```python
import functools

import jax
import jax.numpy as jnp
from jax import lax
from jax.experimental import pallas as pl
from jax.experimental.pallas import tpu as pltpu
from jax.sharding import PartitionSpec as P

STEPS = 2
F32 = jnp.float32
BF16 = jnp.bfloat16
MESH = pl.DeviceIdType.MESH
GROUP = 3
LANE_PARTS = 2
CORES = 2
RING_ROWS = 4
TILES = (4, 2, 2)
PIECES = 2
STRIPES = 5
COPY_PIECES = 8


def ring_place(chip, width):
    row, turn = chip // width, width - 1 - chip % width
    odd = turn % 2
    along = (1 - odd) * (row - 1) + odd * (RING_ROWS - 1 - row)
    return jnp.where(row == 0, chip, width + (RING_ROWS - 1) * turn + along)


def ring_chip(place, width):
    past = jnp.maximum(place - width, 0)
    turn, along = past // (RING_ROWS - 1), past % (RING_ROWS - 1)
    odd = turn % 2
    row = (1 - odd) * (1 + along) + odd * (RING_ROWS - 1 - along)
    return jnp.where(place < width, place, row * width + width - 1 - turn)


def dot(left, right, dims=((1,), (0,))):
    return lax.dot_general(left, right, (dims, ((), ())), preferred_element_type=F32)


def square_sum(block):
    return jnp.sum((block * block).reshape(-1, 8, block.shape[-1]), axis=0)


def lane_fold(block):
    return block[:, :128] + block[:, 128:]


def layer_kernel(n_ctx, q, k, v, r, w0, w1, w2, w_out, out, *scratch):
    (
        ks, us, qs, vin, kt, ut, first0, first1, in2, first2,
        acts, mid, grads, blocks, arrived, kept, tally, tally_in, norm_sums,
        hq, near_hid, far_hid, near_w2, far_w2, far_scale, scale_out,
        w_near, w_far, near, total_out, staged,
        ring_send, ring_recv, pair_send, pair_recv, tally_send, tally_recv,
        side_send, side_recv, w2_send, w2_recv, near_send, near_recv, hid_send, hid_recv, local_sem, out_sem,
    ) = scratch
    tokens, rows = k.shape
    cols = first0.shape[1]
    half = w_out.shape[1] // 2
    ring = n_ctx // CORES
    width = ring // RING_ROWS
    size = rows // ring
    bits = n_ctx.bit_length() - 1
    me = lax.axis_index("ctx")
    head = lax.axis_index("head")
    core = me % CORES
    chip = me // CORES
    place = ring_place(chip, width)
    right = {"ctx": ring_chip((place + 1) % ring, width) * CORES + core}
    left = {"ctx": ring_chip((place + ring - 1) % ring, width) * CORES + core}
    sibling = {"ctx": chip * CORES + 1 - core}
    across = {"head": 1 - head}
    diagonal = {"ctx": chip * CORES + 1 - core, "head": 1 - head}
    tally_partners = [
        {"ctx": me + (1 - 2 * ((me // (1 << bit)) % 2)) * (1 << bit)}
        for bit in range(bits)
    ]

    def remote(source, target, send_sem, recv_sem, device):
        return pltpu.make_async_remote_copy(
            src_ref=source,
            dst_ref=target,
            send_sem=send_sem,
            recv_sem=recv_sem,
            device_id=device,
            device_id_type=MESH,
        )

    def local(slot, source, target):
        return pltpu.make_async_copy(source, target, local_sem.at[slot])

    own_cols = pl.ds(pl.multiple_of(core * cols, 128), cols)
    own, other = slice(0, tokens), slice(tokens, 2 * tokens)
    loads = [
        local(0, k, ks.at[own, :]),
        local(1, v, vin),
        local(2, w0.at[:, own_cols], first0),
        local(3, w1.at[:, own_cols], first1),
        local(4, w2.at[pl.ds(pl.multiple_of(core * cols, 128), cols), :], in2),
        local(5, q, qs.at[own, :]),
    ]
    for load in loads[:5]:
        load.start()

    partners = [right, left, sibling, across, diagonal] + tally_partners
    barrier = pltpu.get_barrier_semaphore()
    for target in partners:
        pl.semaphore_signal(barrier, inc=1, device_id=target, device_id_type=MESH)
    pl.semaphore_wait(barrier, len(partners))

    def pair(slot, source, target):
        return remote(source, target, pair_send.at[slot], pair_recv.at[slot], sibling)

    k_pair = pair(0, k, ks.at[other, :])
    k_pair.start()
    loads[5].start()
    near_cols = pl.ds(pl.multiple_of(head * half, 128), half)
    far_cols = pl.ds(pl.multiple_of((1 - head) * half, 128), half)
    depth = rows // CORES
    own_rows = pl.ds(pl.multiple_of(core * depth, depth), depth)
    w_swap = remote(
        w_out.at[own_rows, far_cols], w_far.at[own_rows, :],
        side_send.at[0], side_recv.at[0], across,
    )
    w_swap.start()

    loads[1].wait()
    rate = jnp.broadcast_to(r[...], (128, tokens)).T
    for t in range(rows // 128):
        at = slice(t * 128, (t + 1) * 128)
        scaled = (rate * vin[:, at].astype(F32)).astype(BF16)
        us[own, at] = scaled
        ut[at, own] = scaled.T
    u_pair = pair(1, us.at[own, :], us.at[other, :])
    u_pair.start()

    def turned(source, target, side):
        for t in range(rows // 128):
            at = slice(t * 128, (t + 1) * 128)
            target[at, side] = source[side, at].T

    loads[0].wait()
    turned(ks, kt, own)
    q_pair = pair(2, q, qs.at[other, :])
    q_pair.start()
    w_copy = local(6, w_out.at[:, near_cols], w_near)
    w_copy.start()
    for load in loads[2:5]:
        load.wait()
    for t in range(rows // 128):
        at = slice(t * 128, (t + 1) * 128)
        first2[at, :] = in2[:, at].T

    firsts = (first0, first1, first2)
    scales = [None] * GROUP

    def weight(step, w):
        if step == 0:
            return firsts[w][...]
        return jnp.concatenate([blocks[2 * w], blocks[2 * w + 1]], axis=1)

    def act_dot(step, w, source, at):
        product = dot(source[at, :], weight(step, w))
        acts[w, at, :] = product

    for w, source in enumerate((ks, ks, us)):
        act_dot(0, w, source, own)

    half_pieces = tokens // 128
    whole = (0, 2 * half_pieces)

    def hid_gates(by, span):
        def one(piece, carry):
            at = pl.ds(pl.multiple_of(piece * 128, 128), 128)
            act, lin = acts[0, at, :], acts[1, at, :]
            if by[0] is not None:
                act, lin = act * by[0], lin * by[1]
            mid[2, at, :] = (act * jax.nn.sigmoid(act) * lin).astype(BF16)
            return carry

        lax.fori_loop(*span, one, 0)

    def err_gates(by, span):
        def one(piece, carry):
            at = pl.ds(pl.multiple_of(piece * 128, 128), 128)
            act, lin, err = acts[0, at, :], acts[1, at, :], acts[2, at, :]
            if by[0] is not None:
                act, lin, err = act * by[0], lin * by[1], err * by[2]
            sig = jax.nn.sigmoid(act)
            mid[0, at, :] = (err * lin * sig * (1.0 + act * (1.0 - sig))).astype(BF16)
            mid[1, at, :] = (err * (act * sig)).astype(BF16)
            return carry

        lax.fori_loop(*span, one, 0)

    hid_gates(scales, (0, half_pieces))
    err_gates(scales, (0, half_pieces))
    k_pair.wait_recv()
    act_dot(0, 0, ks, other)
    act_dot(0, 1, ks, other)
    hid_gates(scales, (half_pieces, 2 * half_pieces))

    flows = [(w, h) for w in range(GROUP) for h in range(LANE_PARTS)]

    def reach(h):
        longer = ring // 2
        return (longer, ring - 1 - longer) if h == 0 else (ring - 1 - longer, longer)

    def chunk(number):
        return pl.ds(pl.multiple_of((number % ring) * size, size), size)

    copies = {}

    def ring_sent(phase):
        all_sent = grads.at[:, : (ring - 1) * size, :]
        remote(all_sent, all_sent, ring_send.at[phase], ring_recv.at[0, 0], right).wait_send()

    for step in range(STEPS):

        def send(flow, slot, source, target, device):
            phase = ring_send.at[0 if slot < ring - 1 else 1]
            copy = remote(source, target, phase, ring_recv.at[flow, slot], device)
            copy.start()
            copies[flow, slot] = copy

        def send_sum(flow, to_right, s):
            far, back = reach(flow % LANE_PARTS)
            at = chunk(place + far - s) if to_right else chunk(place + ring - back + s)
            slot = s if to_right else far + s
            device = right if to_right else left
            send(flow, slot, grads.at[flow, at, :], arrived.at[flow, slot], device)

        def send_block(flow, to_right, t):
            far, back = reach(flow % LANE_PARTS)
            at = chunk(place + ring - t) if to_right else chunk(place + t)
            slot = ring - 1 + (t if to_right else far + t)
            device = right if to_right else left
            here = blocks.at[flow, at, :]
            send(flow, slot, here, here, device)

        def pass_sum(flow, to_right, s):
            far, back = reach(flow % LANE_PARTS)
            slot = s if to_right else far + s
            at = chunk(place + far - 1 - s) if to_right else chunk(place + ring + 1 - back + s)
            copies[flow, slot].wait_recv()
            total = grads[flow, at, :].astype(F32) + arrived[flow, slot].astype(F32)
            grads[flow, at, :] = total.astype(BF16)
            send_sum(flow, to_right, s + 1)

        def send_w2(flow, number):
            here = chunk(number)
            target = far_w2.at[flow % LANE_PARTS, here, :]
            remote(blocks.at[flow, here, :], target, w2_send, w2_recv, across).start()
            target = near_w2.at[flow % LANE_PARTS, here, :]
            remote(
                blocks.at[flow, here, :], target, near_send, near_recv, sibling
            ).start()

        def grad(w):
            source = ut if w == 2 else kt

            for piece in range(PIECES):
                at = slice(piece * (rows // PIECES), (piece + 1) * (rows // PIECES))
                product = dot(source[at, :], mid[w]).astype(BF16)
                grads[2 * w, at, :] = product[:, :128]
                grads[2 * w + 1, at, :] = product[:, 128:]
            for h in range(LANE_PARTS):
                send_sum(2 * w + h, True, 0)
                send_sum(2 * w + h, False, 0)

        if step == 0:
            u_pair.wait_recv()
            turned(us, ut, other)
            grad(2)
            act_dot(0, 2, us, other)
            err_gates(scales, (half_pieces, 2 * half_pieces))
            turned(ks, kt, other)
        else:
            err_gates(scales, whole)
        grad(0)
        grad(1)
        if step == 0:
            for w in range(GROUP):
                norm_sums[0, w] = lane_fold(square_sum(firsts[w][...].astype(F32)))
            norm_pair = pair(3, norm_sums.at[0], norm_sums.at[1])
            norm_pair.start()
        turn = ring // 2 - 1
        ordered = [2 * w + h for w in range(GROUP) for h in range(LANE_PARTS)]
        for s in range(turn):
            for flow in ordered:
                far, back = reach(flow % LANE_PARTS)
                if s < far - 1:
                    pass_sum(flow, True, s)
                if s < back - 1:
                    pass_sum(flow, False, s)
        for flow in ordered:
            far, back = reach(flow % LANE_PARTS)
            w, h = flows[flow]
            at = chunk(place)
            copies[flow, far - 1].wait_recv()
            copies[flow, ring - 2].wait_recv()
            total = grads[flow, at, :].astype(F32) + arrived[flow, far - 1].astype(F32)
            total = total + arrived[flow, ring - 2].astype(F32)
            if step == 0:
                lanes = slice(h * 128, (h + 1) * 128)
                moved = firsts[w][at, lanes].astype(F32) + total
            else:
                moved = kept[flow] * scales[w] + total
            kept[flow] = moved
            rounded = moved.astype(BF16)
            blocks[flow, at, :] = rounded
            send_block(flow, True, 0)
            send_block(flow, False, 0)
            if step == STEPS - 1 and w == 2:
                send_w2(flow, place)
            part = square_sum(rounded.astype(F32))
            tally[0, w] = part if h == 0 else tally[0, w] + part
        tallies = []

        def start_tally(stage):
            copy = remote(
                tally.at[stage], tally_in.at[step * bits + stage],
                tally_send.at[stage], tally_recv.at[step * bits + stage],
                tally_partners[stage],
            )
            copy.start()
            tallies.append(copy)

        def end_tally(stage):
            tallies[stage].wait_recv()
            tally[stage + 1] = tally[stage] + tally_in[step * bits + stage]
            if stage + 1 < bits:
                start_tally(stage + 1)

        def take_block(flow, t):
            far, back = reach(flow % LANE_PARTS)
            for to_right, count in ((True, far), (False, back)):
                if t >= count:
                    continue
                copies[flow, ring - 1 + (t if to_right else far + t)].wait_recv()
                if t < count - 1:
                    send_block(flow, to_right, t + 1)
                if step == STEPS - 1 and flow // LANE_PARTS == 2:
                    send_w2(flow, place + (ring - 1 - t if to_right else 1 + t))

        start_tally(0)
        ended = 0
        for t in range(turn):
            for flow in ordered:
                take_block(flow, t)
                if flow == ordered[3] and ended < bits - 1:
                    end_tally(ended)
                    ended += 1
            if step == STEPS - 1 and t == turn // 2:
                w_swap.wait()
                w_share = pair(4, w_far.at[own_rows, :], w_far.at[own_rows, :])
                w_share.start()
        if step == 0:
            norm_pair.wait()
            norms = [
                jnp.sqrt(jnp.sum(norm_sums[0, w] + norm_sums[1, w], keepdims=True))
                for w in range(GROUP)
            ]
        else:
            q_pair.wait_recv()
            loads[5].wait()
        source = ks if step == 0 else qs
        for w in range(2):
            for h in range(LANE_PARTS):
                take_block(2 * w + h, turn)
            act_dot(1, w, source, own)
            act_dot(1, w, source, other)
        while ended < bits:
            end_tally(ended)
            ended += 1
        scales = [
            norms[w] / jnp.sqrt(jnp.sum(tally[bits, w], keepdims=True) + 1e-06)
            for w in range(GROUP)
        ]
        ring_sent(0)
        if step == 0:
            hid_gates(scales, whole)
            grad(2)
            for h in range(LANE_PARTS):
                take_block(4 + h, turn)
            act_dot(1, 2, us, own)
            act_dot(1, 2, us, other)
        ring_sent(1)
        for copy in tallies:
            copy.wait_send()

    ends = [tokens * sum(TILES[: t + 1]) // sum(TILES) for t in range(len(TILES))]
    tiles = [(end - tokens * part // sum(TILES), end) for end, part in zip(ends, TILES)]
    scale_out[...] = jnp.broadcast_to(scales[2], scale_out.shape)
    scale_swap = remote(
        scale_out, far_scale, side_send.at[1], side_recv.at[1], across
    )
    scale_swap.start()
    hid_copies = []

    def send_hid(slot, source, target, device):
        copy = remote(source, target, hid_send, hid_recv.at[slot], device)
        copy.start()
        return copy

    def hidden_of(side, first, last):
        at = slice(side * tokens + first, side * tokens + last)
        act = acts[0, at, :] * scales[0]
        lin = acts[1, at, :] * scales[1]
        hq[at, :] = (act * jax.nn.sigmoid(act) * lin).astype(BF16)

    def send_tile(t):
        first, last = tiles[t]
        to, at = slice(first, last), slice(tokens + first, tokens + last)
        hid_copies.append((
            send_hid(2 * t, hq.at[to, :], far_hid.at[0, to, :], across),
            send_hid(2 * t + 1, hq.at[at, :], far_hid.at[1, to, :], diagonal),
        ))

    for side in range(CORES):
        hidden_of(side, 0, tokens)
    for h in range(LANE_PARTS):
        take_block(4 + h, turn)
    near_copy = send_hid(2 * len(TILES), hq.at[other, :], near_hid, sibling)
    send_tile(0)
    wide = ((1,), (1,))
    stripe = half // STRIPES

    def near_stripes(first, last):
        def one(c, carry):
            lanes = pl.ds(pl.multiple_of(c * stripe, 128), stripe)
            total_out[:, lanes] = dot(near[...], w_near[:, lanes])
            return carry

        lax.fori_loop(first, last, one, 0)

    near_w2_copy = remote(near_w2, near_w2, near_send, near_recv, sibling)
    near_w2_copy.wait_recv()
    near_copy.wait_recv()
    mine = dot(hq[own, :], jnp.concatenate([blocks[4], blocks[5]], axis=1), wide)
    theirs = dot(near_hid[...], jnp.concatenate([near_w2[0], near_w2[1]], axis=1), wide)
    near[...] = ((mine + theirs) * scales[2]).astype(BF16)
    w_copy.wait()
    near_stripes(0, 2)
    for t in range(1, len(TILES)):
        send_tile(t)
    far_w2_copy = remote(far_w2.at[0:2], far_w2.at[0:2], w2_send, w2_recv, across)
    far_w2_copy.wait_recv()
    far_pair = pair(5, far_w2.at[0:2], far_w2.at[2:4])
    far_pair.start()
    near_stripes(2, STRIPES)
    scale_swap.wait()
    w_share.wait_recv()
    far_pair.wait_recv()
    scale = jnp.max(far_scale[...], keepdims=True)
    for t, (first, last) in enumerate(tiles):
        at = slice(first, last)
        hid_copies[t][0].wait_recv()
        hid_copies[t][1].wait_recv()
        mine = dot(
            far_hid[0, at, :], jnp.concatenate([far_w2[0], far_w2[1]], axis=1), wide
        )
        theirs = dot(
            far_hid[1, at, :], jnp.concatenate([far_w2[2], far_w2[3]], axis=1), wide
        )
        near[at, :] = ((mine + theirs) * scale).astype(BF16)

        def far_cols_of(c, carry):
            lanes = pl.ds(pl.multiple_of(c * stripe, 128), stripe)
            added = total_out[at, lanes] + dot(near[at, :], w_far[:, lanes])
            staged[at, lanes] = added.astype(BF16)
            pltpu.make_async_copy(staged.at[at, lanes], out.at[at, lanes], out_sem).start()
            return carry

        lax.fori_loop(0, STRIPES, far_cols_of, 0)
    pltpu.make_async_copy(staged, out, out_sem).wait()
    hid_sent = us.at[: (CORES + 1) * tokens * cols // rows, :]
    near_w2_copy.wait_send()
    far_w2_copy.wait_send()
    far_pair.wait_send()
    w_share.wait_send()
    remote(hid_sent, hid_sent, hid_send, hid_recv.at[0], sibling).wait_send()
    for copy in (k_pair, u_pair, q_pair):
        copy.wait_send()


def copy_kernel(source, target, held, in_sem, out_sem):
    rows = held.shape[0] // COPY_PIECES
    pieces = [pl.ds(piece * rows, rows) for piece in range(COPY_PIECES)]
    reads = [
        pltpu.make_async_copy(source.at[at, :], held.at[at, :], in_sem.at[piece])
        for piece, at in enumerate(pieces)
    ]
    for read in reads:
        read.start()
    for read, at in zip(reads, pieces):
        read.wait()
        pltpu.make_async_copy(held.at[at, :], target.at[at, :], out_sem).start()
    pltpu.make_async_copy(held, target, out_sem).wait()


def shards(n_ctx, queries, keys, values, rates, w_up, w_gate, w_down, w_out):
    tokens, rows = keys.shape
    cols = w_up.shape[2] // CORES
    half = w_out.shape[1] // 2
    ring = n_ctx // CORES
    size = rows // ring
    bits = n_ctx.bit_length() - 1
    flows = GROUP * LANE_PARTS
    vmem = pl.BlockSpec(memory_space=pltpu.VMEM)
    anywhere = pl.BlockSpec(memory_space=pl.ANY)
    dma = pltpu.SemaphoreType.DMA
    mixed = pl.pallas_call(
        functools.partial(layer_kernel, n_ctx),
        out_shape=jax.ShapeDtypeStruct((tokens, half), BF16),
        in_specs=[anywhere] * 3 + [vmem] + [anywhere] * 4,
        out_specs=anywhere,
        scratch_shapes=[
            pltpu.VMEM((2 * tokens, rows), BF16),
            pltpu.VMEM((2 * tokens, rows), BF16),
            pltpu.VMEM((2 * tokens, rows), BF16),
            pltpu.VMEM((tokens, rows), BF16),
            pltpu.VMEM((rows, 2 * tokens), BF16),
            pltpu.VMEM((rows, 2 * tokens), BF16),
            pltpu.VMEM((rows, cols), BF16),
            pltpu.VMEM((rows, cols), BF16),
            pltpu.VMEM((cols, rows), BF16),
            pltpu.VMEM((rows, cols), BF16),
            pltpu.VMEM((GROUP, 2 * tokens, cols), F32),
            pltpu.VMEM((GROUP, 2 * tokens, cols), BF16),
            pltpu.VMEM((flows, rows, cols // LANE_PARTS), BF16),
            pltpu.VMEM((flows, rows, cols // LANE_PARTS), BF16),
            pltpu.VMEM((flows, ring - 1, size, cols // LANE_PARTS), BF16),
            pltpu.VMEM((flows, size, cols // LANE_PARTS), F32),
            pltpu.VMEM((bits + 1, GROUP, 8, 128), F32),
            pltpu.VMEM((STEPS * bits, GROUP, 8, 128), F32),
            pltpu.VMEM((CORES, GROUP, 8, 128), F32),
            pltpu.VMEM((2 * tokens, cols), BF16),
            pltpu.VMEM((tokens, cols), BF16),
            pltpu.VMEM((CORES, tokens, cols), BF16),
            pltpu.VMEM((LANE_PARTS, rows, cols // LANE_PARTS), BF16),
            pltpu.VMEM((CORES * LANE_PARTS, rows, cols // LANE_PARTS), BF16),
            pltpu.VMEM((8, 128), F32),
            pltpu.VMEM((8, 128), F32),
            pltpu.VMEM((rows, half), BF16),
            pltpu.VMEM((rows, half), BF16),
            pltpu.VMEM((tokens, rows), BF16),
            pltpu.VMEM((tokens, half), F32),
            pltpu.VMEM((tokens, half), BF16),
            dma((2,)),
            dma((flows, 2 * (ring - 1))),
            dma((6,)),
            dma((6,)),
            dma((bits,)),
            dma((STEPS * bits,)),
            dma((2,)),
            dma((2,)),
            dma,
            dma,
            dma,
            dma,
            dma,
            dma((2 * len(TILES) + 1,)),
            dma((7,)),
            dma,
        ],
        compiler_params=pltpu.CompilerParams(
            collective_id=0, has_side_effects=True, vmem_limit_bytes=60 << 20
        ),
    )(queries, keys, values, rates.T, w_up[0], w_gate[0], w_down[0], w_out)
    return pl.pallas_call(
        copy_kernel,
        out_shape=jax.ShapeDtypeStruct((tokens, half), BF16),
        in_specs=[anywhere],
        out_specs=anywhere,
        scratch_shapes=[pltpu.VMEM((tokens, half), BF16), dma((COPY_PIECES,)), dma],
    )(mixed)


def solution(mesh):
    def body(*args):
        return shards(mesh.shape["ctx"], *args)

    return jax.shard_map(
        body,
        mesh=mesh,
        in_specs=(
            P("ctx", "head"),
            P("ctx", "head"),
            P("ctx", "head"),
            P("ctx", "head"),
            P("head", None, None),
            P("head", None, None),
            P("head", None, None),
            P("head", None),
        ),
        out_specs=P("ctx", "head"),
        check_vma=False,
    )
```

```python
import functools

import jax
import jax.numpy as jnp
from jax import lax
from jax.experimental import pallas as pl
from jax.experimental.pallas import tpu as pltpu
from jax.sharding import PartitionSpec as P

STEPS = 2
F32 = jnp.float32
BF16 = jnp.bfloat16
MESH = pl.DeviceIdType.MESH
GROUP = 3
LANE_PARTS = 2
CORES = 2
RING_ROWS = 4
TILES = (4, 2, 2)
PIECES = 2
STRIPES = 5
COPY_PIECES = 8


def ring_place(chip, width):
    row, turn = chip // width, width - 1 - chip % width
    odd = turn % 2
    along = (1 - odd) * (row - 1) + odd * (RING_ROWS - 1 - row)
    return jnp.where(row == 0, chip, width + (RING_ROWS - 1) * turn + along)


def ring_chip(place, width):
    past = jnp.maximum(place - width, 0)
    turn, along = past // (RING_ROWS - 1), past % (RING_ROWS - 1)
    odd = turn % 2
    row = (1 - odd) * (1 + along) + odd * (RING_ROWS - 1 - along)
    return jnp.where(place < width, place, row * width + width - 1 - turn)


def dot(left, right, dims=((1,), (0,))):
    return lax.dot_general(left, right, (dims, ((), ())), preferred_element_type=F32)


def square_sum(block):
    return jnp.sum((block * block).reshape(-1, 8, block.shape[-1]), axis=0)


def lane_fold(block):
    return block[:, :128] + block[:, 128:]


def layer_kernel(n_ctx, q, k, v, r, w0, w1, w2, w_out, out, *scratch):
    (
        ks, us, qs, vin, kt, ut, first0, first1, in2, first2,
        acts, mid, grads, blocks, arrived, kept, tally, tally_in, norm_sums,
        hq, near_hid, far_hid, near_w2, far_w2, far_scale, scale_out,
        w_near, w_far, near, total_out, staged,
        ring_send, ring_recv, pair_send, pair_recv, tally_send, tally_recv,
        side_send, side_recv, w2_send, w2_recv, near_send, near_recv, hid_send, hid_recv, local_sem, out_sem,
    ) = scratch
    tokens, rows = k.shape
    cols = first0.shape[1]
    half = w_out.shape[1] // 2
    ring = n_ctx // CORES
    width = ring // RING_ROWS
    size = rows // ring
    bits = n_ctx.bit_length() - 1
    me = lax.axis_index("ctx")
    head = lax.axis_index("head")
    core = me % CORES
    chip = me // CORES
    place = ring_place(chip, width)
    right = {"ctx": ring_chip((place + 1) % ring, width) * CORES + core}
    left = {"ctx": ring_chip((place + ring - 1) % ring, width) * CORES + core}
    sibling = {"ctx": chip * CORES + 1 - core}
    across = {"head": 1 - head}
    diagonal = {"ctx": chip * CORES + 1 - core, "head": 1 - head}
    tally_partners = [
        {"ctx": me + (1 - 2 * ((me // (1 << bit)) % 2)) * (1 << bit)}
        for bit in range(bits)
    ]

    def remote(source, target, send_sem, recv_sem, device):
        return pltpu.make_async_remote_copy(
            src_ref=source,
            dst_ref=target,
            send_sem=send_sem,
            recv_sem=recv_sem,
            device_id=device,
            device_id_type=MESH,
        )

    def local(slot, source, target):
        return pltpu.make_async_copy(source, target, local_sem.at[slot])

    own_cols = pl.ds(pl.multiple_of(core * cols, 128), cols)
    own, other = slice(0, tokens), slice(tokens, 2 * tokens)
    loads = [
        local(0, k, ks.at[own, :]),
        local(1, v, vin),
        local(2, w0.at[:, own_cols], first0),
        local(3, w1.at[:, own_cols], first1),
        local(4, w2.at[pl.ds(pl.multiple_of(core * cols, 128), cols), :], in2),
        local(5, q, qs.at[own, :]),
    ]
    for load in loads[:5]:
        load.start()

    partners = [right, left, sibling, across, diagonal] + tally_partners
    barrier = pltpu.get_barrier_semaphore()
    for target in partners:
        pl.semaphore_signal(barrier, inc=1, device_id=target, device_id_type=MESH)
    pl.semaphore_wait(barrier, len(partners))

    def pair(slot, source, target):
        return remote(source, target, pair_send.at[slot], pair_recv.at[slot], sibling)

    k_pair = pair(0, k, ks.at[other, :])
    k_pair.start()
    loads[5].start()
    near_cols = pl.ds(pl.multiple_of(head * half, 128), half)
    far_cols = pl.ds(pl.multiple_of((1 - head) * half, 128), half)
    depth = rows // CORES
    own_rows = pl.ds(pl.multiple_of(core * depth, depth), depth)
    w_swap = remote(
        w_out.at[own_rows, far_cols], w_far.at[own_rows, :],
        side_send.at[0], side_recv.at[0], across,
    )
    w_swap.start()

    loads[1].wait()
    rate = jnp.broadcast_to(r[...], (128, tokens)).T
    for t in range(rows // 128):
        at = slice(t * 128, (t + 1) * 128)
        scaled = (rate * vin[:, at].astype(F32)).astype(BF16)
        us[own, at] = scaled
        ut[at, own] = scaled.T
    u_pair = pair(1, us.at[own, :], us.at[other, :])
    u_pair.start()

    def turned(source, target, side):
        for t in range(rows // 128):
            at = slice(t * 128, (t + 1) * 128)
            target[at, side] = source[side, at].T

    loads[0].wait()
    turned(ks, kt, own)
    q_pair = pair(2, q, qs.at[other, :])
    q_pair.start()
    w_copy = local(6, w_out.at[:, near_cols], w_near)
    w_copy.start()
    for load in loads[2:5]:
        load.wait()
    for t in range(rows // 128):
        at = slice(t * 128, (t + 1) * 128)
        first2[at, :] = in2[:, at].T

    firsts = (first0, first1, first2)
    scales = [None] * GROUP

    def weight(step, w):
        if step == 0:
            return firsts[w][...]
        return jnp.concatenate([blocks[2 * w], blocks[2 * w + 1]], axis=1)

    def act_dot(step, w, source, at):
        product = dot(source[at, :], weight(step, w))
        acts[w, at, :] = product

    for w, source in enumerate((ks, ks, us)):
        act_dot(0, w, source, own)

    half_pieces = tokens // 128
    whole = (0, 2 * half_pieces)

    def hid_gates(by, span):
        def one(piece, carry):
            at = pl.ds(pl.multiple_of(piece * 128, 128), 128)
            act, lin = acts[0, at, :], acts[1, at, :]
            if by[0] is not None:
                act, lin = act * by[0], lin * by[1]
            mid[2, at, :] = (act * jax.nn.sigmoid(act) * lin).astype(BF16)
            return carry

        lax.fori_loop(*span, one, 0)

    def err_gates(by, span):
        def one(piece, carry):
            at = pl.ds(pl.multiple_of(piece * 128, 128), 128)
            act, lin, err = acts[0, at, :], acts[1, at, :], acts[2, at, :]
            if by[0] is not None:
                act, lin, err = act * by[0], lin * by[1], err * by[2]
            sig = jax.nn.sigmoid(act)
            mid[0, at, :] = (err * lin * sig * (1.0 + act * (1.0 - sig))).astype(BF16)
            mid[1, at, :] = (err * (act * sig)).astype(BF16)
            return carry

        lax.fori_loop(*span, one, 0)

    hid_gates(scales, (0, half_pieces))
    err_gates(scales, (0, half_pieces))
    k_pair.wait_recv()
    act_dot(0, 0, ks, other)
    act_dot(0, 1, ks, other)
    hid_gates(scales, (half_pieces, 2 * half_pieces))

    flows = [(w, h) for w in range(GROUP) for h in range(LANE_PARTS)]

    def reach(h):
        longer = ring // 2
        return (longer, ring - 1 - longer) if h == 0 else (ring - 1 - longer, longer)

    def chunk(number):
        return pl.ds(pl.multiple_of((number % ring) * size, size), size)

    copies = {}

    def ring_sent(phase):
        all_sent = grads.at[:, : (ring - 1) * size, :]
        remote(all_sent, all_sent, ring_send.at[phase], ring_recv.at[0, 0], right).wait_send()

    for step in range(STEPS):

        def send(flow, slot, source, target, device):
            phase = ring_send.at[0 if slot < ring - 1 else 1]
            copy = remote(source, target, phase, ring_recv.at[flow, slot], device)
            copy.start()
            copies[flow, slot] = copy

        def send_sum(flow, to_right, s):
            far, back = reach(flow % LANE_PARTS)
            at = chunk(place + far - s) if to_right else chunk(place + ring - back + s)
            slot = s if to_right else far + s
            device = right if to_right else left
            send(flow, slot, grads.at[flow, at, :], arrived.at[flow, slot], device)

        def send_block(flow, to_right, t):
            far, back = reach(flow % LANE_PARTS)
            at = chunk(place + ring - t) if to_right else chunk(place + t)
            slot = ring - 1 + (t if to_right else far + t)
            device = right if to_right else left
            here = blocks.at[flow, at, :]
            send(flow, slot, here, here, device)

        def pass_sum(flow, to_right, s):
            far, back = reach(flow % LANE_PARTS)
            slot = s if to_right else far + s
            at = chunk(place + far - 1 - s) if to_right else chunk(place + ring + 1 - back + s)
            copies[flow, slot].wait_recv()
            total = grads[flow, at, :].astype(F32) + arrived[flow, slot].astype(F32)
            grads[flow, at, :] = total.astype(BF16)
            send_sum(flow, to_right, s + 1)

        def send_w2(flow, number):
            here = chunk(number)
            target = far_w2.at[flow % LANE_PARTS, here, :]
            remote(blocks.at[flow, here, :], target, w2_send, w2_recv, across).start()
            target = near_w2.at[flow % LANE_PARTS, here, :]
            remote(
                blocks.at[flow, here, :], target, near_send, near_recv, sibling
            ).start()

        def grad(w):
            source = ut if w == 2 else kt

            for piece in range(PIECES):
                at = slice(piece * (rows // PIECES), (piece + 1) * (rows // PIECES))
                product = dot(source[at, :], mid[w]).astype(BF16)
                grads[2 * w, at, :] = product[:, :128]
                grads[2 * w + 1, at, :] = product[:, 128:]
            for h in range(LANE_PARTS):
                send_sum(2 * w + h, True, 0)
                send_sum(2 * w + h, False, 0)

        if step == 0:
            turned(ks, kt, other)
            u_pair.wait_recv()
            turned(us, ut, other)
            grad(2)
            act_dot(0, 2, us, other)
            err_gates(scales, (half_pieces, 2 * half_pieces))
        else:
            err_gates(scales, whole)
        grad(0)
        grad(1)
        if step == 0:
            for w in range(GROUP):
                norm_sums[0, w] = lane_fold(square_sum(firsts[w][...].astype(F32)))
            norm_pair = pair(3, norm_sums.at[0], norm_sums.at[1])
            norm_pair.start()
        turn = ring // 2 - 1
        ordered = [2 * w + h for w in range(GROUP) for h in range(LANE_PARTS)]
        for s in range(turn):
            for flow in ordered:
                far, back = reach(flow % LANE_PARTS)
                if s < far - 1:
                    pass_sum(flow, True, s)
                if s < back - 1:
                    pass_sum(flow, False, s)
        for flow in ordered:
            far, back = reach(flow % LANE_PARTS)
            w, h = flows[flow]
            at = chunk(place)
            copies[flow, far - 1].wait_recv()
            copies[flow, ring - 2].wait_recv()
            total = grads[flow, at, :].astype(F32) + arrived[flow, far - 1].astype(F32)
            total = total + arrived[flow, ring - 2].astype(F32)
            if step == 0:
                lanes = slice(h * 128, (h + 1) * 128)
                moved = firsts[w][at, lanes].astype(F32) + total
            else:
                moved = kept[flow] * scales[w] + total
            kept[flow] = moved
            rounded = moved.astype(BF16)
            blocks[flow, at, :] = rounded
            send_block(flow, True, 0)
            send_block(flow, False, 0)
            if step == STEPS - 1 and w == 2:
                send_w2(flow, place)
            part = square_sum(rounded.astype(F32))
            tally[0, w] = part if h == 0 else tally[0, w] + part
        tallies = []

        def start_tally(stage):
            copy = remote(
                tally.at[stage], tally_in.at[step * bits + stage],
                tally_send.at[stage], tally_recv.at[step * bits + stage],
                tally_partners[stage],
            )
            copy.start()
            tallies.append(copy)

        def end_tally(stage):
            tallies[stage].wait_recv()
            tally[stage + 1] = tally[stage] + tally_in[step * bits + stage]
            if stage + 1 < bits:
                start_tally(stage + 1)

        def take_block(flow, t):
            far, back = reach(flow % LANE_PARTS)
            for to_right, count in ((True, far), (False, back)):
                if t >= count:
                    continue
                copies[flow, ring - 1 + (t if to_right else far + t)].wait_recv()
                if t < count - 1:
                    send_block(flow, to_right, t + 1)
                if step == STEPS - 1 and flow // LANE_PARTS == 2:
                    send_w2(flow, place + (ring - 1 - t if to_right else 1 + t))

        if step > 0:
            q_pair.wait_recv()
            loads[5].wait()
        wanted = (ks, ks, us) if step == 0 else (qs, qs)

        def pair_dot(w, one, two, fresh):
            pair_at = (chunk(one), chunk(two))
            right_side = jnp.concatenate(
                [
                    jnp.concatenate([blocks[2 * w, at, :], blocks[2 * w + 1, at, :]], axis=1)
                    for at in pair_at
                ],
                axis=0,
            )
            for side in (own, other):
                left_side = jnp.concatenate([wanted[w][side, at] for at in pair_at], axis=1)
                product = dot(left_side, right_side)
                acts[w, side, :] = product if fresh else acts[w, side, :] + product

        in_pairs = size % 128 == 0
        start_tally(0)
        ended = 0
        for t in range(turn):
            for flow in ordered:
                take_block(flow, t)
                w, h = flows[flow]
                if in_pairs and h == LANE_PARTS - 1 and w < len(wanted):
                    pair_dot(w, place + ring - 1 - t, place + 1 + t, t == 0)
                if flow == ordered[3] and ended < bits - 1:
                    end_tally(ended)
                    ended += 1
            if step == STEPS - 1 and t == turn // 2:
                w_swap.wait()
                w_share = pair(4, w_far.at[own_rows, :], w_far.at[own_rows, :])
                w_share.start()
        if step == 0:
            norm_pair.wait()
            norms = [
                jnp.sqrt(jnp.sum(norm_sums[0, w] + norm_sums[1, w], keepdims=True))
                for w in range(GROUP)
            ]

        def last_dot(w):
            for h in range(LANE_PARTS):
                take_block(2 * w + h, turn)
            if w >= len(wanted):
                return
            if in_pairs:
                pair_dot(w, place, place + ring // 2, False)
            else:
                act_dot(1, w, wanted[w], own)
                act_dot(1, w, wanted[w], other)

        last_dot(0)
        last_dot(1)
        while ended < bits:
            end_tally(ended)
            ended += 1
        scales = [
            norms[w] / jnp.sqrt(jnp.sum(tally[bits, w], keepdims=True) + 1e-06)
            for w in range(GROUP)
        ]
        ring_sent(0)
        if step == 0:
            hid_gates(scales, whole)
            grad(2)
            last_dot(2)
        ring_sent(1)
        for copy in tallies:
            copy.wait_send()

    ends = [tokens * sum(TILES[: t + 1]) // sum(TILES) for t in range(len(TILES))]
    tiles = [(end - tokens * part // sum(TILES), end) for end, part in zip(ends, TILES)]
    scale_out[...] = jnp.broadcast_to(scales[2], scale_out.shape)
    scale_swap = remote(
        scale_out, far_scale, side_send.at[1], side_recv.at[1], across
    )
    scale_swap.start()
    hid_copies = []

    def send_hid(slot, source, target, device):
        copy = remote(source, target, hid_send.at[slot // 2], hid_recv.at[slot], device)
        copy.start()
        return copy

    def hidden_of(side, first, last):
        at = slice(side * tokens + first, side * tokens + last)
        act = acts[0, at, :] * scales[0]
        lin = acts[1, at, :] * scales[1]
        hq[at, :] = (act * jax.nn.sigmoid(act) * lin).astype(BF16)

    def send_tile(t):
        first, last = tiles[t]
        to, at = slice(first, last), slice(tokens + first, tokens + last)
        hid_copies.append((
            send_hid(2 * t, hq.at[to, :], far_hid.at[0, to, :], across),
            send_hid(2 * t + 1, hq.at[at, :], far_hid.at[1, to, :], diagonal),
        ))

    for side in range(CORES):
        hidden_of(side, 0, tokens)
    last_dot(2)
    near_copy = send_hid(2 * len(TILES), hq.at[other, :], near_hid, sibling)
    send_tile(0)
    wide = ((1,), (1,))
    stripe = half // STRIPES

    def tile_sent(t):
        first, last = tiles[t]
        both = far_hid.at[:, first:last, :]
        remote(both, both, hid_send.at[t], hid_recv.at[2 * t], across).wait_send()

    def near_stripes(first, last):
        def one(c, carry):
            lanes = pl.ds(pl.multiple_of(c * stripe, 128), stripe)
            total_out[:, lanes] = dot(near[...], w_near[:, lanes])
            return carry

        lax.fori_loop(first, last, one, 0)

    near_w2_copy = remote(near_w2, near_w2, near_send, near_recv, sibling)
    near_w2_copy.wait_recv()
    near_copy.wait_recv()
    mine = dot(hq[own, :], jnp.concatenate([blocks[4], blocks[5]], axis=1), wide)
    theirs = dot(near_hid[...], jnp.concatenate([near_w2[0], near_w2[1]], axis=1), wide)
    near[...] = ((mine + theirs) * scales[2]).astype(BF16)
    w_copy.wait()
    near_stripes(0, 2)
    send_tile(1)
    send_tile(2)
    far_w2_copy = remote(far_w2.at[0:2], far_w2.at[0:2], w2_send, w2_recv, across)
    far_w2_copy.wait_recv()
    far_pair = pair(5, far_w2.at[0:2], far_w2.at[2:4])
    far_pair.start()
    near_stripes(2, STRIPES)
    scale_swap.wait()
    w_share.wait_recv()
    far_pair.wait_recv()
    scale = jnp.max(far_scale[...], keepdims=True)
    for t, (first, last) in enumerate(tiles):
        at = slice(first, last)
        hid_copies[t][0].wait_recv()
        hid_copies[t][1].wait_recv()
        mine = dot(
            far_hid[0, at, :], jnp.concatenate([far_w2[0], far_w2[1]], axis=1), wide
        )
        theirs = dot(
            far_hid[1, at, :], jnp.concatenate([far_w2[2], far_w2[3]], axis=1), wide
        )
        near[at, :] = ((mine + theirs) * scale).astype(BF16)

        def far_cols_of(c, carry):
            lanes = pl.ds(pl.multiple_of(c * stripe, 128), stripe)
            added = total_out[at, lanes] + dot(near[at, :], w_far[:, lanes])
            staged[at, lanes] = added.astype(BF16)
            pltpu.make_async_copy(staged.at[at, lanes], out.at[at, lanes], out_sem).start()
            return carry

        lax.fori_loop(0, STRIPES, far_cols_of, 0)
    pltpu.make_async_copy(staged, out, out_sem).wait()
    for t in range(len(TILES)):
        tile_sent(t)
    near_copy.wait_send()
    near_w2_copy.wait_send()
    far_w2_copy.wait_send()
    far_pair.wait_send()
    w_share.wait_send()
    for copy in (k_pair, u_pair, q_pair):
        copy.wait_send()


def copy_kernel(source, target, held, in_sem, out_sem):
    rows = held.shape[0] // COPY_PIECES
    pieces = [pl.ds(piece * rows, rows) for piece in range(COPY_PIECES)]
    reads = [
        pltpu.make_async_copy(source.at[at, :], held.at[at, :], in_sem.at[piece])
        for piece, at in enumerate(pieces)
    ]
    for read in reads:
        read.start()
    for read, at in zip(reads, pieces):
        read.wait()
        pltpu.make_async_copy(held.at[at, :], target.at[at, :], out_sem).start()
    pltpu.make_async_copy(held, target, out_sem).wait()


def shards(n_ctx, queries, keys, values, rates, w_up, w_gate, w_down, w_out):
    tokens, rows = keys.shape
    cols = w_up.shape[2] // CORES
    half = w_out.shape[1] // 2
    ring = n_ctx // CORES
    size = rows // ring
    bits = n_ctx.bit_length() - 1
    flows = GROUP * LANE_PARTS
    vmem = pl.BlockSpec(memory_space=pltpu.VMEM)
    anywhere = pl.BlockSpec(memory_space=pl.ANY)
    dma = pltpu.SemaphoreType.DMA
    mixed = pl.pallas_call(
        functools.partial(layer_kernel, n_ctx),
        out_shape=jax.ShapeDtypeStruct((tokens, half), BF16),
        in_specs=[anywhere] * 3 + [vmem] + [anywhere] * 4,
        out_specs=anywhere,
        scratch_shapes=[
            pltpu.VMEM((2 * tokens, rows), BF16),
            pltpu.VMEM((2 * tokens, rows), BF16),
            pltpu.VMEM((2 * tokens, rows), BF16),
            pltpu.VMEM((tokens, rows), BF16),
            pltpu.VMEM((rows, 2 * tokens), BF16),
            pltpu.VMEM((rows, 2 * tokens), BF16),
            pltpu.VMEM((rows, cols), BF16),
            pltpu.VMEM((rows, cols), BF16),
            pltpu.VMEM((cols, rows), BF16),
            pltpu.VMEM((rows, cols), BF16),
            pltpu.VMEM((GROUP, 2 * tokens, cols), F32),
            pltpu.VMEM((GROUP, 2 * tokens, cols), BF16),
            pltpu.VMEM((flows, rows, cols // LANE_PARTS), BF16),
            pltpu.VMEM((flows, rows, cols // LANE_PARTS), BF16),
            pltpu.VMEM((flows, ring - 1, size, cols // LANE_PARTS), BF16),
            pltpu.VMEM((flows, size, cols // LANE_PARTS), F32),
            pltpu.VMEM((bits + 1, GROUP, 8, 128), F32),
            pltpu.VMEM((STEPS * bits, GROUP, 8, 128), F32),
            pltpu.VMEM((CORES, GROUP, 8, 128), F32),
            pltpu.VMEM((2 * tokens, cols), BF16),
            pltpu.VMEM((tokens, cols), BF16),
            pltpu.VMEM((CORES, tokens, cols), BF16),
            pltpu.VMEM((LANE_PARTS, rows, cols // LANE_PARTS), BF16),
            pltpu.VMEM((CORES * LANE_PARTS, rows, cols // LANE_PARTS), BF16),
            pltpu.VMEM((8, 128), F32),
            pltpu.VMEM((8, 128), F32),
            pltpu.VMEM((rows, half), BF16),
            pltpu.VMEM((rows, half), BF16),
            pltpu.VMEM((tokens, rows), BF16),
            pltpu.VMEM((tokens, half), F32),
            pltpu.VMEM((tokens, half), BF16),
            dma((2,)),
            dma((flows, 2 * (ring - 1))),
            dma((6,)),
            dma((6,)),
            dma((bits,)),
            dma((STEPS * bits,)),
            dma((2,)),
            dma((2,)),
            dma,
            dma,
            dma,
            dma,
            dma((len(TILES) + 1,)),
            dma((2 * len(TILES) + 1,)),
            dma((7,)),
            dma,
        ],
        compiler_params=pltpu.CompilerParams(
            collective_id=0, has_side_effects=True, vmem_limit_bytes=60 << 20
        ),
    )(queries, keys, values, rates.T, w_up[0], w_gate[0], w_down[0], w_out)
    return pl.pallas_call(
        copy_kernel,
        out_shape=jax.ShapeDtypeStruct((tokens, half), BF16),
        in_specs=[anywhere],
        out_specs=anywhere,
        scratch_shapes=[pltpu.VMEM((tokens, half), BF16), dma((COPY_PIECES,)), dma],
    )(mixed)


def solution(mesh):
    def body(*args):
        return shards(mesh.shape["ctx"], *args)

    return jax.shard_map(
        body,
        mesh=mesh,
        in_specs=(
            P("ctx", "head"),
            P("ctx", "head"),
            P("ctx", "head"),
            P("ctx", "head"),
            P("head", None, None),
            P("head", None, None),
            P("head", None, None),
            P("head", None),
        ),
        out_specs=P("ctx", "head"),
        check_vma=False,
    )
```

```python
import functools

import jax
import jax.numpy as jnp
from jax import lax
from jax.experimental import pallas as pl
from jax.experimental.pallas import tpu as pltpu
from jax.sharding import PartitionSpec as P

STEPS = 2
F32 = jnp.float32
BF16 = jnp.bfloat16
MESH = pl.DeviceIdType.MESH
GROUP = 3
LANE_PARTS = 2
CORES = 2
RING_ROWS = 4
TILES = (1, 1)
PIECES = 2
STRIPES = 5
COPY_PIECES = 8


def ring_place(chip, width):
    row, turn = chip // width, width - 1 - chip % width
    odd = turn % 2
    along = (1 - odd) * (row - 1) + odd * (RING_ROWS - 1 - row)
    return jnp.where(row == 0, chip, width + (RING_ROWS - 1) * turn + along)


def ring_chip(place, width):
    past = jnp.maximum(place - width, 0)
    turn, along = past // (RING_ROWS - 1), past % (RING_ROWS - 1)
    odd = turn % 2
    row = (1 - odd) * (1 + along) + odd * (RING_ROWS - 1 - along)
    return jnp.where(place < width, place, row * width + width - 1 - turn)


def dot(left, right, dims=((1,), (0,))):
    return lax.dot_general(left, right, (dims, ((), ())), preferred_element_type=F32)


def square_sum(block):
    return jnp.sum((block * block).reshape(-1, 8, block.shape[-1]), axis=0)


def lane_fold(block):
    return block[:, :128] + block[:, 128:]


def layer_kernel(n_ctx, q, k, v, r, w0, w1, w2, w_out, out, *scratch):
    (
        ks, us, qs, vin, kt, ut, first0, first1, in2, first2,
        acts, mid, grads, blocks, arrived, kept, tally, tally_in, norm_sums,
        hq, near_hid, far_hid, near_w2, far_w2, far_scale, scale_out,
        w_near, w_far, near, total_out, staged,
        ring_send, ring_recv, pair_send, pair_recv, tally_send, tally_recv,
        side_send, side_recv, w2_send, w2_recv, relay_sem, near_send, near_recv, hid_send, hid_recv, local_sem, out_sem,
    ) = scratch
    tokens, rows = k.shape
    cols = first0.shape[1]
    half = w_out.shape[1] // 2
    ring = n_ctx // CORES
    width = ring // RING_ROWS
    size = rows // ring
    bits = n_ctx.bit_length() - 1
    me = lax.axis_index("ctx")
    head = lax.axis_index("head")
    core = me % CORES
    chip = me // CORES
    place = ring_place(chip, width)
    right = {"ctx": ring_chip((place + 1) % ring, width) * CORES + core}
    left = {"ctx": ring_chip((place + ring - 1) % ring, width) * CORES + core}
    sibling = {"ctx": chip * CORES + 1 - core}
    across = {"head": 1 - head}
    diagonal = {"ctx": chip * CORES + 1 - core, "head": 1 - head}
    tally_partners = [
        {"ctx": me + (1 - 2 * ((me // (1 << bit)) % 2)) * (1 << bit)}
        for bit in range(bits)
    ]

    def remote(source, target, send_sem, recv_sem, device):
        return pltpu.make_async_remote_copy(
            src_ref=source,
            dst_ref=target,
            send_sem=send_sem,
            recv_sem=recv_sem,
            device_id=device,
            device_id_type=MESH,
        )

    def local(slot, source, target):
        return pltpu.make_async_copy(source, target, local_sem.at[slot])

    own_cols = pl.ds(pl.multiple_of(core * cols, 128), cols)
    own, other = slice(0, tokens), slice(tokens, 2 * tokens)
    loads = [
        local(0, k, ks.at[own, :]),
        local(1, v, vin),
        local(2, w0.at[:, own_cols], first0),
        local(3, w1.at[:, own_cols], first1),
        local(4, w2.at[pl.ds(pl.multiple_of(core * cols, 128), cols), :], in2),
        local(5, q, qs.at[own, :]),
    ]
    for load in loads[:5]:
        load.start()

    partners = [right, left, sibling, across, diagonal] + tally_partners
    barrier = pltpu.get_barrier_semaphore()
    for target in partners:
        pl.semaphore_signal(barrier, inc=1, device_id=target, device_id_type=MESH)
    pl.semaphore_wait(barrier, len(partners))

    def pair(slot, source, target):
        return remote(source, target, pair_send.at[slot], pair_recv.at[slot], sibling)

    k_pair = pair(0, k, ks.at[other, :])
    k_pair.start()
    loads[5].start()
    near_cols = pl.ds(pl.multiple_of(head * half, 128), half)
    far_cols = pl.ds(pl.multiple_of((1 - head) * half, 128), half)
    depth = rows // CORES
    own_rows = pl.ds(pl.multiple_of(core * depth, depth), depth)
    w_swap = remote(
        w_out.at[own_rows, far_cols], w_far.at[own_rows, :],
        side_send.at[0], side_recv.at[0], across,
    )
    w_swap.start()

    loads[1].wait()
    rate = jnp.broadcast_to(r[...], (128, tokens)).T
    for t in range(rows // 128):
        at = slice(t * 128, (t + 1) * 128)
        scaled = (rate * vin[:, at].astype(F32)).astype(BF16)
        us[own, at] = scaled
        ut[at, own] = scaled.T
    u_pair = pair(1, us.at[own, :], us.at[other, :])
    u_pair.start()

    def turned(source, target, side):
        for t in range(rows // 128):
            at = slice(t * 128, (t + 1) * 128)
            target[at, side] = source[side, at].T

    loads[0].wait()
    turned(ks, kt, own)
    q_pair = pair(2, q, qs.at[other, :])
    q_pair.start()
    w_copy = local(6, w_out.at[:, near_cols], w_near)
    w_copy.start()
    for load in loads[2:5]:
        load.wait()
    for t in range(rows // 128):
        at = slice(t * 128, (t + 1) * 128)
        first2[at, :] = in2[:, at].T

    firsts = (first0, first1, first2)
    scales = [None] * GROUP

    def weight(step, w):
        if step == 0:
            return firsts[w][...]
        return jnp.concatenate([blocks[2 * w], blocks[2 * w + 1]], axis=1)

    def act_dot(step, w, source, at):
        product = dot(source[at, :], weight(step, w))
        acts[w, at, :] = product

    for w, source in enumerate((ks, ks, us)):
        act_dot(0, w, source, own)

    half_pieces = tokens // 128
    whole = (0, 2 * half_pieces)

    def hid_gates(by, span):
        def one(piece, carry):
            at = pl.ds(pl.multiple_of(piece * 128, 128), 128)
            act, lin = acts[0, at, :], acts[1, at, :]
            if by[0] is not None:
                act, lin = act * by[0], lin * by[1]
            mid[2, at, :] = (act * jax.nn.sigmoid(act) * lin).astype(BF16)
            return carry

        lax.fori_loop(*span, one, 0)

    def err_gates(by, span):
        def one(piece, carry):
            at = pl.ds(pl.multiple_of(piece * 128, 128), 128)
            act, lin, err = acts[0, at, :], acts[1, at, :], acts[2, at, :]
            if by[0] is not None:
                act, lin, err = act * by[0], lin * by[1], err * by[2]
            sig = jax.nn.sigmoid(act)
            mid[0, at, :] = (err * lin * sig * (1.0 + act * (1.0 - sig))).astype(BF16)
            mid[1, at, :] = (err * (act * sig)).astype(BF16)
            return carry

        lax.fori_loop(*span, one, 0)

    hid_gates(scales, (0, half_pieces))
    err_gates(scales, (0, half_pieces))
    k_pair.wait_recv()
    act_dot(0, 0, ks, other)
    act_dot(0, 1, ks, other)
    hid_gates(scales, (half_pieces, 2 * half_pieces))

    flows = [(w, h) for w in range(GROUP) for h in range(LANE_PARTS)]

    def reach(h):
        longer = ring // 2
        return (longer, ring - 1 - longer) if h == 0 else (ring - 1 - longer, longer)

    def chunk(number):
        return pl.ds(pl.multiple_of((number % ring) * size, size), size)

    copies = {}

    def ring_sent(phase):
        all_sent = grads.at[:, : (ring - 1) * size, :]
        remote(all_sent, all_sent, ring_send.at[phase], ring_recv.at[0, 0], right).wait_send()

    for step in range(STEPS):

        def send(flow, slot, source, target, device):
            phase = ring_send.at[0 if slot < ring - 1 else 1]
            copy = remote(source, target, phase, ring_recv.at[flow, slot], device)
            copy.start()
            copies[flow, slot] = copy

        def send_sum(flow, to_right, s):
            far, back = reach(flow % LANE_PARTS)
            at = chunk(place + far - s) if to_right else chunk(place + ring - back + s)
            slot = s if to_right else far + s
            device = right if to_right else left
            send(flow, slot, grads.at[flow, at, :], arrived.at[flow, slot], device)

        def send_block(flow, to_right, t):
            far, back = reach(flow % LANE_PARTS)
            at = chunk(place + ring - t) if to_right else chunk(place + t)
            slot = ring - 1 + (t if to_right else far + t)
            device = right if to_right else left
            here = blocks.at[flow, at, :]
            send(flow, slot, here, here, device)

        def pass_sum(flow, to_right, s):
            far, back = reach(flow % LANE_PARTS)
            slot = s if to_right else far + s
            at = chunk(place + far - 1 - s) if to_right else chunk(place + ring + 1 - back + s)
            copies[flow, slot].wait_recv()
            total = grads[flow, at, :].astype(F32) + arrived[flow, slot].astype(F32)
            grads[flow, at, :] = total.astype(BF16)
            send_sum(flow, to_right, s + 1)

        def send_w2(flow, offset):
            here = chunk(place + ring + offset)
            if abs(offset) < ring // 2:
                slot = 1 if offset == ring // 2 - 1 else 0
                target = far_w2.at[flow % LANE_PARTS, here, :]
                remote(
                    blocks.at[flow, here, :], target, w2_send, w2_recv.at[slot], across
                ).start()
            target = near_w2.at[flow % LANE_PARTS, here, :]
            remote(
                blocks.at[flow, here, :], target, near_send, near_recv, sibling
            ).start()

        def grad(w):
            source = ut if w == 2 else kt

            for piece in range(PIECES):
                at = slice(piece * (rows // PIECES), (piece + 1) * (rows // PIECES))
                product = dot(source[at, :], mid[w]).astype(BF16)
                grads[2 * w, at, :] = product[:, :128]
                grads[2 * w + 1, at, :] = product[:, 128:]
            for h in range(LANE_PARTS):
                send_sum(2 * w + h, True, 0)
                send_sum(2 * w + h, False, 0)

        if step == 0:
            turned(ks, kt, other)
            u_pair.wait_recv()
            turned(us, ut, other)
            grad(2)
            act_dot(0, 2, us, other)
            err_gates(scales, (half_pieces, 2 * half_pieces))
        else:
            err_gates(scales, whole)
        grad(0)
        grad(1)
        if step == 0:
            for w in range(GROUP):
                norm_sums[0, w] = lane_fold(square_sum(firsts[w][...].astype(F32)))
            norm_pair = pair(3, norm_sums.at[0], norm_sums.at[1])
            norm_pair.start()
        turn = ring // 2 - 1
        ordered = [2 * w + h for w in range(GROUP) for h in range(LANE_PARTS)]
        for s in range(turn):
            for flow in ordered:
                far, back = reach(flow % LANE_PARTS)
                if s < far - 1:
                    pass_sum(flow, True, s)
                if s < back - 1:
                    pass_sum(flow, False, s)
        for flow in ordered:
            far, back = reach(flow % LANE_PARTS)
            w, h = flows[flow]
            at = chunk(place)
            copies[flow, far - 1].wait_recv()
            copies[flow, ring - 2].wait_recv()
            total = grads[flow, at, :].astype(F32) + arrived[flow, far - 1].astype(F32)
            total = total + arrived[flow, ring - 2].astype(F32)
            if step == 0:
                lanes = slice(h * 128, (h + 1) * 128)
                moved = firsts[w][at, lanes].astype(F32) + total
            else:
                moved = kept[flow] * scales[w] + total
            kept[flow] = moved
            rounded = moved.astype(BF16)
            blocks[flow, at, :] = rounded
            send_block(flow, True, 0)
            send_block(flow, False, 0)
            if step == STEPS - 1 and w == 2:
                send_w2(flow, 0)
            part = square_sum(rounded.astype(F32))
            tally[0, w] = part if h == 0 else tally[0, w] + part
        tallies = []

        def start_tally(stage):
            copy = remote(
                tally.at[stage], tally_in.at[step * bits + stage],
                tally_send.at[stage], tally_recv.at[step * bits + stage],
                tally_partners[stage],
            )
            copy.start()
            tallies.append(copy)

        def end_tally(stage):
            tallies[stage].wait_recv()
            tally[stage + 1] = tally[stage] + tally_in[step * bits + stage]
            if stage + 1 < bits:
                start_tally(stage + 1)

        def take_block(flow, t):
            far, back = reach(flow % LANE_PARTS)
            for to_right, count in ((True, far), (False, back)):
                if t >= count:
                    continue
                copies[flow, ring - 1 + (t if to_right else far + t)].wait_recv()
                if t < count - 1:
                    send_block(flow, to_right, t + 1)
                if step == STEPS - 1 and flow // LANE_PARTS == 2:
                    send_w2(flow, -1 - t if to_right else 1 + t)

        if step > 0:
            q_pair.wait_recv()
            loads[5].wait()
        wanted = (ks, ks, us) if step == 0 else (qs, qs)

        def pair_dot(w, one, two, fresh):
            pair_at = (chunk(one), chunk(two))
            right_side = jnp.concatenate(
                [
                    jnp.concatenate([blocks[2 * w, at, :], blocks[2 * w + 1, at, :]], axis=1)
                    for at in pair_at
                ],
                axis=0,
            )
            for side in (own, other):
                left_side = jnp.concatenate([wanted[w][side, at] for at in pair_at], axis=1)
                product = dot(left_side, right_side)
                acts[w, side, :] = product if fresh else acts[w, side, :] + product

        in_pairs = size % 128 == 0
        start_tally(0)
        ended = 0
        for t in range(turn):
            for flow in ordered:
                take_block(flow, t)
                w, h = flows[flow]
                if in_pairs and h == LANE_PARTS - 1 and w < len(wanted):
                    pair_dot(w, place + ring - 1 - t, place + 1 + t, t == 0)
                if flow == ordered[3] and ended < bits - 1:
                    end_tally(ended)
                    ended += 1
            if step == STEPS - 1 and t == turn // 2:
                w_swap.wait()
                w_share = pair(4, w_far.at[own_rows, :], w_far.at[own_rows, :])
                w_share.start()
        if step == 0:
            norm_pair.wait()
            norms = [
                jnp.sqrt(jnp.sum(norm_sums[0, w] + norm_sums[1, w], keepdims=True))
                for w in range(GROUP)
            ]

        def last_dot(w):
            for h in range(LANE_PARTS):
                take_block(2 * w + h, turn)
            if w >= len(wanted):
                return
            if in_pairs:
                pair_dot(w, place, place + ring // 2, False)
            else:
                act_dot(1, w, wanted[w], own)
                act_dot(1, w, wanted[w], other)

        last_dot(0)
        last_dot(1)
        while ended < bits:
            end_tally(ended)
            ended += 1
        scales = [
            norms[w] / jnp.sqrt(jnp.sum(tally[bits, w], keepdims=True) + 1e-06)
            for w in range(GROUP)
        ]
        ring_sent(0)
        if step == 0:
            hid_gates(scales, whole)
            grad(2)
            last_dot(2)
        ring_sent(1)
        for copy in tallies:
            copy.wait_send()

    ends = [tokens * sum(TILES[: t + 1]) // sum(TILES) for t in range(len(TILES))]
    tiles = [(end - tokens * part // sum(TILES), end) for end, part in zip(ends, TILES)]
    scale_out[...] = jnp.broadcast_to(scales[2], scale_out.shape)
    scale_swap = remote(
        scale_out, far_scale, side_send.at[1], side_recv.at[1], across
    )
    scale_swap.start()
    hid_copies = []

    def send_hid(slot, source, target, device):
        copy = remote(source, target, hid_send.at[slot // 2], hid_recv.at[slot], device)
        copy.start()
        return copy

    def hidden_of(side, first, last):
        at = slice(side * tokens + first, side * tokens + last)
        act = acts[0, at, :] * scales[0]
        lin = acts[1, at, :] * scales[1]
        hq[at, :] = (act * jax.nn.sigmoid(act) * lin).astype(BF16)

    def send_tile(t):
        first, last = tiles[t]
        to, at = slice(first, last), slice(tokens + first, tokens + last)
        hid_copies.append((
            send_hid(2 * t, hq.at[to, :], far_hid.at[0, to, :], across),
            send_hid(2 * t + 1, hq.at[at, :], far_hid.at[1, to, :], diagonal),
        ))

    for side in range(CORES):
        hidden_of(side, 0, tokens)
    last_dot(2)
    near_copy = send_hid(2 * len(TILES), hq.at[other, :], near_hid, sibling)
    send_tile(0)
    wide = ((1,), (1,))
    stripe = half // STRIPES

    def tile_sent(t):
        first, last = tiles[t]
        both = far_hid.at[:, first:last, :]
        remote(both, both, hid_send.at[t], hid_recv.at[2 * t], across).wait_send()

    def near_stripes(first, last):
        def one(c, carry):
            lanes = pl.ds(pl.multiple_of(c * stripe, 128), stripe)
            total_out[:, lanes] = dot(near[...], w_near[:, lanes])
            return carry

        lax.fori_loop(first, last, one, 0)

    near_w2_copy = remote(near_w2, near_w2, near_send, near_recv, sibling)
    near_w2_copy.wait_recv()
    near_copy.wait_recv()
    mine = dot(hq[own, :], jnp.concatenate([blocks[4], blocks[5]], axis=1), wide)
    theirs = dot(near_hid[...], jnp.concatenate([near_w2[0], near_w2[1]], axis=1), wide)
    near[...] = ((mine + theirs) * scales[2]).astype(BF16)
    for t in range(1, len(TILES)):
        send_tile(t)
    w_copy.wait()
    near_stripes(0, 2)
    next_w2 = far_w2.at[0:2, chunk(place + ring // 2 - 1), :]
    remote(next_w2, next_w2, w2_send, w2_recv.at[1], across).wait_recv()
    relay = remote(next_w2, next_w2, relay_sem.at[0], relay_sem.at[1], left)
    relay.start()
    near_stripes(2, STRIPES)
    most_w2 = far_w2.at[0:2, : (ring - 2) * size, :]
    remote(most_w2, most_w2, w2_send, w2_recv.at[0], across).wait_recv()
    relay.wait_recv()
    far_pair = pair(5, far_w2.at[0:2], far_w2.at[2:4])
    far_pair.start()
    scale_swap.wait()
    w_share.wait_recv()
    far_pair.wait_recv()
    scale = jnp.max(far_scale[...], keepdims=True)
    for t, (first, last) in enumerate(tiles):
        at = slice(first, last)
        hid_copies[t][0].wait_recv()
        hid_copies[t][1].wait_recv()
        mine = dot(
            far_hid[0, at, :], jnp.concatenate([far_w2[0], far_w2[1]], axis=1), wide
        )
        theirs = dot(
            far_hid[1, at, :], jnp.concatenate([far_w2[2], far_w2[3]], axis=1), wide
        )
        near[at, :] = ((mine + theirs) * scale).astype(BF16)

        def far_cols_of(c, carry):
            lanes = pl.ds(pl.multiple_of(c * stripe, 128), stripe)
            added = total_out[at, lanes] + dot(near[at, :], w_far[:, lanes])
            staged[at, lanes] = added.astype(BF16)
            pltpu.make_async_copy(staged.at[at, lanes], out.at[at, lanes], out_sem).start()
            return carry

        lax.fori_loop(0, STRIPES, far_cols_of, 0)
    pltpu.make_async_copy(staged, out, out_sem).wait()
    for t in range(len(TILES)):
        tile_sent(t)
    near_copy.wait_send()
    near_w2_copy.wait_send()
    sent_w2 = far_w2.at[0:2, : (ring - 1) * size, :]
    remote(sent_w2, sent_w2, w2_send, w2_recv.at[0], across).wait_send()
    relay.wait_send()
    far_pair.wait_send()
    w_share.wait_send()
    for copy in (k_pair, u_pair, q_pair):
        copy.wait_send()


def copy_kernel(source, target, held, in_sem, out_sem):
    rows = held.shape[0] // COPY_PIECES
    pieces = [pl.ds(piece * rows, rows) for piece in range(COPY_PIECES)]
    reads = [
        pltpu.make_async_copy(source.at[at, :], held.at[at, :], in_sem.at[piece])
        for piece, at in enumerate(pieces)
    ]
    for read in reads:
        read.start()
    for read, at in zip(reads, pieces):
        read.wait()
        pltpu.make_async_copy(held.at[at, :], target.at[at, :], out_sem).start()
    pltpu.make_async_copy(held, target, out_sem).wait()


def shards(n_ctx, queries, keys, values, rates, w_up, w_gate, w_down, w_out):
    tokens, rows = keys.shape
    cols = w_up.shape[2] // CORES
    half = w_out.shape[1] // 2
    ring = n_ctx // CORES
    size = rows // ring
    bits = n_ctx.bit_length() - 1
    flows = GROUP * LANE_PARTS
    vmem = pl.BlockSpec(memory_space=pltpu.VMEM)
    anywhere = pl.BlockSpec(memory_space=pl.ANY)
    dma = pltpu.SemaphoreType.DMA
    mixed = pl.pallas_call(
        functools.partial(layer_kernel, n_ctx),
        out_shape=jax.ShapeDtypeStruct((tokens, half), BF16),
        in_specs=[anywhere] * 3 + [vmem] + [anywhere] * 4,
        out_specs=anywhere,
        scratch_shapes=[
            pltpu.VMEM((2 * tokens, rows), BF16),
            pltpu.VMEM((2 * tokens, rows), BF16),
            pltpu.VMEM((2 * tokens, rows), BF16),
            pltpu.VMEM((tokens, rows), BF16),
            pltpu.VMEM((rows, 2 * tokens), BF16),
            pltpu.VMEM((rows, 2 * tokens), BF16),
            pltpu.VMEM((rows, cols), BF16),
            pltpu.VMEM((rows, cols), BF16),
            pltpu.VMEM((cols, rows), BF16),
            pltpu.VMEM((rows, cols), BF16),
            pltpu.VMEM((GROUP, 2 * tokens, cols), F32),
            pltpu.VMEM((GROUP, 2 * tokens, cols), BF16),
            pltpu.VMEM((flows, rows, cols // LANE_PARTS), BF16),
            pltpu.VMEM((flows, rows, cols // LANE_PARTS), BF16),
            pltpu.VMEM((flows, ring - 1, size, cols // LANE_PARTS), BF16),
            pltpu.VMEM((flows, size, cols // LANE_PARTS), F32),
            pltpu.VMEM((bits + 1, GROUP, 8, 128), F32),
            pltpu.VMEM((STEPS * bits, GROUP, 8, 128), F32),
            pltpu.VMEM((CORES, GROUP, 8, 128), F32),
            pltpu.VMEM((2 * tokens, cols), BF16),
            pltpu.VMEM((tokens, cols), BF16),
            pltpu.VMEM((CORES, tokens, cols), BF16),
            pltpu.VMEM((LANE_PARTS, rows, cols // LANE_PARTS), BF16),
            pltpu.VMEM((CORES * LANE_PARTS, rows, cols // LANE_PARTS), BF16),
            pltpu.VMEM((8, 128), F32),
            pltpu.VMEM((8, 128), F32),
            pltpu.VMEM((rows, half), BF16),
            pltpu.VMEM((rows, half), BF16),
            pltpu.VMEM((tokens, rows), BF16),
            pltpu.VMEM((tokens, half), F32),
            pltpu.VMEM((tokens, half), BF16),
            dma((2,)),
            dma((flows, 2 * (ring - 1))),
            dma((6,)),
            dma((6,)),
            dma((bits,)),
            dma((STEPS * bits,)),
            dma((2,)),
            dma((2,)),
            dma,
            dma((2,)),
            dma((2,)),
            dma,
            dma,
            dma((len(TILES) + 1,)),
            dma((2 * len(TILES) + 1,)),
            dma((7,)),
            dma,
        ],
        compiler_params=pltpu.CompilerParams(
            collective_id=0, has_side_effects=True, vmem_limit_bytes=60 << 20
        ),
    )(queries, keys, values, rates.T, w_up[0], w_gate[0], w_down[0], w_out)
    return pl.pallas_call(
        copy_kernel,
        out_shape=jax.ShapeDtypeStruct((tokens, half), BF16),
        in_specs=[anywhere],
        out_specs=anywhere,
        scratch_shapes=[pltpu.VMEM((tokens, half), BF16), dma((COPY_PIECES,)), dma],
    )(mixed)


def solution(mesh):
    def body(*args):
        return shards(mesh.shape["ctx"], *args)

    return jax.shard_map(
        body,
        mesh=mesh,
        in_specs=(
            P("ctx", "head"),
            P("ctx", "head"),
            P("ctx", "head"),
            P("ctx", "head"),
            P("head", None, None),
            P("head", None, None),
            P("head", None, None),
            P("head", None),
        ),
        out_specs=P("ctx", "head"),
        check_vma=False,
    )
```

```python
import functools

import jax
import jax.numpy as jnp
from jax import lax
from jax.experimental import pallas as pl
from jax.experimental.pallas import tpu as pltpu
from jax.sharding import PartitionSpec as P

STEPS = 2
F32 = jnp.float32
BF16 = jnp.bfloat16
MESH = pl.DeviceIdType.MESH
GROUP = 3
LANE_PARTS = 2
CORES = 2
RING_ROWS = 4
TILES = (1, 1)
PIECES = 2
STRIPES = 5


def ring_place(chip, width):
    row, turn = chip // width, width - 1 - chip % width
    odd = turn % 2
    along = (1 - odd) * (row - 1) + odd * (RING_ROWS - 1 - row)
    return jnp.where(row == 0, chip, width + (RING_ROWS - 1) * turn + along)


def ring_chip(place, width):
    past = jnp.maximum(place - width, 0)
    turn, along = past // (RING_ROWS - 1), past % (RING_ROWS - 1)
    odd = turn % 2
    row = (1 - odd) * (1 + along) + odd * (RING_ROWS - 1 - along)
    return jnp.where(place < width, place, row * width + width - 1 - turn)


def dot(left, right, dims=((1,), (0,))):
    return lax.dot_general(left, right, (dims, ((), ())), preferred_element_type=F32)


def square_sum(block):
    return jnp.sum((block * block).reshape(-1, 8, block.shape[-1]), axis=0)


def lane_fold(block):
    return block[:, :128] + block[:, 128:]


def layer_kernel(n_ctx, q, k, v, r, w0, w1, w2, w_out, out, *scratch):
    (
        ks, us, qs, vin, kt, ut, first0, first1, in2, first2,
        acts, mid, grads, blocks, arrived, kept, tally, tally_in, norm_sums,
        hq, near_hid, far_hid, near_w2, far_w2, far_scale, scale_out,
        w_near, w_far, near, total_out,
        ring_send, ring_recv, pair_send, pair_recv, tally_send, tally_recv,
        side_send, side_recv, w2_send, w2_recv, relay_sem, near_send, near_recv, hid_send, hid_recv, local_sem,
    ) = scratch
    tokens, rows = k.shape
    cols = first0.shape[1]
    half = w_out.shape[1] // 2
    ring = n_ctx // CORES
    width = ring // RING_ROWS
    size = rows // ring
    bits = n_ctx.bit_length() - 1
    me = lax.axis_index("ctx")
    head = lax.axis_index("head")
    core = me % CORES
    chip = me // CORES
    place = ring_place(chip, width)
    right = {"ctx": ring_chip((place + 1) % ring, width) * CORES + core}
    left = {"ctx": ring_chip((place + ring - 1) % ring, width) * CORES + core}
    sibling = {"ctx": chip * CORES + 1 - core}
    across = {"head": 1 - head}
    diagonal = {"ctx": chip * CORES + 1 - core, "head": 1 - head}
    tally_partners = [
        {"ctx": me + (1 - 2 * ((me // (1 << bit)) % 2)) * (1 << bit)}
        for bit in range(bits)
    ]

    def remote(source, target, send_sem, recv_sem, device):
        return pltpu.make_async_remote_copy(
            src_ref=source,
            dst_ref=target,
            send_sem=send_sem,
            recv_sem=recv_sem,
            device_id=device,
            device_id_type=MESH,
        )

    def local(slot, source, target):
        return pltpu.make_async_copy(source, target, local_sem.at[slot])

    own_cols = pl.ds(pl.multiple_of(core * cols, 128), cols)
    own, other = slice(0, tokens), slice(tokens, 2 * tokens)
    loads = [
        local(0, k, ks.at[own, :]),
        local(1, v, vin),
        local(2, w0.at[:, own_cols], first0),
        local(3, w1.at[:, own_cols], first1),
        local(4, w2.at[pl.ds(pl.multiple_of(core * cols, 128), cols), :], in2),
        local(5, q, qs.at[own, :]),
    ]
    for load in loads[:5]:
        load.start()

    partners = [right, left, sibling, across, diagonal] + tally_partners
    barrier = pltpu.get_barrier_semaphore()
    for target in partners:
        pl.semaphore_signal(barrier, inc=1, device_id=target, device_id_type=MESH)
    pl.semaphore_wait(barrier, len(partners))

    def pair(slot, source, target):
        return remote(source, target, pair_send.at[slot], pair_recv.at[slot], sibling)

    k_pair = pair(0, k, ks.at[other, :])
    k_pair.start()
    loads[5].start()
    near_cols = pl.ds(pl.multiple_of(head * half, 128), half)
    far_cols = pl.ds(pl.multiple_of((1 - head) * half, 128), half)
    depth = rows // CORES
    own_rows = pl.ds(pl.multiple_of(core * depth, depth), depth)
    w_swap = remote(
        w_out.at[own_rows, far_cols], w_far.at[own_rows, :],
        side_send.at[0], side_recv.at[0], across,
    )
    w_swap.start()

    loads[1].wait()
    rate = jnp.broadcast_to(r[...], (128, tokens)).T
    for t in range(rows // 128):
        at = slice(t * 128, (t + 1) * 128)
        scaled = (rate * vin[:, at].astype(F32)).astype(BF16)
        us[own, at] = scaled
        ut[at, own] = scaled.T
    u_pair = pair(1, us.at[own, :], us.at[other, :])
    u_pair.start()

    def turned(source, target, side):
        for t in range(rows // 128):
            at = slice(t * 128, (t + 1) * 128)
            target[at, side] = source[side, at].T

    loads[0].wait()
    turned(ks, kt, own)
    q_pair = pair(2, q, qs.at[other, :])
    q_pair.start()
    w_copy = local(6, w_out.at[:, near_cols], w_near)
    w_copy.start()
    for load in loads[2:5]:
        load.wait()
    for t in range(rows // 128):
        at = slice(t * 128, (t + 1) * 128)
        first2[at, :] = in2[:, at].T

    firsts = (first0, first1, first2)
    scales = [None] * GROUP

    def weight(step, w):
        if step == 0:
            return firsts[w][...]
        return jnp.concatenate([blocks[2 * w], blocks[2 * w + 1]], axis=1)

    def act_dot(step, w, source, at):
        product = dot(source[at, :], weight(step, w))
        acts[w, at, :] = product

    for w, source in enumerate((ks, ks, us)):
        act_dot(0, w, source, own)

    half_pieces = tokens // 128
    whole = (0, 2 * half_pieces)

    def hid_gates(by, span):
        def one(piece, carry):
            at = pl.ds(pl.multiple_of(piece * 128, 128), 128)
            act, lin = acts[0, at, :], acts[1, at, :]
            if by[0] is not None:
                act, lin = act * by[0], lin * by[1]
            mid[2, at, :] = (act * jax.nn.sigmoid(act) * lin).astype(BF16)
            return carry

        lax.fori_loop(*span, one, 0)

    def err_gates(by, span):
        def one(piece, carry):
            at = pl.ds(pl.multiple_of(piece * 128, 128), 128)
            act, lin, err = acts[0, at, :], acts[1, at, :], acts[2, at, :]
            if by[0] is not None:
                act, lin, err = act * by[0], lin * by[1], err * by[2]
            sig = jax.nn.sigmoid(act)
            mid[0, at, :] = (err * lin * sig * (1.0 + act * (1.0 - sig))).astype(BF16)
            mid[1, at, :] = (err * (act * sig)).astype(BF16)
            return carry

        lax.fori_loop(*span, one, 0)

    hid_gates(scales, (0, half_pieces))
    err_gates(scales, (0, half_pieces))
    k_pair.wait_recv()
    act_dot(0, 0, ks, other)
    act_dot(0, 1, ks, other)
    hid_gates(scales, (half_pieces, 2 * half_pieces))

    flows = [(w, h) for w in range(GROUP) for h in range(LANE_PARTS)]

    def reach(h):
        longer = ring // 2
        return (longer, ring - 1 - longer) if h == 0 else (ring - 1 - longer, longer)

    def chunk(number):
        return pl.ds(pl.multiple_of((number % ring) * size, size), size)

    copies = {}

    def ring_sent(phase):
        all_sent = grads.at[:, : (ring - 1) * size, :]
        remote(all_sent, all_sent, ring_send.at[phase], ring_recv.at[0, 0], right).wait_send()

    for step in range(STEPS):

        def send(flow, slot, source, target, device):
            phase = ring_send.at[0 if slot < ring - 1 else 1]
            copy = remote(source, target, phase, ring_recv.at[flow, slot], device)
            copy.start()
            copies[flow, slot] = copy

        def send_sum(flow, to_right, s):
            far, back = reach(flow % LANE_PARTS)
            at = chunk(place + far - s) if to_right else chunk(place + ring - back + s)
            slot = s if to_right else far + s
            device = right if to_right else left
            send(flow, slot, grads.at[flow, at, :], arrived.at[flow, slot], device)

        def send_block(flow, to_right, t):
            far, back = reach(flow % LANE_PARTS)
            at = chunk(place + ring - t) if to_right else chunk(place + t)
            slot = ring - 1 + (t if to_right else far + t)
            device = right if to_right else left
            here = blocks.at[flow, at, :]
            send(flow, slot, here, here, device)

        def pass_sum(flow, to_right, s):
            far, back = reach(flow % LANE_PARTS)
            slot = s if to_right else far + s
            at = chunk(place + far - 1 - s) if to_right else chunk(place + ring + 1 - back + s)
            copies[flow, slot].wait_recv()
            total = grads[flow, at, :].astype(F32) + arrived[flow, slot].astype(F32)
            grads[flow, at, :] = total.astype(BF16)
            send_sum(flow, to_right, s + 1)

        def send_w2(flow, offset):
            here = chunk(place + ring + offset)
            if abs(offset) < ring // 2:
                slot = 1 if offset == ring // 2 - 1 else 0
                target = far_w2.at[flow % LANE_PARTS, here, :]
                remote(
                    blocks.at[flow, here, :], target, w2_send, w2_recv.at[slot], across
                ).start()
            target = near_w2.at[flow % LANE_PARTS, here, :]
            remote(
                blocks.at[flow, here, :], target, near_send, near_recv, sibling
            ).start()

        def grad(w):
            source = ut if w == 2 else kt

            for piece in range(PIECES):
                at = slice(piece * (rows // PIECES), (piece + 1) * (rows // PIECES))
                product = dot(source[at, :], mid[w]).astype(BF16)
                grads[2 * w, at, :] = product[:, :128]
                grads[2 * w + 1, at, :] = product[:, 128:]
            for h in range(LANE_PARTS):
                send_sum(2 * w + h, True, 0)
                send_sum(2 * w + h, False, 0)

        if step == 0:
            turned(ks, kt, other)
            u_pair.wait_recv()
            turned(us, ut, other)
            grad(2)
            act_dot(0, 2, us, other)
            err_gates(scales, (half_pieces, 2 * half_pieces))
        else:
            err_gates(scales, whole)
        grad(0)
        grad(1)
        if step == 0:
            for w in range(GROUP):
                norm_sums[0, w] = lane_fold(square_sum(firsts[w][...].astype(F32)))
            norm_pair = pair(3, norm_sums.at[0], norm_sums.at[1])
            norm_pair.start()
        turn = ring // 2 - 1
        ordered = [2 * w + h for w in range(GROUP) for h in range(LANE_PARTS)]
        for s in range(turn):
            for flow in ordered:
                far, back = reach(flow % LANE_PARTS)
                if s < far - 1:
                    pass_sum(flow, True, s)
                if s < back - 1:
                    pass_sum(flow, False, s)
        for flow in ordered:
            far, back = reach(flow % LANE_PARTS)
            w, h = flows[flow]
            at = chunk(place)
            copies[flow, far - 1].wait_recv()
            copies[flow, ring - 2].wait_recv()
            total = grads[flow, at, :].astype(F32) + arrived[flow, far - 1].astype(F32)
            total = total + arrived[flow, ring - 2].astype(F32)
            if step == 0:
                lanes = slice(h * 128, (h + 1) * 128)
                moved = firsts[w][at, lanes].astype(F32) + total
            else:
                moved = kept[flow] * scales[w] + total
            kept[flow] = moved
            rounded = moved.astype(BF16)
            blocks[flow, at, :] = rounded
            send_block(flow, True, 0)
            send_block(flow, False, 0)
            if step == STEPS - 1 and w == 2:
                send_w2(flow, 0)
            part = square_sum(rounded.astype(F32))
            tally[0, w] = part if h == 0 else tally[0, w] + part
        tallies = []

        def start_tally(stage):
            copy = remote(
                tally.at[stage], tally_in.at[step * bits + stage],
                tally_send.at[stage], tally_recv.at[step * bits + stage],
                tally_partners[stage],
            )
            copy.start()
            tallies.append(copy)

        def end_tally(stage):
            tallies[stage].wait_recv()
            tally[stage + 1] = tally[stage] + tally_in[step * bits + stage]
            if stage + 1 < bits:
                start_tally(stage + 1)

        def take_block(flow, t):
            far, back = reach(flow % LANE_PARTS)
            for to_right, count in ((True, far), (False, back)):
                if t >= count:
                    continue
                copies[flow, ring - 1 + (t if to_right else far + t)].wait_recv()
                if t < count - 1:
                    send_block(flow, to_right, t + 1)
                if step == STEPS - 1 and flow // LANE_PARTS == 2:
                    send_w2(flow, -1 - t if to_right else 1 + t)

        if step > 0:
            q_pair.wait_recv()
            loads[5].wait()
        wanted = (ks, ks, us) if step == 0 else (qs, qs)

        def pair_dot(w, one, two, fresh):
            pair_at = (chunk(one), chunk(two))
            right_side = jnp.concatenate(
                [
                    jnp.concatenate([blocks[2 * w, at, :], blocks[2 * w + 1, at, :]], axis=1)
                    for at in pair_at
                ],
                axis=0,
            )
            for side in (own, other):
                left_side = jnp.concatenate([wanted[w][side, at] for at in pair_at], axis=1)
                product = dot(left_side, right_side)
                acts[w, side, :] = product if fresh else acts[w, side, :] + product

        in_pairs = size % 128 == 0
        start_tally(0)
        ended = 0
        for t in range(turn):
            for flow in ordered:
                take_block(flow, t)
                w, h = flows[flow]
                if in_pairs and h == LANE_PARTS - 1 and w < len(wanted):
                    pair_dot(w, place + ring - 1 - t, place + 1 + t, t == 0)
                if flow == ordered[3] and ended < bits - 1:
                    end_tally(ended)
                    ended += 1
            if step == STEPS - 1 and t == turn // 2:
                w_swap.wait()
                w_share = pair(4, w_far.at[own_rows, :], w_far.at[own_rows, :])
                w_share.start()
        if step == 0:
            norm_pair.wait()
            norms = [
                jnp.sqrt(jnp.sum(norm_sums[0, w] + norm_sums[1, w], keepdims=True))
                for w in range(GROUP)
            ]

        def last_dot(w):
            for h in range(LANE_PARTS):
                take_block(2 * w + h, turn)
            if w >= len(wanted):
                return
            if in_pairs:
                pair_dot(w, place, place + ring // 2, False)
            else:
                act_dot(1, w, wanted[w], own)
                act_dot(1, w, wanted[w], other)

        last_dot(0)
        last_dot(1)
        while ended < bits:
            end_tally(ended)
            ended += 1
        scales = [
            norms[w] / jnp.sqrt(jnp.sum(tally[bits, w], keepdims=True) + 1e-06)
            for w in range(GROUP)
        ]
        ring_sent(0)
        if step == 0:
            hid_gates(scales, whole)
            grad(2)
            last_dot(2)
        ring_sent(1)
        for copy in tallies:
            copy.wait_send()

    ends = [tokens * sum(TILES[: t + 1]) // sum(TILES) for t in range(len(TILES))]
    tiles = [(end - tokens * part // sum(TILES), end) for end, part in zip(ends, TILES)]
    scale_out[...] = jnp.broadcast_to(scales[2], scale_out.shape)
    scale_swap = remote(
        scale_out, far_scale, side_send.at[1], side_recv.at[1], across
    )
    scale_swap.start()
    hid_copies = []

    def send_hid(slot, source, target, device):
        copy = remote(source, target, hid_send.at[slot // 2], hid_recv.at[slot], device)
        copy.start()
        return copy

    def hidden_of(side, first, last):
        at = slice(side * tokens + first, side * tokens + last)
        act = acts[0, at, :] * scales[0]
        lin = acts[1, at, :] * scales[1]
        hq[at, :] = (act * jax.nn.sigmoid(act) * lin).astype(BF16)

    def send_tile(t):
        first, last = tiles[t]
        to, at = slice(first, last), slice(tokens + first, tokens + last)
        hid_copies.append((
            send_hid(2 * t, hq.at[to, :], far_hid.at[0, to, :], across),
            send_hid(2 * t + 1, hq.at[at, :], far_hid.at[1, to, :], diagonal),
        ))

    for side in range(CORES):
        hidden_of(side, 0, tokens)
    last_dot(2)
    near_copy = send_hid(2 * len(TILES), hq.at[other, :], near_hid, sibling)
    send_tile(0)
    wide = ((1,), (1,))
    stripe = half // STRIPES

    def tile_sent(t):
        first, last = tiles[t]
        both = far_hid.at[:, first:last, :]
        remote(both, both, hid_send.at[t], hid_recv.at[2 * t], across).wait_send()

    def near_stripes(first, last):
        def one(c, carry):
            lanes = pl.ds(pl.multiple_of(c * stripe, 128), stripe)
            total_out[:, lanes] = dot(near[...], w_near[:, lanes])
            return carry

        lax.fori_loop(first, last, one, 0)

    near_w2_copy = remote(near_w2, near_w2, near_send, near_recv, sibling)
    near_w2_copy.wait_recv()
    near_copy.wait_recv()
    mine = dot(hq[own, :], jnp.concatenate([blocks[4], blocks[5]], axis=1), wide)
    theirs = dot(near_hid[...], jnp.concatenate([near_w2[0], near_w2[1]], axis=1), wide)
    near[...] = ((mine + theirs) * scales[2]).astype(BF16)
    for t in range(1, len(TILES)):
        send_tile(t)
    w_copy.wait()
    near_stripes(0, 2)
    next_w2 = far_w2.at[0:2, chunk(place + ring // 2 - 1), :]
    remote(next_w2, next_w2, w2_send, w2_recv.at[1], across).wait_recv()
    relay = remote(next_w2, next_w2, relay_sem.at[0], relay_sem.at[1], left)
    relay.start()
    near_stripes(2, STRIPES)
    most_w2 = far_w2.at[0:2, : (ring - 2) * size, :]
    remote(most_w2, most_w2, w2_send, w2_recv.at[0], across).wait_recv()
    relay.wait_recv()
    far_pair = pair(5, far_w2.at[0:2], far_w2.at[2:4])
    far_pair.start()
    scale_swap.wait()
    w_share.wait_recv()
    far_pair.wait_recv()
    scale = jnp.max(far_scale[...], keepdims=True)
    for t, (first, last) in enumerate(tiles):
        at = slice(first, last)
        hid_copies[t][0].wait_recv()
        hid_copies[t][1].wait_recv()
        mine = dot(
            far_hid[0, at, :], jnp.concatenate([far_w2[0], far_w2[1]], axis=1), wide
        )
        theirs = dot(
            far_hid[1, at, :], jnp.concatenate([far_w2[2], far_w2[3]], axis=1), wide
        )
        near[at, :] = ((mine + theirs) * scale).astype(BF16)

        def far_cols_of(c, carry):
            lanes = pl.ds(pl.multiple_of(c * stripe, 128), stripe)
            added = total_out[at, lanes] + dot(near[at, :], w_far[:, lanes])
            out[at, lanes] = added.astype(BF16)
            return carry

        lax.fori_loop(0, STRIPES, far_cols_of, 0)
    for t in range(len(TILES)):
        tile_sent(t)
    near_copy.wait_send()
    near_w2_copy.wait_send()
    sent_w2 = far_w2.at[0:2, : (ring - 1) * size, :]
    remote(sent_w2, sent_w2, w2_send, w2_recv.at[0], across).wait_send()
    relay.wait_send()
    far_pair.wait_send()
    w_share.wait_send()
    for copy in (k_pair, u_pair, q_pair):
        copy.wait_send()


def shards(n_ctx, queries, keys, values, rates, w_up, w_gate, w_down, w_out):
    tokens, rows = keys.shape
    cols = w_up.shape[2] // CORES
    half = w_out.shape[1] // 2
    ring = n_ctx // CORES
    size = rows // ring
    bits = n_ctx.bit_length() - 1
    flows = GROUP * LANE_PARTS
    vmem = pl.BlockSpec(memory_space=pltpu.VMEM)
    anywhere = pl.BlockSpec(memory_space=pl.ANY)
    dma = pltpu.SemaphoreType.DMA
    return pl.pallas_call(
        functools.partial(layer_kernel, n_ctx),
        out_shape=pltpu.VMEM((tokens, half), BF16),
        in_specs=[anywhere] * 3 + [vmem] + [anywhere] * 4,
        out_specs=vmem,
        scratch_shapes=[
            pltpu.VMEM((2 * tokens, rows), BF16),
            pltpu.VMEM((2 * tokens, rows), BF16),
            pltpu.VMEM((2 * tokens, rows), BF16),
            pltpu.VMEM((tokens, rows), BF16),
            pltpu.VMEM((rows, 2 * tokens), BF16),
            pltpu.VMEM((rows, 2 * tokens), BF16),
            pltpu.VMEM((rows, cols), BF16),
            pltpu.VMEM((rows, cols), BF16),
            pltpu.VMEM((cols, rows), BF16),
            pltpu.VMEM((rows, cols), BF16),
            pltpu.VMEM((GROUP, 2 * tokens, cols), F32),
            pltpu.VMEM((GROUP, 2 * tokens, cols), BF16),
            pltpu.VMEM((flows, rows, cols // LANE_PARTS), BF16),
            pltpu.VMEM((flows, rows, cols // LANE_PARTS), BF16),
            pltpu.VMEM((flows, ring - 1, size, cols // LANE_PARTS), BF16),
            pltpu.VMEM((flows, size, cols // LANE_PARTS), F32),
            pltpu.VMEM((bits + 1, GROUP, 8, 128), F32),
            pltpu.VMEM((STEPS * bits, GROUP, 8, 128), F32),
            pltpu.VMEM((CORES, GROUP, 8, 128), F32),
            pltpu.VMEM((2 * tokens, cols), BF16),
            pltpu.VMEM((tokens, cols), BF16),
            pltpu.VMEM((CORES, tokens, cols), BF16),
            pltpu.VMEM((LANE_PARTS, rows, cols // LANE_PARTS), BF16),
            pltpu.VMEM((CORES * LANE_PARTS, rows, cols // LANE_PARTS), BF16),
            pltpu.VMEM((8, 128), F32),
            pltpu.VMEM((8, 128), F32),
            pltpu.VMEM((rows, half), BF16),
            pltpu.VMEM((rows, half), BF16),
            pltpu.VMEM((tokens, rows), BF16),
            pltpu.VMEM((tokens, half), F32),
            dma((2,)),
            dma((flows, 2 * (ring - 1))),
            dma((6,)),
            dma((6,)),
            dma((bits,)),
            dma((STEPS * bits,)),
            dma((2,)),
            dma((2,)),
            dma,
            dma((2,)),
            dma((2,)),
            dma,
            dma,
            dma((len(TILES) + 1,)),
            dma((2 * len(TILES) + 1,)),
            dma((7,)),
        ],
        compiler_params=pltpu.CompilerParams(
            collective_id=0, has_side_effects=True, vmem_limit_bytes=60 << 20
        ),
    )(queries, keys, values, rates.T, w_up[0], w_gate[0], w_down[0], w_out)


def solution(mesh):
    def body(*args):
        return shards(mesh.shape["ctx"], *args)

    return jax.shard_map(
        body,
        mesh=mesh,
        in_specs=(
            P("ctx", "head"),
            P("ctx", "head"),
            P("ctx", "head"),
            P("ctx", "head"),
            P("head", None, None),
            P("head", None, None),
            P("head", None, None),
            P("head", None),
        ),
        out_specs=P("ctx", "head"),
        check_vma=False,
    )
```

```python
import functools

import jax
import jax.numpy as jnp
from jax import lax
from jax.experimental import pallas as pl
from jax.experimental.pallas import tpu as pltpu
from jax.sharding import PartitionSpec as P

STEPS = 2
F32 = jnp.float32
BF16 = jnp.bfloat16
MESH = pl.DeviceIdType.MESH
GROUP = 3
LANE_PARTS = 2
CORES = 2
RING_ROWS = 4
TILES = (1, 1)
PIECES = 2
STRIPES = 5


def ring_place(chip, width):
    row, turn = chip // width, width - 1 - chip % width
    odd = turn % 2
    along = (1 - odd) * (row - 1) + odd * (RING_ROWS - 1 - row)
    return jnp.where(row == 0, chip, width + (RING_ROWS - 1) * turn + along)


def ring_chip(place, width):
    past = jnp.maximum(place - width, 0)
    turn, along = past // (RING_ROWS - 1), past % (RING_ROWS - 1)
    odd = turn % 2
    row = (1 - odd) * (1 + along) + odd * (RING_ROWS - 1 - along)
    return jnp.where(place < width, place, row * width + width - 1 - turn)


def dot(left, right, dims=((1,), (0,))):
    return lax.dot_general(left, right, (dims, ((), ())), preferred_element_type=F32)


def square_sum(block):
    return jnp.sum((block * block).reshape(-1, 8, block.shape[-1]), axis=0)


def lane_fold(block):
    return block[:, :128] + block[:, 128:]


def layer_kernel(n_ctx, q, k, v, r, w0, w1, w2, w_out, out, *scratch):
    (
        ks, us, qs, vin, kt, ut, first0, first1, in2, first2,
        acts, mid, grads, blocks, arrived, kept, tally, tally_in, norm_sums,
        hq, near_hid, far_hid, near_w2, far_w2, far_scale, scale_out,
        w_near, w_far, near, total_out,
        ring_send, ring_recv, pair_send, pair_recv, tally_send, tally_recv,
        side_send, side_recv, w2_send, w2_recv, relay_sem, near_send, near_recv, hid_send, hid_recv, local_sem,
    ) = scratch
    tokens, rows = k.shape
    cols = first0.shape[1]
    half = w_out.shape[1] // 2
    ring = n_ctx // CORES
    width = ring // RING_ROWS
    size = rows // ring
    bits = n_ctx.bit_length() - 1
    me = lax.axis_index("ctx")
    head = lax.axis_index("head")
    core = me % CORES
    chip = me // CORES
    place = ring_place(chip, width)
    right = {"ctx": ring_chip((place + 1) % ring, width) * CORES + core}
    left = {"ctx": ring_chip((place + ring - 1) % ring, width) * CORES + core}
    sibling = {"ctx": chip * CORES + 1 - core}
    across = {"head": 1 - head}
    diagonal = {"ctx": chip * CORES + 1 - core, "head": 1 - head}
    tally_partners = [
        {"ctx": me + (1 - 2 * ((me // (1 << bit)) % 2)) * (1 << bit)}
        for bit in range(bits)
    ]

    def remote(source, target, send_sem, recv_sem, device):
        return pltpu.make_async_remote_copy(
            src_ref=source,
            dst_ref=target,
            send_sem=send_sem,
            recv_sem=recv_sem,
            device_id=device,
            device_id_type=MESH,
        )

    def local(slot, source, target):
        return pltpu.make_async_copy(source, target, local_sem.at[slot])

    own_cols = pl.ds(pl.multiple_of(core * cols, 128), cols)
    own, other = slice(0, tokens), slice(tokens, 2 * tokens)
    loads = [
        local(0, k, ks.at[own, :]),
        local(1, v, vin),
        local(2, w0.at[:, own_cols], first0),
        local(3, w1.at[:, own_cols], first1),
        local(4, w2.at[pl.ds(pl.multiple_of(core * cols, 128), cols), :], in2),
        local(5, q, qs.at[own, :]),
    ]
    for load in loads[:5]:
        load.start()

    partners = [right, left, sibling, across, diagonal]
    barrier = pltpu.get_barrier_semaphore()
    for target in partners:
        pl.semaphore_signal(barrier, inc=1, device_id=target, device_id_type=MESH)
    pl.semaphore_wait(barrier, len(partners))

    def pair(slot, source, target):
        return remote(source, target, pair_send.at[slot], pair_recv.at[slot], sibling)

    k_pair = pair(0, k, ks.at[other, :])
    k_pair.start()
    loads[5].start()
    near_cols = pl.ds(pl.multiple_of(head * half, 128), half)
    far_cols = pl.ds(pl.multiple_of((1 - head) * half, 128), half)
    depth = rows // CORES
    own_rows = pl.ds(pl.multiple_of(core * depth, depth), depth)
    w_swap = remote(
        w_out.at[own_rows, far_cols], w_far.at[own_rows, :],
        side_send.at[0], side_recv.at[0], across,
    )
    w_swap.start()

    loads[1].wait()
    rate = jnp.broadcast_to(r[...], (128, tokens)).T
    for t in range(rows // 128):
        at = slice(t * 128, (t + 1) * 128)
        scaled = (rate * vin[:, at].astype(F32)).astype(BF16)
        us[own, at] = scaled
        ut[at, own] = scaled.T
    u_pair = pair(1, us.at[own, :], us.at[other, :])
    u_pair.start()

    def turned(source, target, side):
        for t in range(rows // 128):
            at = slice(t * 128, (t + 1) * 128)
            target[at, side] = source[side, at].T

    loads[0].wait()
    turned(ks, kt, own)
    q_pair = pair(2, q, qs.at[other, :])
    q_pair.start()
    w_copy = local(6, w_out.at[:, near_cols], w_near)
    w_copy.start()
    for load in loads[2:5]:
        load.wait()
    for t in range(rows // 128):
        at = slice(t * 128, (t + 1) * 128)
        first2[at, :] = in2[:, at].T

    firsts = (first0, first1, first2)
    scales = [None] * GROUP

    def weight(step, w):
        if step == 0:
            return firsts[w][...]
        return jnp.concatenate([blocks[2 * w], blocks[2 * w + 1]], axis=1)

    def act_dot(step, w, source, at):
        product = dot(source[at, :], weight(step, w))
        acts[w, at, :] = product

    for w, source in enumerate((ks, ks, us)):
        act_dot(0, w, source, own)

    half_pieces = tokens // 128
    whole = (0, 2 * half_pieces)

    def hid_gates(by, span):
        def one(piece, carry):
            at = pl.ds(pl.multiple_of(piece * 128, 128), 128)
            act, lin = acts[0, at, :], acts[1, at, :]
            if by[0] is not None:
                act, lin = act * by[0], lin * by[1]
            mid[2, at, :] = (act * jax.nn.sigmoid(act) * lin).astype(BF16)
            return carry

        lax.fori_loop(*span, one, 0)

    def err_gates(by, span):
        def one(piece, carry):
            at = pl.ds(pl.multiple_of(piece * 128, 128), 128)
            act, lin, err = acts[0, at, :], acts[1, at, :], acts[2, at, :]
            if by[0] is not None:
                act, lin, err = act * by[0], lin * by[1], err * by[2]
            sig = jax.nn.sigmoid(act)
            mid[0, at, :] = (err * lin * sig * (1.0 + act * (1.0 - sig))).astype(BF16)
            mid[1, at, :] = (err * (act * sig)).astype(BF16)
            return carry

        lax.fori_loop(*span, one, 0)

    hid_gates(scales, (0, half_pieces))
    err_gates(scales, (0, half_pieces))
    k_pair.wait_recv()
    act_dot(0, 0, ks, other)
    act_dot(0, 1, ks, other)
    hid_gates(scales, (half_pieces, 2 * half_pieces))

    flows = [(w, h) for w in range(GROUP) for h in range(LANE_PARTS)]

    def reach(h):
        longer = ring // 2
        return (longer, ring - 1 - longer) if h == 0 else (ring - 1 - longer, longer)

    def chunk(number):
        return pl.ds(pl.multiple_of((number % ring) * size, size), size)

    copies = {}

    def ring_sent(phase):
        all_sent = grads.at[:, : (ring - 1) * size, :]
        remote(all_sent, all_sent, ring_send.at[phase], ring_recv.at[0, 0], right).wait_send()

    for step in range(STEPS):

        def send(flow, slot, source, target, device):
            phase = ring_send.at[0 if slot < ring - 1 else 1]
            copy = remote(source, target, phase, ring_recv.at[flow, slot], device)
            copy.start()
            copies[flow, slot] = copy

        def send_sum(flow, to_right, s):
            far, back = reach(flow % LANE_PARTS)
            at = chunk(place + far - s) if to_right else chunk(place + ring - back + s)
            slot = s if to_right else far + s
            device = right if to_right else left
            send(flow, slot, grads.at[flow, at, :], arrived.at[flow, slot], device)

        def send_block(flow, to_right, t):
            far, back = reach(flow % LANE_PARTS)
            at = chunk(place + ring - t) if to_right else chunk(place + t)
            slot = ring - 1 + (t if to_right else far + t)
            device = right if to_right else left
            here = blocks.at[flow, at, :]
            send(flow, slot, here, here, device)

        def pass_sum(flow, to_right, s):
            far, back = reach(flow % LANE_PARTS)
            slot = s if to_right else far + s
            at = chunk(place + far - 1 - s) if to_right else chunk(place + ring + 1 - back + s)
            copies[flow, slot].wait_recv()
            total = grads[flow, at, :].astype(F32) + arrived[flow, slot].astype(F32)
            grads[flow, at, :] = total.astype(BF16)
            send_sum(flow, to_right, s + 1)

        def send_w2(flow, offset):
            here = chunk(place + ring + offset)
            if abs(offset) < ring // 2:
                slot = 1 if offset == ring // 2 - 1 else 0
                target = far_w2.at[flow % LANE_PARTS, here, :]
                remote(
                    blocks.at[flow, here, :], target, w2_send, w2_recv.at[slot], across
                ).start()
            target = near_w2.at[flow % LANE_PARTS, here, :]
            remote(
                blocks.at[flow, here, :], target, near_send, near_recv, sibling
            ).start()

        def grad(w):
            source = ut if w == 2 else kt

            for piece in range(PIECES):
                at = slice(piece * (rows // PIECES), (piece + 1) * (rows // PIECES))
                product = dot(source[at, :], mid[w]).astype(BF16)
                grads[2 * w, at, :] = product[:, :128]
                grads[2 * w + 1, at, :] = product[:, 128:]
            for h in range(LANE_PARTS):
                send_sum(2 * w + h, True, 0)
                send_sum(2 * w + h, False, 0)

        if step == 0:
            turned(ks, kt, other)
            u_pair.wait_recv()
            turned(us, ut, other)
            grad(2)
            act_dot(0, 2, us, other)
            err_gates(scales, (half_pieces, 2 * half_pieces))
        else:
            err_gates(scales, whole)
        grad(0)
        grad(1)
        if step == 0:
            for w in range(GROUP):
                norm_sums[0, w] = lane_fold(square_sum(firsts[w][...].astype(F32)))
            norm_pair = pair(3, norm_sums.at[0], norm_sums.at[1])
            norm_pair.start()
        turn = ring // 2 - 1
        ordered = [2 * w + h for w in range(GROUP) for h in range(LANE_PARTS)]
        for s in range(turn):
            for flow in ordered:
                far, back = reach(flow % LANE_PARTS)
                if s < far - 1:
                    pass_sum(flow, True, s)
                if s < back - 1:
                    pass_sum(flow, False, s)
        for flow in ordered:
            far, back = reach(flow % LANE_PARTS)
            w, h = flows[flow]
            at = chunk(place)
            copies[flow, far - 1].wait_recv()
            copies[flow, ring - 2].wait_recv()
            total = grads[flow, at, :].astype(F32) + arrived[flow, far - 1].astype(F32)
            total = total + arrived[flow, ring - 2].astype(F32)
            if step == 0:
                lanes = slice(h * 128, (h + 1) * 128)
                moved = firsts[w][at, lanes].astype(F32) + total
            else:
                moved = kept[flow] * scales[w] + total
            kept[flow] = moved
            rounded = moved.astype(BF16)
            blocks[flow, at, :] = rounded
            send_block(flow, True, 0)
            send_block(flow, False, 0)
            if step == STEPS - 1 and w == 2:
                send_w2(flow, 0)
            part = square_sum(rounded.astype(F32))
            tally[0, w] = part if h == 0 else tally[0, w] + part
        tallies = []

        def start_tally(stage):
            copy = remote(
                tally.at[stage], tally_in.at[step * bits + stage],
                tally_send.at[stage], tally_recv.at[step * bits + stage],
                tally_partners[stage],
            )
            copy.start()
            tallies.append(copy)

        def end_tally(stage):
            tallies[stage].wait_recv()
            tally[stage + 1] = tally[stage] + tally_in[step * bits + stage]
            if stage + 1 < bits:
                start_tally(stage + 1)

        def take_block(flow, t):
            far, back = reach(flow % LANE_PARTS)
            for to_right, count in ((True, far), (False, back)):
                if t >= count:
                    continue
                copies[flow, ring - 1 + (t if to_right else far + t)].wait_recv()
                if t < count - 1:
                    send_block(flow, to_right, t + 1)
                if step == STEPS - 1 and flow // LANE_PARTS == 2:
                    send_w2(flow, -1 - t if to_right else 1 + t)

        if step > 0:
            q_pair.wait_recv()
            loads[5].wait()
        wanted = (ks, ks, us) if step == 0 else (qs, qs)

        def pair_dot(w, one, two, fresh):
            pair_at = (chunk(one), chunk(two))
            right_side = jnp.concatenate(
                [
                    jnp.concatenate([blocks[2 * w, at, :], blocks[2 * w + 1, at, :]], axis=1)
                    for at in pair_at
                ],
                axis=0,
            )
            for side in (own, other):
                left_side = jnp.concatenate([wanted[w][side, at] for at in pair_at], axis=1)
                product = dot(left_side, right_side)
                acts[w, side, :] = product if fresh else acts[w, side, :] + product

        in_pairs = size % 128 == 0
        start_tally(0)
        ended = 0
        for t in range(turn):
            for flow in ordered:
                take_block(flow, t)
                w, h = flows[flow]
                if in_pairs and h == LANE_PARTS - 1 and w < len(wanted):
                    pair_dot(w, place + ring - 1 - t, place + 1 + t, t == 0)
                if flow == ordered[3] and ended < bits - 1:
                    end_tally(ended)
                    ended += 1
            if step == STEPS - 1 and t == turn // 2:
                w_swap.wait()
                w_share = pair(4, w_far.at[own_rows, :], w_far.at[own_rows, :])
                w_share.start()
        if step == 0:
            norm_pair.wait()
            norms = [
                jnp.sqrt(jnp.sum(norm_sums[0, w] + norm_sums[1, w], keepdims=True))
                for w in range(GROUP)
            ]

        def last_dot(w):
            for h in range(LANE_PARTS):
                take_block(2 * w + h, turn)
            if w >= len(wanted):
                return
            if in_pairs:
                pair_dot(w, place, place + ring // 2, False)
            else:
                act_dot(1, w, wanted[w], own)
                act_dot(1, w, wanted[w], other)

        last_dot(0)
        last_dot(1)
        while ended < bits:
            end_tally(ended)
            ended += 1
        scales = [
            norms[w] / jnp.sqrt(jnp.sum(tally[bits, w], keepdims=True) + 1e-06)
            for w in range(GROUP)
        ]
        ring_sent(0)
        if step == 0:
            hid_gates(scales, whole)
            grad(2)
            last_dot(2)
        ring_sent(1)
        for copy in tallies:
            copy.wait_send()

    ends = [tokens * sum(TILES[: t + 1]) // sum(TILES) for t in range(len(TILES))]
    tiles = [(end - tokens * part // sum(TILES), end) for end, part in zip(ends, TILES)]
    scale_out[...] = jnp.broadcast_to(scales[2], scale_out.shape)
    scale_swap = remote(
        scale_out, far_scale, side_send.at[1], side_recv.at[1], across
    )
    scale_swap.start()
    hid_copies = []

    def send_hid(slot, source, target, device):
        copy = remote(source, target, hid_send.at[slot // 2], hid_recv.at[slot], device)
        copy.start()
        return copy

    def hidden_of(side, first, last):
        at = slice(side * tokens + first, side * tokens + last)
        act = acts[0, at, :] * scales[0]
        lin = acts[1, at, :] * scales[1]
        hq[at, :] = (act * jax.nn.sigmoid(act) * lin).astype(BF16)

    def send_tile(t):
        first, last = tiles[t]
        to, at = slice(first, last), slice(tokens + first, tokens + last)
        hid_copies.append((
            send_hid(2 * t, hq.at[to, :], far_hid.at[0, to, :], across),
            send_hid(2 * t + 1, hq.at[at, :], far_hid.at[1, to, :], diagonal),
        ))

    for side in range(CORES):
        hidden_of(side, 0, tokens)
    last_dot(2)
    near_copy = send_hid(2 * len(TILES), hq.at[other, :], near_hid, sibling)
    send_tile(0)
    wide = ((1,), (1,))
    stripe = half // STRIPES

    def tile_sent(t):
        first, last = tiles[t]
        both = far_hid.at[:, first:last, :]
        remote(both, both, hid_send.at[t], hid_recv.at[2 * t], across).wait_send()

    def near_stripes(first, last):
        def one(c, carry):
            lanes = pl.ds(pl.multiple_of(c * stripe, 128), stripe)
            total_out[:, lanes] = dot(near[...], w_near[:, lanes])
            return carry

        lax.fori_loop(first, last, one, 0)

    near_w2_copy = remote(near_w2, near_w2, near_send, near_recv, sibling)
    near_w2_copy.wait_recv()
    near_copy.wait_recv()
    mine = dot(hq[own, :], jnp.concatenate([blocks[4], blocks[5]], axis=1), wide)
    theirs = dot(near_hid[...], jnp.concatenate([near_w2[0], near_w2[1]], axis=1), wide)
    near[...] = ((mine + theirs) * scales[2]).astype(BF16)
    for t in range(1, len(TILES)):
        send_tile(t)
    w_copy.wait()
    near_stripes(0, 2)
    next_w2 = far_w2.at[0:2, chunk(place + ring // 2 - 1), :]
    remote(next_w2, next_w2, w2_send, w2_recv.at[1], across).wait_recv()
    relay = remote(next_w2, next_w2, relay_sem.at[0], relay_sem.at[1], left)
    relay.start()
    near_stripes(2, STRIPES)
    most_w2 = far_w2.at[0:2, : (ring - 2) * size, :]
    remote(most_w2, most_w2, w2_send, w2_recv.at[0], across).wait_recv()
    relay.wait_recv()
    far_pair = pair(5, far_w2.at[0:2], far_w2.at[2:4])
    far_pair.start()
    scale_swap.wait()
    w_share.wait_recv()
    far_pair.wait_recv()
    scale = jnp.max(far_scale[...], keepdims=True)
    for t, (first, last) in enumerate(tiles):
        at = slice(first, last)
        hid_copies[t][0].wait_recv()
        hid_copies[t][1].wait_recv()
        mine = dot(
            far_hid[0, at, :], jnp.concatenate([far_w2[0], far_w2[1]], axis=1), wide
        )
        theirs = dot(
            far_hid[1, at, :], jnp.concatenate([far_w2[2], far_w2[3]], axis=1), wide
        )
        near[at, :] = ((mine + theirs) * scale).astype(BF16)

        def far_cols_of(c, carry):
            lanes = pl.ds(pl.multiple_of(c * stripe, 128), stripe)
            added = total_out[at, lanes] + dot(near[at, :], w_far[:, lanes])
            out[at, lanes] = added.astype(BF16)
            return carry

        lax.fori_loop(0, STRIPES, far_cols_of, 0)
    for t in range(len(TILES)):
        tile_sent(t)
    near_copy.wait_send()
    near_w2_copy.wait_send()
    sent_w2 = far_w2.at[0:2, : (ring - 1) * size, :]
    remote(sent_w2, sent_w2, w2_send, w2_recv.at[0], across).wait_send()
    relay.wait_send()
    far_pair.wait_send()
    w_share.wait_send()
    for copy in (k_pair, u_pair, q_pair):
        copy.wait_send()


def shards(n_ctx, queries, keys, values, rates, w_up, w_gate, w_down, w_out):
    tokens, rows = keys.shape
    cols = w_up.shape[2] // CORES
    half = w_out.shape[1] // 2
    ring = n_ctx // CORES
    size = rows // ring
    bits = n_ctx.bit_length() - 1
    flows = GROUP * LANE_PARTS
    vmem = pl.BlockSpec(memory_space=pltpu.VMEM)
    anywhere = pl.BlockSpec(memory_space=pl.ANY)
    dma = pltpu.SemaphoreType.DMA
    return pl.pallas_call(
        functools.partial(layer_kernel, n_ctx),
        out_shape=pltpu.VMEM((tokens, half), BF16),
        in_specs=[anywhere] * 3 + [vmem] + [anywhere] * 4,
        out_specs=vmem,
        scratch_shapes=[
            pltpu.VMEM((2 * tokens, rows), BF16),
            pltpu.VMEM((2 * tokens, rows), BF16),
            pltpu.VMEM((2 * tokens, rows), BF16),
            pltpu.VMEM((tokens, rows), BF16),
            pltpu.VMEM((rows, 2 * tokens), BF16),
            pltpu.VMEM((rows, 2 * tokens), BF16),
            pltpu.VMEM((rows, cols), BF16),
            pltpu.VMEM((rows, cols), BF16),
            pltpu.VMEM((cols, rows), BF16),
            pltpu.VMEM((rows, cols), BF16),
            pltpu.VMEM((GROUP, 2 * tokens, cols), F32),
            pltpu.VMEM((GROUP, 2 * tokens, cols), BF16),
            pltpu.VMEM((flows, rows, cols // LANE_PARTS), BF16),
            pltpu.VMEM((flows, rows, cols // LANE_PARTS), BF16),
            pltpu.VMEM((flows, ring - 1, size, cols // LANE_PARTS), BF16),
            pltpu.VMEM((flows, size, cols // LANE_PARTS), F32),
            pltpu.VMEM((bits + 1, GROUP, 8, 128), F32),
            pltpu.VMEM((STEPS * bits, GROUP, 8, 128), F32),
            pltpu.VMEM((CORES, GROUP, 8, 128), F32),
            pltpu.VMEM((2 * tokens, cols), BF16),
            pltpu.VMEM((tokens, cols), BF16),
            pltpu.VMEM((CORES, tokens, cols), BF16),
            pltpu.VMEM((LANE_PARTS, rows, cols // LANE_PARTS), BF16),
            pltpu.VMEM((CORES * LANE_PARTS, rows, cols // LANE_PARTS), BF16),
            pltpu.VMEM((8, 128), F32),
            pltpu.VMEM((8, 128), F32),
            pltpu.VMEM((rows, half), BF16),
            pltpu.VMEM((rows, half), BF16),
            pltpu.VMEM((tokens, rows), BF16),
            pltpu.VMEM((tokens, half), F32),
            dma((2,)),
            dma((flows, 2 * (ring - 1))),
            dma((6,)),
            dma((6,)),
            dma((bits,)),
            dma((STEPS * bits,)),
            dma((2,)),
            dma((2,)),
            dma,
            dma((2,)),
            dma((2,)),
            dma,
            dma,
            dma((len(TILES) + 1,)),
            dma((2 * len(TILES) + 1,)),
            dma((7,)),
        ],
        compiler_params=pltpu.CompilerParams(
            collective_id=0, has_side_effects=True, vmem_limit_bytes=60 << 20
        ),
    )(queries, keys, values, rates.T, w_up[0], w_gate[0], w_down[0], w_out)


def solution(mesh):
    def body(*args):
        return shards(mesh.shape["ctx"], *args)

    return jax.shard_map(
        body,
        mesh=mesh,
        in_specs=(
            P("ctx", "head"),
            P("ctx", "head"),
            P("ctx", "head"),
            P("ctx", "head"),
            P("head", None, None),
            P("head", None, None),
            P("head", None, None),
            P("head", None),
        ),
        out_specs=P("ctx", "head"),
        check_vma=False,
    )
```

```python
import functools

import jax
import jax.numpy as jnp
from jax import lax
from jax.experimental import pallas as pl
from jax.experimental.pallas import tpu as pltpu
from jax.sharding import PartitionSpec as P

STEPS = 2
F32 = jnp.float32
BF16 = jnp.bfloat16
MESH = pl.DeviceIdType.MESH
GROUP = 3
LANE_PARTS = 2
CORES = 2
RING_ROWS = 4
TILES = (1, 1)
PIECES = 2
STRIPES = 2


def ring_place(chip, width):
    row, turn = chip // width, width - 1 - chip % width
    odd = turn % 2
    along = (1 - odd) * (row - 1) + odd * (RING_ROWS - 1 - row)
    return jnp.where(row == 0, chip, width + (RING_ROWS - 1) * turn + along)


def ring_chip(place, width):
    past = jnp.maximum(place - width, 0)
    turn, along = past // (RING_ROWS - 1), past % (RING_ROWS - 1)
    odd = turn % 2
    row = (1 - odd) * (1 + along) + odd * (RING_ROWS - 1 - along)
    return jnp.where(place < width, place, row * width + width - 1 - turn)


def dot(left, right, dims=((1,), (0,))):
    return lax.dot_general(left, right, (dims, ((), ())), preferred_element_type=F32)


def square_sum(block):
    return jnp.sum((block * block).reshape(-1, 8, block.shape[-1]), axis=0)


def lane_fold(block):
    return block[:, :128] + block[:, 128:]


def layer_kernel(n_ctx, q, k, v, r, w0, w1, w2, w_out, out, *scratch):
    (
        ks, us, qs, vin, kt, ut, first0, first1, in2, first2,
        acts, mid, grads, blocks, arrived, kept, tally, tally_in, norm_sums,
        hq, near_hid, far_hid, near_w2, far_w2, far_scale, scale_out,
        w_near, w_far, near, total_out,
        ring_send, ring_recv, pair_send, pair_recv, tally_send, tally_recv,
        side_send, side_recv, w2_send, w2_recv, relay_sem, near_send, near_recv, hid_send, hid_recv, local_sem,
    ) = scratch
    tokens, rows = k.shape
    cols = first0.shape[1]
    half = w_out.shape[1] // 2
    ring = n_ctx // CORES
    width = ring // RING_ROWS
    size = rows // ring
    bits = n_ctx.bit_length() - 1
    me = lax.axis_index("ctx")
    head = lax.axis_index("head")
    core = me % CORES
    chip = me // CORES
    place = ring_place(chip, width)
    right = {"ctx": ring_chip((place + 1) % ring, width) * CORES + core}
    left = {"ctx": ring_chip((place + ring - 1) % ring, width) * CORES + core}
    sibling = {"ctx": chip * CORES + 1 - core}
    across = {"head": 1 - head}
    diagonal = {"ctx": chip * CORES + 1 - core, "head": 1 - head}
    tally_partners = [
        {"ctx": me + (1 - 2 * ((me // (1 << bit)) % 2)) * (1 << bit)}
        for bit in range(bits)
    ]

    def remote(source, target, send_sem, recv_sem, device):
        return pltpu.make_async_remote_copy(
            src_ref=source,
            dst_ref=target,
            send_sem=send_sem,
            recv_sem=recv_sem,
            device_id=device,
            device_id_type=MESH,
        )

    def local(slot, source, target):
        return pltpu.make_async_copy(source, target, local_sem.at[slot])

    own_cols = pl.ds(pl.multiple_of(core * cols, 128), cols)
    own, other = slice(0, tokens), slice(tokens, 2 * tokens)
    loads = [
        local(0, k, ks.at[own, :]),
        local(1, v, vin),
        local(2, w0.at[:, own_cols], first0),
        local(3, w1.at[:, own_cols], first1),
        local(4, w2.at[pl.ds(pl.multiple_of(core * cols, 128), cols), :], in2),
        local(5, q, qs.at[own, :]),
    ]
    for load in loads[:5]:
        load.start()

    partners = [right, left, sibling, across, diagonal]
    barrier = pltpu.get_barrier_semaphore()
    for target in partners:
        pl.semaphore_signal(barrier, inc=1, device_id=target, device_id_type=MESH)
    pl.semaphore_wait(barrier, len(partners))

    def pair(slot, source, target):
        return remote(source, target, pair_send.at[slot], pair_recv.at[slot], sibling)

    k_pair = pair(0, k, ks.at[other, :])
    k_pair.start()
    loads[5].start()
    near_cols = pl.ds(pl.multiple_of(head * half, 128), half)
    far_cols = pl.ds(pl.multiple_of((1 - head) * half, 128), half)
    depth = rows // CORES
    own_rows = pl.ds(pl.multiple_of(core * depth, depth), depth)
    w_swap = remote(
        w_out.at[own_rows, far_cols], w_far.at[own_rows, :],
        side_send.at[0], side_recv.at[0], across,
    )
    w_swap.start()

    loads[1].wait()
    rate = jnp.broadcast_to(r[...], (128, tokens)).T
    for t in range(rows // 128):
        at = slice(t * 128, (t + 1) * 128)
        scaled = (rate * vin[:, at].astype(F32)).astype(BF16)
        us[own, at] = scaled
        ut[at, own] = scaled.T
    u_pair = pair(1, us.at[own, :], us.at[other, :])
    u_pair.start()

    def turned(source, target, side):
        for t in range(rows // 128):
            at = slice(t * 128, (t + 1) * 128)
            target[at, side] = source[side, at].T

    loads[0].wait()
    turned(ks, kt, own)
    q_pair = pair(2, q, qs.at[other, :])
    q_pair.start()
    w_copy = local(6, w_out.at[:, near_cols], w_near)
    w_copy.start()
    for load in loads[2:5]:
        load.wait()
    for t in range(rows // 128):
        at = slice(t * 128, (t + 1) * 128)
        first2[at, :] = in2[:, at].T

    firsts = (first0, first1, first2)
    scales = [None] * GROUP

    def weight(step, w):
        if step == 0:
            return firsts[w][...]
        return jnp.concatenate([blocks[2 * w], blocks[2 * w + 1]], axis=1)

    def act_dot(step, w, source, at):
        product = dot(source[at, :], weight(step, w))
        acts[w, at, :] = product

    for w, source in enumerate((ks, ks, us)):
        act_dot(0, w, source, own)

    half_pieces = tokens // 128
    whole = (0, 2 * half_pieces)

    def hid_gates(by, span):
        def one(piece, carry):
            at = pl.ds(pl.multiple_of(piece * 128, 128), 128)
            act, lin = acts[0, at, :], acts[1, at, :]
            if by[0] is not None:
                act, lin = act * by[0], lin * by[1]
            mid[2, at, :] = (act * jax.nn.sigmoid(act) * lin).astype(BF16)
            return carry

        lax.fori_loop(*span, one, 0)

    def err_gates(by, span):
        def one(piece, carry):
            at = pl.ds(pl.multiple_of(piece * 128, 128), 128)
            act, lin, err = acts[0, at, :], acts[1, at, :], acts[2, at, :]
            if by[0] is not None:
                act, lin, err = act * by[0], lin * by[1], err * by[2]
            sig = jax.nn.sigmoid(act)
            mid[0, at, :] = (err * lin * sig * (1.0 + act * (1.0 - sig))).astype(BF16)
            mid[1, at, :] = (err * (act * sig)).astype(BF16)
            return carry

        lax.fori_loop(*span, one, 0)

    hid_gates(scales, (0, half_pieces))
    err_gates(scales, (0, half_pieces))
    k_pair.wait_recv()
    act_dot(0, 0, ks, other)
    act_dot(0, 1, ks, other)
    hid_gates(scales, (half_pieces, 2 * half_pieces))

    flows = [(w, h) for w in range(GROUP) for h in range(LANE_PARTS)]

    def reach(h):
        longer = ring // 2
        return (longer, ring - 1 - longer) if h == 0 else (ring - 1 - longer, longer)

    def chunk(number):
        return pl.ds(pl.multiple_of((number % ring) * size, size), size)

    copies = {}

    def ring_sent(phase):
        all_sent = grads.at[:, : (ring - 1) * size, :]
        remote(all_sent, all_sent, ring_send.at[phase], ring_recv.at[0, 0], right).wait_send()

    for step in range(STEPS):

        def send(flow, slot, source, target, device):
            phase = ring_send.at[0 if slot < ring - 1 else 1]
            copy = remote(source, target, phase, ring_recv.at[flow, slot], device)
            copy.start()
            copies[flow, slot] = copy

        def send_sum(flow, to_right, s):
            far, back = reach(flow % LANE_PARTS)
            at = chunk(place + far - s) if to_right else chunk(place + ring - back + s)
            slot = s if to_right else far + s
            device = right if to_right else left
            send(flow, slot, grads.at[flow, at, :], arrived.at[flow, slot], device)

        def send_block(flow, to_right, t):
            far, back = reach(flow % LANE_PARTS)
            at = chunk(place + ring - t) if to_right else chunk(place + t)
            slot = ring - 1 + (t if to_right else far + t)
            device = right if to_right else left
            here = blocks.at[flow, at, :]
            send(flow, slot, here, here, device)

        def pass_sum(flow, to_right, s):
            far, back = reach(flow % LANE_PARTS)
            slot = s if to_right else far + s
            at = chunk(place + far - 1 - s) if to_right else chunk(place + ring + 1 - back + s)
            copies[flow, slot].wait_recv()
            total = grads[flow, at, :].astype(F32) + arrived[flow, slot].astype(F32)
            grads[flow, at, :] = total.astype(BF16)
            send_sum(flow, to_right, s + 1)

        def send_w2(flow, offset):
            here = chunk(place + ring + offset)
            if abs(offset) < ring // 2:
                slot = 1 if offset == ring // 2 - 1 else 0
                target = far_w2.at[flow % LANE_PARTS, here, :]
                remote(
                    blocks.at[flow, here, :], target, w2_send, w2_recv.at[slot], across
                ).start()
            target = near_w2.at[flow % LANE_PARTS, here, :]
            remote(
                blocks.at[flow, here, :], target, near_send, near_recv, sibling
            ).start()

        def grad(w):
            source = ut if w == 2 else kt

            for piece in range(PIECES):
                at = slice(piece * (rows // PIECES), (piece + 1) * (rows // PIECES))
                product = dot(source[at, :], mid[w]).astype(BF16)
                grads[2 * w, at, :] = product[:, :128]
                grads[2 * w + 1, at, :] = product[:, 128:]
            for h in range(LANE_PARTS):
                send_sum(2 * w + h, True, 0)
                send_sum(2 * w + h, False, 0)

        if step == 0:
            turned(ks, kt, other)
            u_pair.wait_recv()
            turned(us, ut, other)
            grad(2)
            act_dot(0, 2, us, other)
            err_gates(scales, (half_pieces, 2 * half_pieces))
        else:
            err_gates(scales, whole)
        grad(0)
        grad(1)
        if step == 0:
            for w in range(GROUP):
                norm_sums[0, w] = lane_fold(square_sum(firsts[w][...].astype(F32)))
            norm_pair = pair(3, norm_sums.at[0], norm_sums.at[1])
            norm_pair.start()
        turn = ring // 2 - 1
        ordered = [2 * w + h for w in range(GROUP) for h in range(LANE_PARTS)]
        for s in range(turn):
            for flow in ordered:
                far, back = reach(flow % LANE_PARTS)
                if s < far - 1:
                    pass_sum(flow, True, s)
                if s < back - 1:
                    pass_sum(flow, False, s)
        for flow in ordered:
            far, back = reach(flow % LANE_PARTS)
            w, h = flows[flow]
            at = chunk(place)
            copies[flow, far - 1].wait_recv()
            copies[flow, ring - 2].wait_recv()
            total = grads[flow, at, :].astype(F32) + arrived[flow, far - 1].astype(F32)
            total = total + arrived[flow, ring - 2].astype(F32)
            if step == 0:
                lanes = slice(h * 128, (h + 1) * 128)
                moved = firsts[w][at, lanes].astype(F32) + total
            else:
                moved = kept[flow] * scales[w] + total
            kept[flow] = moved
            rounded = moved.astype(BF16)
            blocks[flow, at, :] = rounded
            send_block(flow, True, 0)
            send_block(flow, False, 0)
            if step == STEPS - 1 and w == 2:
                send_w2(flow, 0)
            part = square_sum(rounded.astype(F32))
            tally[0, w] = part if h == 0 else tally[0, w] + part
        tallies = []

        def start_tally(stage):
            copy = remote(
                tally.at[stage], tally_in.at[step * bits + stage],
                tally_send.at[stage], tally_recv.at[step * bits + stage],
                tally_partners[stage],
            )
            copy.start()
            tallies.append(copy)

        def end_tally(stage):
            tallies[stage].wait_recv()
            tally[stage + 1] = tally[stage] + tally_in[step * bits + stage]
            if stage + 1 < bits:
                start_tally(stage + 1)

        def take_block(flow, t):
            far, back = reach(flow % LANE_PARTS)
            for to_right, count in ((True, far), (False, back)):
                if t >= count:
                    continue
                copies[flow, ring - 1 + (t if to_right else far + t)].wait_recv()
                if t < count - 1:
                    send_block(flow, to_right, t + 1)
                if step == STEPS - 1 and flow // LANE_PARTS == 2:
                    send_w2(flow, -1 - t if to_right else 1 + t)

        if step > 0:
            q_pair.wait_recv()
            loads[5].wait()
        wanted = (ks, ks, us) if step == 0 else (qs, qs)

        def pair_dot(w, one, two, fresh):
            pair_at = (chunk(one), chunk(two))
            right_side = jnp.concatenate(
                [
                    jnp.concatenate([blocks[2 * w, at, :], blocks[2 * w + 1, at, :]], axis=1)
                    for at in pair_at
                ],
                axis=0,
            )
            for side in (own, other):
                left_side = jnp.concatenate([wanted[w][side, at] for at in pair_at], axis=1)
                product = dot(left_side, right_side)
                acts[w, side, :] = product if fresh else acts[w, side, :] + product

        in_pairs = size % 128 == 0
        start_tally(0)
        ended = 0
        for t in range(turn):
            for flow in ordered:
                take_block(flow, t)
                w, h = flows[flow]
                if in_pairs and h == LANE_PARTS - 1 and w < len(wanted):
                    pair_dot(w, place + ring - 1 - t, place + 1 + t, t == 0)
                if flow == ordered[3] and ended < bits - 1:
                    end_tally(ended)
                    ended += 1
            if step == STEPS - 1 and t == turn // 2:
                w_swap.wait()
                w_share = pair(4, w_far.at[own_rows, :], w_far.at[own_rows, :])
                w_share.start()
        if step == 0:
            norm_pair.wait()
            norms = [
                jnp.sqrt(jnp.sum(norm_sums[0, w] + norm_sums[1, w], keepdims=True))
                for w in range(GROUP)
            ]

        def last_dot(w):
            for h in range(LANE_PARTS):
                take_block(2 * w + h, turn)
            if w >= len(wanted):
                return
            if in_pairs:
                pair_dot(w, place, place + ring // 2, False)
            else:
                act_dot(1, w, wanted[w], own)
                act_dot(1, w, wanted[w], other)

        last_dot(0)
        last_dot(1)
        while ended < bits:
            end_tally(ended)
            ended += 1
        scales = [
            norms[w] / jnp.sqrt(jnp.sum(tally[bits, w], keepdims=True) + 1e-06)
            for w in range(GROUP)
        ]
        ring_sent(0)
        if step == 0:
            hid_gates(scales, whole)
            grad(2)
            last_dot(2)
        ring_sent(1)
        for copy in tallies:
            copy.wait_send()

    ends = [tokens * sum(TILES[: t + 1]) // sum(TILES) for t in range(len(TILES))]
    tiles = [(end - tokens * part // sum(TILES), end) for end, part in zip(ends, TILES)]
    scale_out[...] = jnp.broadcast_to(scales[2], scale_out.shape)
    scale_swap = remote(
        scale_out, far_scale, side_send.at[1], side_recv.at[1], across
    )
    scale_swap.start()
    hid_copies = []

    def send_hid(slot, source, target, device):
        copy = remote(source, target, hid_send.at[slot // 2], hid_recv.at[slot], device)
        copy.start()
        return copy

    def hidden_of(side, first, last):
        at = slice(side * tokens + first, side * tokens + last)
        act = acts[0, at, :] * scales[0]
        lin = acts[1, at, :] * scales[1]
        hq[at, :] = (act * jax.nn.sigmoid(act) * lin).astype(BF16)

    def send_tile(t):
        first, last = tiles[t]
        to, at = slice(first, last), slice(tokens + first, tokens + last)
        hid_copies.append((
            send_hid(2 * t, hq.at[to, :], far_hid.at[0, to, :], across),
            send_hid(2 * t + 1, hq.at[at, :], far_hid.at[1, to, :], diagonal),
        ))

    for side in range(CORES):
        hidden_of(side, 0, tokens)
    last_dot(2)
    near_copy = send_hid(2 * len(TILES), hq.at[other, :], near_hid, sibling)
    send_tile(0)
    wide = ((1,), (1,))
    stripe = half // STRIPES

    def tile_sent(t):
        first, last = tiles[t]
        both = far_hid.at[:, first:last, :]
        remote(both, both, hid_send.at[t], hid_recv.at[2 * t], across).wait_send()

    def near_stripes(first, last):
        def one(c, carry):
            lanes = pl.ds(pl.multiple_of(c * stripe, 128), stripe)
            total_out[:, lanes] = dot(near[...], w_near[:, lanes])
            return carry

        lax.fori_loop(first, last, one, 0)

    near_w2_copy = remote(near_w2, near_w2, near_send, near_recv, sibling)
    near_w2_copy.wait_recv()
    near_copy.wait_recv()
    mine = dot(hq[own, :], jnp.concatenate([blocks[4], blocks[5]], axis=1), wide)
    theirs = dot(near_hid[...], jnp.concatenate([near_w2[0], near_w2[1]], axis=1), wide)
    near[...] = ((mine + theirs) * scales[2]).astype(BF16)
    for t in range(1, len(TILES)):
        send_tile(t)
    w_copy.wait()
    near_stripes(0, 1)
    next_w2 = far_w2.at[0:2, chunk(place + ring // 2 - 1), :]
    remote(next_w2, next_w2, w2_send, w2_recv.at[1], across).wait_recv()
    relay = remote(next_w2, next_w2, relay_sem.at[0], relay_sem.at[1], left)
    relay.start()
    near_stripes(1, STRIPES)
    most_w2 = far_w2.at[0:2, : (ring - 2) * size, :]
    remote(most_w2, most_w2, w2_send, w2_recv.at[0], across).wait_recv()
    relay.wait_recv()
    far_pair = pair(5, far_w2.at[0:2], far_w2.at[2:4])
    far_pair.start()
    scale_swap.wait()
    w_share.wait_recv()
    far_pair.wait_recv()
    scale = jnp.max(far_scale[...], keepdims=True)
    for t, (first, last) in enumerate(tiles):
        at = slice(first, last)
        hid_copies[t][0].wait_recv()
        hid_copies[t][1].wait_recv()
        mine = dot(
            far_hid[0, at, :], jnp.concatenate([far_w2[0], far_w2[1]], axis=1), wide
        )
        theirs = dot(
            far_hid[1, at, :], jnp.concatenate([far_w2[2], far_w2[3]], axis=1), wide
        )
        near[at, :] = ((mine + theirs) * scale).astype(BF16)

        def far_cols_of(c, carry):
            lanes = pl.ds(pl.multiple_of(c * stripe, 128), stripe)
            added = total_out[at, lanes] + dot(near[at, :], w_far[:, lanes])
            out[at, lanes] = added.astype(BF16)
            return carry

        lax.fori_loop(0, STRIPES, far_cols_of, 0)
    for t in range(len(TILES)):
        tile_sent(t)
    near_copy.wait_send()
    near_w2_copy.wait_send()
    sent_w2 = far_w2.at[0:2, : (ring - 1) * size, :]
    remote(sent_w2, sent_w2, w2_send, w2_recv.at[0], across).wait_send()
    relay.wait_send()
    far_pair.wait_send()
    w_share.wait_send()
    for copy in (k_pair, u_pair, q_pair):
        copy.wait_send()


def shards(n_ctx, queries, keys, values, rates, w_up, w_gate, w_down, w_out):
    tokens, rows = keys.shape
    cols = w_up.shape[2] // CORES
    half = w_out.shape[1] // 2
    ring = n_ctx // CORES
    size = rows // ring
    bits = n_ctx.bit_length() - 1
    flows = GROUP * LANE_PARTS
    vmem = pl.BlockSpec(memory_space=pltpu.VMEM)
    anywhere = pl.BlockSpec(memory_space=pl.ANY)
    dma = pltpu.SemaphoreType.DMA
    return pl.pallas_call(
        functools.partial(layer_kernel, n_ctx),
        out_shape=pltpu.VMEM((tokens, half), BF16),
        in_specs=[anywhere] * 3 + [vmem] + [anywhere] * 4,
        out_specs=vmem,
        scratch_shapes=[
            pltpu.VMEM((2 * tokens, rows), BF16),
            pltpu.VMEM((2 * tokens, rows), BF16),
            pltpu.VMEM((2 * tokens, rows), BF16),
            pltpu.VMEM((tokens, rows), BF16),
            pltpu.VMEM((rows, 2 * tokens), BF16),
            pltpu.VMEM((rows, 2 * tokens), BF16),
            pltpu.VMEM((rows, cols), BF16),
            pltpu.VMEM((rows, cols), BF16),
            pltpu.VMEM((cols, rows), BF16),
            pltpu.VMEM((rows, cols), BF16),
            pltpu.VMEM((GROUP, 2 * tokens, cols), F32),
            pltpu.VMEM((GROUP, 2 * tokens, cols), BF16),
            pltpu.VMEM((flows, rows, cols // LANE_PARTS), BF16),
            pltpu.VMEM((flows, rows, cols // LANE_PARTS), BF16),
            pltpu.VMEM((flows, ring - 1, size, cols // LANE_PARTS), BF16),
            pltpu.VMEM((flows, size, cols // LANE_PARTS), F32),
            pltpu.VMEM((bits + 1, GROUP, 8, 128), F32),
            pltpu.VMEM((STEPS * bits, GROUP, 8, 128), F32),
            pltpu.VMEM((CORES, GROUP, 8, 128), F32),
            pltpu.VMEM((2 * tokens, cols), BF16),
            pltpu.VMEM((tokens, cols), BF16),
            pltpu.VMEM((CORES, tokens, cols), BF16),
            pltpu.VMEM((LANE_PARTS, rows, cols // LANE_PARTS), BF16),
            pltpu.VMEM((CORES * LANE_PARTS, rows, cols // LANE_PARTS), BF16),
            pltpu.VMEM((8, 128), F32),
            pltpu.VMEM((8, 128), F32),
            pltpu.VMEM((rows, half), BF16),
            pltpu.VMEM((rows, half), BF16),
            pltpu.VMEM((tokens, rows), BF16),
            pltpu.VMEM((tokens, half), F32),
            dma((2,)),
            dma((flows, 2 * (ring - 1))),
            dma((6,)),
            dma((6,)),
            dma((bits,)),
            dma((STEPS * bits,)),
            dma((2,)),
            dma((2,)),
            dma,
            dma((2,)),
            dma((2,)),
            dma,
            dma,
            dma((len(TILES) + 1,)),
            dma((2 * len(TILES) + 1,)),
            dma((7,)),
        ],
        compiler_params=pltpu.CompilerParams(
            collective_id=0, has_side_effects=True, vmem_limit_bytes=60 << 20
        ),
    )(queries, keys, values, rates.T, w_up[0], w_gate[0], w_down[0], w_out)


def solution(mesh):
    def body(*args):
        return shards(mesh.shape["ctx"], *args)

    return jax.shard_map(
        body,
        mesh=mesh,
        in_specs=(
            P("ctx", "head"),
            P("ctx", "head"),
            P("ctx", "head"),
            P("ctx", "head"),
            P("head", None, None),
            P("head", None, None),
            P("head", None, None),
            P("head", None),
        ),
        out_specs=P("ctx", "head"),
        check_vma=False,
    )
```
